32 devices in a mesh: gx: 8 (over y, x, core), gy: 4 (over z).
Axes of the slice: x: 2, y: 2, z: 4, core: 2. Of those that a mesh axis runs over, the one named last changes fastest.
Arguments:
- east_flow: float32 [8, 1024, 2048], P(None, 'gx', 'gy'), may hold values from -36 to 36
- north_flow: float32 [8, 1024, 2048], P(None, 'gx', 'gy'), may hold values from -36 to 36
Outputs:
- stress: float32 [3, 8, 256, 512], P(None, None, 'gx', 'gy')
- library: float32 [48, 8, 256, 512], P(None, None, 'gx', 'gy')
The draws below stay inside these ranges and needn't reach their ends.
All inputs are finite; a program needn't handle non-finite values.
Results may differ from the reference program's by a relative error of at most 0.0003.
Values sent between devices are 32-bit elements; how exact they have to be, the bound alone decides.
No kernel may reach another device: no remote copies, remote signals or barrier semaphores. Data moves between devices by JAX's collectives and lax.ppermute only.
A program may use at most 128 MiB of HBM per device.

```python
import jax
import jax.numpy as jnp
from jax import lax

LEV = 8
NX = 1024
NY = 2048


def shard_levels(own_key, dims, cuts, low, high):
    gain = 1.0
    for axis_at, parts in cuts:
        draws = jax.random.uniform(jax.random.fold_in(jax.random.fold_in(own_key, 6), axis_at), (parts,), jnp.float32, low / len(cuts), high / len(cuts))
        gain = gain * jnp.repeat(jnp.exp(draws), dims[axis_at] // parts).reshape((-1,) + (1,) * (len(dims) - 1 - axis_at))
    return gain


def bell_draw(key, dims, width, most, split=(), dtype=jnp.bfloat16):
    drawn = jax.random.normal(key, dims, jnp.float32) * width
    if len(split) > 0:
        drawn = shard_levels(key, dims, split, -0.22, 0.18) * drawn
    return jnp.clip(drawn, min=-most, max=most).astype(dtype)


def setup_inputs(seed: int = 0) -> dict:
    keys = jax.random.split(jax.random.key(seed), 3)
    return {
        "east_flow": bell_draw(keys[0], (LEV, NX, NY), 6.0, 36.0, ((1, 8), (2, 4)), jnp.float32),
        "north_flow": bell_draw(keys[1], (LEV, NX, NY), 6.0, 36.0, ((1, 8), (2, 4)), jnp.float32),
    }


spread_cells = 5.5


def gauss_taps():
    offsets = jnp.arange(33).astype(jnp.float32) - 16.0
    bumps = jnp.exp(-0.5 * (offsets / spread_cells) ** 2)
    return bumps / jnp.sum(bumps)


def coarse_smooth(field, weights):
    count_x, count_y = field.shape
    extended = jnp.concatenate([field[count_x - 16:], field, field[:16]], axis=0)
    rows_out = jnp.zeros((count_x // 4, count_y), jnp.float32)
    for offset in range(33):
        rows_out = rows_out + weights[offset] * extended[offset:offset + count_x:4]
    extended = jnp.concatenate([rows_out[:, count_y - 16:], rows_out, rows_out[:, :16]], axis=1)
    result = jnp.zeros((count_x // 4, count_y // 4), jnp.float32)
    for offset in range(33):
        result = result + weights[offset] * extended[:, offset:offset + count_y:4]
    return result


def first_form(plus_two, plus_one, minus_one, minus_two):
    return ((8.0 * plus_one - plus_two) - 8.0 * minus_one + minus_two) / 12.0


def second_form(plus_two, plus_one, centre, minus_one, minus_two):
    return (((16.0 * plus_one - plus_two) - 30.0 * centre) + 16.0 * minus_one - minus_two) / 12.0


def moved(field, step, axis):
    return jnp.roll(field, -step, axis)


def first_diff(field, axis):
    return first_form(moved(field, 2, axis), moved(field, 1, axis), moved(field, -1, axis), moved(field, -2, axis))


def second_diff(field, axis):
    return second_form(moved(field, 2, axis), moved(field, 1, axis), field, moved(field, -1, axis), moved(field, -2, axis))


def build_library(east_mean, north_mean, grad_ux, grad_uy, grad_vx, grad_vy, curve_uxx, curve_uxy, curve_uyy, curve_vxx, curve_vxy, curve_vyy):
    vorticity = grad_vx - grad_uy
    features = [grad_ux, grad_uy, grad_vx, grad_vy, curve_uxx, curve_uxy, curve_uyy, curve_vxx, curve_vxy, curve_vyy, curve_vxx - curve_uxy, curve_vxy - curve_uyy]
    columns = []
    for feature in features:
        columns.append(feature)
        columns.append(east_mean * feature)
        columns.append(north_mean * feature)
        columns.append(vorticity * feature)
    return jnp.stack(columns, axis=0)


def one_level(pair):
    east, north = pair
    weights = gauss_taps()
    means = [coarse_smooth(field, weights) for field in (east, north, east * east, east * north, north * north)]
    east_mean, north_mean = means[0], means[1]
    stress = jnp.stack([means[2] - east_mean * east_mean, means[3] - east_mean * north_mean, means[4] - north_mean * north_mean], axis=0)
    along_ux = first_diff(east_mean, 0)
    along_vx = first_diff(north_mean, 0)
    library = build_library(east_mean, north_mean, along_ux, first_diff(east_mean, 1), along_vx, first_diff(north_mean, 1),
                            second_diff(east_mean, 0), first_diff(along_ux, 1), second_diff(east_mean, 1),
                            second_diff(north_mean, 0), first_diff(along_vx, 1), second_diff(north_mean, 1))
    return stress, library


def reference(east_flow, north_flow):
    stress, library = lax.map(one_level, (east_flow, north_flow))
    return jnp.transpose(stress, (1, 0, 2, 3)), jnp.transpose(library, (1, 0, 2, 3))
```

```python
import functools

import jax
import jax.numpy as jnp
import numpy as np
from jax import lax
from jax.experimental import pallas as pl
from jax.experimental.pallas import tpu as pltpu
from jax.sharding import PartitionSpec as P

spread_cells = 5.5
REACH = 16
STEP = 4
EXT = REACH // STEP
RIM = 2
WIDE = EXT + RIM
EDGE = 32
HALF = 64
MSG = 24
F32, BF16 = jnp.float32, jnp.bfloat16


def taps(cells, count_in):
    offsets = np.arange(2 * REACH + 1) - REACH
    bumps = np.exp(-0.5 * (offsets / spread_cells) ** 2)
    lag = np.arange(count_in)[None, :] - STEP * np.asarray(cells)[:, None]
    inside = np.abs(lag) <= REACH
    return np.where(inside, np.exp(-0.5 * (lag / spread_cells) ** 2), 0.0) / bumps.sum()


def pieces(values):
    high = values.astype(BF16)
    low = (values - high.astype(np.float64)).astype(BF16)
    return high, low


def left_operand(rows):
    high, low = pieces(rows)
    return np.concatenate(
        [np.concatenate([high, high], 1), np.concatenate([low, np.zeros_like(low)], 1)], 0
    )


def message_rows(count_x):
    coarse = count_x // STEP
    low_wide = list(range(-EXT, RIM))
    high_wide = list(range(coarse - RIM, coarse + EXT))
    low_short = list(range(-EXT, 0))
    high_short = list(range(coarse, coarse + EXT))

    def rows(cells):
        full = taps(cells, count_x)
        return np.concatenate([full[:, :EDGE], full[:, count_x - EDGE :]], 1)

    sides = {"low": (rows(low_wide), rows(low_short)), "high": (rows(high_wide), rows(high_short))}

    def placed(at, part):
        block = np.zeros((8, 2 * EDGE))
        block[at : at + part.shape[0]] = part
        return block

    both = {"wide": [], "uu": [], "uv": [], "vv": []}
    for first, second in (("high", "low"), ("low", "high")):
        wide = np.concatenate([placed(0, sides[s][0]) for s in (first, second)], 0)
        uu = np.concatenate([placed(0, sides[s][1]) for s in (first, second)], 0)
        uv = np.concatenate([placed(4, sides[s][1]) for s in (first, second)], 0)
        vv = np.concatenate(
            [placed(6, sides[s][1][:2]) for s in (first, second)]
            + [placed(6, sides[s][1][2:]) for s in (first, second)],
            0,
        )
        for name, value in (("wide", wide), ("uu", uu), ("uv", uv), ("vv", vv)):
            both[name].append(left_operand(value))
    return tuple(np.stack(both[name]) for name in ("wide", "uu", "uv", "vv"))


def column_weights(count_y):
    coarse = count_y // STEP
    own = taps(range(coarse), count_y).T
    strips = np.zeros((count_y, 2 * HALF))
    strips[:, :WIDE] = taps(range(-EXT, RIM), count_y).T
    strips[:, HALF : HALF + WIDE] = taps(range(coarse - RIM, coarse + EXT), count_y).T
    return pieces(np.concatenate([own, strips], 1))


def split(values):
    high = values.astype(BF16)
    return high, (values - high.astype(F32)).astype(BF16)


def row_sums(left, field):
    high, low = split(field)
    both = jnp.dot(left, jnp.concatenate([high, low], 0), preferred_element_type=F32)
    half = both.shape[0] // 2
    return both[:half] + both[half:]


def column_sums(rows, w_high, w_low):
    high, low = split(rows)
    total = jnp.dot(high, w_high, preferred_element_type=F32)
    total = total + jnp.dot(high, w_low, preferred_element_type=F32)
    return total + jnp.dot(low, w_high, preferred_element_type=F32)


def products(u, v):
    return u, v, u * u, u * v, v * v


def edge_kernel(block, ut, ub, vt, vb, wide, cuu, cuv, cvv, w_high, w_low, e_ref, o_ref):
    odd = lax.rem(lax.axis_index("gx"), 2)
    step = pl.program_id(0)
    levels = e_ref.shape[0] - 1

    @pl.when(step == 0)
    def _():
        e_ref[levels] = jnp.zeros(e_ref.shape[1:], F32)
        o_ref[levels] = jnp.zeros(o_ref.shape[1:], F32)

    gathered = []
    for q in range(block):
        u = jnp.concatenate([ut[q], ub[q]], 0)
        v = jnp.concatenate([vt[q], vb[q]], 0)
        _, _, uu, uv, vv = products(u, v)
        last = row_sums(cvv[odd], vv)
        gathered.append(row_sums(wide[odd], u) + last[:16])
        gathered.append(row_sums(wide[odd], v) + last[16:])
        gathered.append(row_sums(cuu[odd], uu) + row_sums(cuv[odd], uv))
    sums = column_sums(jnp.concatenate(gathered, 0), w_high[...], w_low[...])
    lanes = e_ref.shape[2]
    for q in range(block):
        level = step * block + q
        for place, ref in ((0, e_ref), (8, o_ref)):
            part = jnp.concatenate(
                [sums[48 * q + 16 * t + place : 48 * q + 16 * t + place + 8] for t in range(3)], 0
            )
            ref[level] = part[:, :lanes]
            ref[levels] += pltpu.roll(part[:, lanes:], WIDE * level, 1)


def own_kernel(block, u_ref, v_ref, c_ref, w_high, w_low, p_ref, s_ref):
    step = pl.program_id(0)

    @pl.when(step == 0)
    def _():
        s_ref[...] = jnp.zeros(s_ref.shape, F32)

    coarse, lanes = p_ref.shape[2:]
    for q in range(block):
        fields = products(u_ref[q], v_ref[q])
        rows = jnp.concatenate([row_sums(c_ref[...], f) for f in fields], 0)
        sums = column_sums(rows, w_high[...], w_low[...])
        for k in range(5):
            p_ref[q, k] = sums[coarse * k : coarse * (k + 1), :lanes]
        s_ref[...] += pltpu.roll(sums[:, lanes:], WIDE * (step * block + q), 1)


def low_and_high(odd, e, o):
    return jnp.where(odd == 0, o, e), jnp.where(odd == 0, e, o)


def add_rows(wide_refs, short_refs, own_low, own_high, got_low, got_high):
    for k, ref in enumerate(wide_refs):
        count = ref.shape[0]
        at = 8 * k
        ref[0:RIM] = own_low[at + EXT - RIM : at + EXT]
        ref[count - RIM : count] = own_high[at + RIM : at + 2 * RIM]
        ref[0:WIDE] = ref[0:WIDE] + got_low[at : at + WIDE]
        ref[count - WIDE : count] = ref[count - WIDE : count] + got_high[at : at + WIDE]
    for k, ref in enumerate(short_refs):
        count = ref.shape[0]
        if k < 2:
            at = 16 + EXT * k
            ref[0:EXT] = ref[0:EXT] + got_low[at : at + EXT]
            ref[count - EXT : count] = ref[count - EXT : count] + got_high[at : at + EXT]
        else:
            for h in range(2):
                at = 8 * h + WIDE
                ref[2 * h : 2 * h + 2] = ref[2 * h : 2 * h + 2] + got_low[at : at + 2]
                back = count - EXT + 2 * h
                ref[back : back + 2] = ref[back : back + 2] + got_high[at : at + 2]


def strip_kernel(s_ref, own_e, own_o, got_e, got_o, e_ref, o_ref, us, vs, uus, uvs, vvs):
    odd_x = lax.rem(lax.axis_index("gx"), 2)
    odd_y = lax.rem(lax.axis_index("gy"), 2)
    coarse = uus.shape[0]
    us[RIM : RIM + coarse] = s_ref[0:coarse]
    vs[RIM : RIM + coarse] = s_ref[coarse : 2 * coarse]
    uus[...] = s_ref[2 * coarse : 3 * coarse]
    uvs[...] = s_ref[3 * coarse : 4 * coarse]
    vvs[...] = s_ref[4 * coarse : 5 * coarse]
    own_low, own_high = low_and_high(odd_x, own_e[0], own_o[0])
    got_low, got_high = low_and_high(odd_x, got_e[0], got_o[0])
    add_rows((us, vs), (uus, uvs, vvs), own_low, own_high, got_low, got_high)
    rim_rows = us.shape[0]
    start = -(-rim_rows // 8) * 8
    pairs = (
        (0, us[...], vs[...]),
        (start, uus[...], uvs[...]),
        (start + coarse, vvs[0 : coarse // 2], vvs[coarse // 2 : coarse]),
    )
    for at, a, b in pairs:
        lane = lax.broadcasted_iota(jnp.int32, a.shape, 1)
        low = jnp.where(lane < HALF, a, pltpu.roll(b, HALF, 1))
        high = jnp.where(lane < HALF, pltpu.roll(a, HALF, 1), b)
        e_ref[at : at + a.shape[0]] = jnp.where(odd_y == 0, high, low)
        o_ref[at : at + a.shape[0]] = jnp.where(odd_y == 0, low, high)


def first_form(plus_two, plus_one, minus_one, minus_two):
    return (8.0 * plus_one - plus_two - 8.0 * minus_one + minus_two) * (1.0 / 12.0)


def second_form(plus_two, plus_one, centre, minus_one, minus_two):
    return (16.0 * plus_one - plus_two - 30.0 * centre + 16.0 * minus_one - minus_two) * (1.0 / 12.0)


def final_kernel(
    p_ref, xe_own, xo_own, xe_got, xo_got, ye_own, yo_own, ye_got, yo_got, st_ref, lib_ref,
    us, vs, uus, uvs, vvs, low_side, high_side, slopes,
):
    odd_x = lax.rem(lax.axis_index("gx"), 2)
    odd_y = lax.rem(lax.axis_index("gy"), 2)
    level = pl.program_id(0)
    coarse, lanes = p_ref.shape[2:]
    rim_rows = us.shape[0]

    @pl.when(level == 0)
    def _():
        own_low, own_high = low_and_high(odd_y, ye_own[...], yo_own[...])
        got_low, got_high = low_and_high(odd_y, ye_got[...], yo_got[...])
        place = lax.rem(lax.rem(lax.broadcasted_iota(jnp.int32, own_low.shape, 1), HALF), WIDE)
        back = pltpu.roll(own_low, lanes - RIM, 1)
        ahead = pltpu.roll(own_high, RIM, 1)
        low_side[...] = got_low + jnp.where(place < RIM, back, 0.0)
        high_side[...] = got_high + jnp.where(place >= EXT, ahead, 0.0)

    us[RIM : RIM + coarse] = p_ref[0, 0]
    vs[RIM : RIM + coarse] = p_ref[0, 1]
    for k, ref in enumerate((uus, uvs, vvs)):
        ref[...] = p_ref[0, 2 + k]
    own_low, own_high = low_and_high(odd_x, xe_own[0], xo_own[0])
    got_low, got_high = low_and_high(odd_x, xe_got[0], xo_got[0])
    add_rows((us, vs), (uus, uvs, vvs), own_low, own_high, got_low, got_high)

    shift = WIDE * level

    def sides(at, count, second):
        base = HALF if second else 0
        low = pltpu.roll(low_side[at : at + count], lanes - RIM - base - shift, 1)
        high = pltpu.roll(high_side[at : at + count], lanes - EXT - base - shift, 1)
        return low, high

    def joined(field, low, high):
        lane = lax.broadcasted_iota(jnp.int32, field.shape, 1)
        return field + jnp.where(lane < EXT, low, 0.0) + jnp.where(lane >= lanes - EXT, high, 0.0)

    means = []
    found = []
    for k, ref in enumerate((us, vs)):
        low, high = sides(0, rim_rows, k == 1)
        f = joined(ref[...], low, high)
        ref[...] = f
        lane = lax.broadcasted_iota(jnp.int32, f.shape, 1)
        plus_one = pltpu.roll(jnp.where(lane < 1, high, f), lanes - 1, 1)
        plus_two = pltpu.roll(jnp.where(lane < 2, high, f), lanes - 2, 1)
        minus_one = pltpu.roll(jnp.where(lane >= lanes - 1, low, f), 1, 1)
        minus_two = pltpu.roll(jnp.where(lane >= lanes - 2, low, f), 2, 1)
        slopes[...] = first_form(plus_two, plus_one, minus_one, minus_two)

        def row(source, by):
            return source[RIM + by : RIM + by + coarse]

        curve_y = second_form(plus_two, plus_one, f, minus_one, minus_two)[RIM : RIM + coarse]
        centre = row(ref, 0)
        shifted = [row(ref, by) for by in (2, 1, -1, -2)]
        grad_x = first_form(*shifted)
        curve_x = second_form(shifted[0], shifted[1], centre, shifted[2], shifted[3])
        grad_y = row(slopes, 0)
        cross = first_form(*[row(slopes, by) for by in (2, 1, -1, -2)])
        means.append(centre)
        found.append((grad_x, grad_y, curve_x, cross, curve_y))

    u, v = means
    start = -(-rim_rows // 8) * 8
    low, high = sides(start, coarse, False)
    st_ref[0, 0] = joined(uus[...], low, high) - u * u
    low, high = sides(start, coarse, True)
    st_ref[1, 0] = joined(uvs[...], low, high) - u * v
    for h in range(2):
        part = slice(coarse // 2 * h, coarse // 2 * (h + 1))
        low, high = sides(start + coarse, coarse // 2, h == 1)
        st_ref[2, 0, part] = joined(vvs[part], low, high) - v[part] * v[part]

    (ux, uy, uxx, uxy, uyy), (vx, vy, vxx, vxy, vyy) = found
    vorticity = vx - uy
    features = (ux, uy, vx, vy, uxx, uxy, uyy, vxx, vxy, vyy, vxx - uxy, vxy - uyy)
    for k, feature in enumerate(features):
        lib_ref[4 * k, 0] = feature
        lib_ref[4 * k + 1, 0] = u * feature
        lib_ref[4 * k + 2, 0] = v * feature
        lib_ref[4 * k + 3, 0] = vorticity * feature


def swapped(axis, even, odd):
    count = lax.axis_size(axis)
    assert count % 2 == 0
    pairs = [(i, i ^ 1) for i in range(count)]
    others = [(i, (i + 1) % count if i % 2 else (i - 1) % count) for i in range(count)]
    return lax.ppermute(even, axis, pairs), lax.ppermute(odd, axis, others)


def whole(shape):
    return pl.BlockSpec(shape, lambda *_: (0,) * len(shape))


def per_device(east_flow, north_flow):
    levels, count_x, count_y = east_flow.shape
    coarse, lanes = count_x // STEP, count_y // STEP
    assert lanes == 2 * HALF and WIDE * levels <= HALF and coarse % 16 == 0
    w_high, w_low = (jnp.asarray(w) for w in column_weights(count_y))
    edge_rows = tuple(jnp.asarray(c) for c in message_rows(count_x))
    own_rows = jnp.asarray(left_operand(taps(range(coarse), count_x)))
    shape = functools.partial(jax.ShapeDtypeStruct, dtype=F32)

    block = 2
    top = pl.BlockSpec((block, EDGE, count_y), lambda i: (i, 0, 0))
    bottom = pl.BlockSpec((block, EDGE, count_y), lambda i: (i, count_x // EDGE - 1, 0))
    message = (levels + 1, MSG, lanes)
    xe, xo = pl.pallas_call(
        functools.partial(edge_kernel, block),
        grid=(levels // block,),
        in_specs=[top, bottom, top, bottom]
        + [whole(c.shape) for c in edge_rows]
        + [whole(w_high.shape), whole(w_low.shape)],
        out_specs=[whole(message)] * 2,
        out_shape=[shape(message)] * 2,
        name="edge",
    )(east_flow, east_flow, north_flow, north_flow, *edge_rows, w_high, w_low)
    xe_got, xo_got = swapped("gx", xe, xo)

    block = 1
    fine = pl.BlockSpec((block, count_x, count_y), lambda i: (i, 0, 0))
    strip = (5 * coarse, lanes)
    partial_sums, strips = pl.pallas_call(
        functools.partial(own_kernel, block),
        grid=(levels // block,),
        in_specs=[fine, fine, whole(own_rows.shape), whole(w_high.shape), whole(w_low.shape)],
        out_specs=[pl.BlockSpec((block, 5, coarse, lanes), lambda i: (i, 0, 0, 0)), whole(strip)],
        out_shape=[shape((levels, 5, coarse, lanes)), shape(strip)],
        name="own",
    )(east_flow, north_flow, own_rows, w_high, w_low)

    rim_rows = coarse + 2 * RIM
    start = -(-rim_rows // 8) * 8
    side = (start + coarse + coarse // 2, lanes)
    rows = [pltpu.VMEM((rim_rows, lanes), F32)] * 2 + [pltpu.VMEM((coarse, lanes), F32)] * 3
    slab = pl.BlockSpec((1, MSG, lanes), lambda i: (levels, 0, 0))
    ye, yo = pl.pallas_call(
        strip_kernel,
        grid=(1,),
        in_specs=[whole(strip)] + [slab] * 4,
        out_specs=[whole(side)] * 2,
        out_shape=[shape(side)] * 2,
        scratch_shapes=rows,
        name="strips",
    )(strips, xe, xo, xe_got, xo_got)
    ye_got, yo_got = swapped("gy", ye, yo)

    one = pl.BlockSpec((1, MSG, lanes), lambda i: (i, 0, 0))
    stress, library = pl.pallas_call(
        final_kernel,
        grid=(levels,),
        in_specs=[pl.BlockSpec((1, 5, coarse, lanes), lambda i: (i, 0, 0, 0))] + [one] * 4 + [whole(side)] * 4,
        out_specs=[
            pl.BlockSpec((3, 1, coarse, lanes), lambda i: (0, i, 0, 0)),
            pl.BlockSpec((48, 1, coarse, lanes), lambda i: (0, i, 0, 0)),
        ],
        out_shape=[shape((3, levels, coarse, lanes)), shape((48, levels, coarse, lanes))],
        scratch_shapes=rows
        + [pltpu.VMEM(side, F32)] * 2
        + [pltpu.VMEM((rim_rows, lanes), F32)],
        name="final",
    )(partial_sums, xe, xo, xe_got, xo_got, ye, yo, ye_got, yo_got)
    return stress, library


def solution(mesh):
    return jax.shard_map(
        per_device,
        mesh=mesh,
        in_specs=(P(None, "gx", "gy"), P(None, "gx", "gy")),
        out_specs=(P(None, None, "gx", "gy"), P(None, None, "gx", "gy")),
        check_vma=False,
    )
```

```python
import functools

import jax
import jax.numpy as jnp
import numpy as np
from jax import lax
from jax.experimental import pallas as pl
from jax.experimental.pallas import tpu as pltpu
from jax.sharding import PartitionSpec as P

spread_cells = 5.5
REACH = 16
STEP = 4
EXT = REACH // STEP
RIM = 2
WIDE = EXT + RIM
EDGE = 32
HALF = 64
MSG = 24
F32, BF16 = jnp.float32, jnp.bfloat16
VMEM_BYTES = 24 << 20
EDGE_UNROLL, OWN_UNROLL, OWN_CHUNK, FINAL_UNROLL = 2, 2, 2, 1


def taps(cells, count_in):
    offsets = np.arange(2 * REACH + 1) - REACH
    bumps = np.exp(-0.5 * (offsets / spread_cells) ** 2)
    lag = np.arange(count_in)[None, :] - STEP * np.asarray(cells)[:, None]
    inside = np.abs(lag) <= REACH
    return np.where(inside, np.exp(-0.5 * (lag / spread_cells) ** 2), 0.0) / bumps.sum()


def pieces(values):
    high = values.astype(BF16)
    low = (values - high.astype(np.float64)).astype(BF16)
    return high, low


def left_operand(rows):
    high, low = pieces(rows)
    return np.concatenate(
        [np.concatenate([high, high], 1), np.concatenate([low, np.zeros_like(low)], 1)], 0
    )


def message_rows(count_x):
    coarse = count_x // STEP
    low_wide = list(range(-EXT, RIM))
    high_wide = list(range(coarse - RIM, coarse + EXT))
    low_short = list(range(-EXT, 0))
    high_short = list(range(coarse, coarse + EXT))

    def rows(cells):
        full = taps(cells, count_x)
        return np.concatenate([full[:, :EDGE], full[:, count_x - EDGE :]], 1)

    sides = {"low": (rows(low_wide), rows(low_short)), "high": (rows(high_wide), rows(high_short))}

    def placed(at, part):
        block = np.zeros((8, 2 * EDGE))
        block[at : at + part.shape[0]] = part
        return block

    both = {"wide": [], "uu": [], "uv": [], "vv": []}
    for first, second in (("high", "low"), ("low", "high")):
        wide = np.concatenate([placed(0, sides[s][0]) for s in (first, second)], 0)
        uu = np.concatenate([placed(0, sides[s][1]) for s in (first, second)], 0)
        uv = np.concatenate([placed(4, sides[s][1]) for s in (first, second)], 0)
        vv = np.concatenate(
            [placed(6, sides[s][1][:2]) for s in (first, second)]
            + [placed(6, sides[s][1][2:]) for s in (first, second)],
            0,
        )
        for name, value in (("wide", wide), ("uu", uu), ("uv", uv), ("vv", vv)):
            both[name].append(left_operand(value))
    return tuple(np.stack(both[name]) for name in ("wide", "uu", "uv", "vv"))


def column_weights(count_y):
    coarse = count_y // STEP
    own = taps(range(coarse), count_y).T
    strips = np.zeros((count_y, 2 * HALF))
    strips[:, :WIDE] = taps(range(-EXT, RIM), count_y).T
    strips[:, HALF : HALF + WIDE] = taps(range(coarse - RIM, coarse + EXT), count_y).T
    return pieces(np.concatenate([own, strips], 1))


def split(values):
    high = values.astype(BF16)
    return high, (values - high.astype(F32)).astype(BF16)


def row_sums(left, field):
    high, low = split(field)
    both = jnp.dot(left, jnp.concatenate([high, low], 0), preferred_element_type=F32)
    half = both.shape[0] // 2
    return both[:half] + both[half:]


def column_sums(high, low, w_high, w_low):
    total = jnp.dot(high, w_high, preferred_element_type=F32)
    total = total + jnp.dot(high, w_low, preferred_element_type=F32)
    return total + jnp.dot(low, w_high, preferred_element_type=F32)


def products(u, v):
    return u, v, u * u, u * v, v * v


def each(count, unroll, body):
    lax.fori_loop(0, count, lambda i, _: (body(i), None)[1], None, unroll=unroll)


def edge_kernel(
    u_hbm, v_hbm, *refs,
):
    consts, (e_ref, o_ref, u_ref, v_ref), kept = refs[:7], refs[7:11], refs[11:14]
    wide, cuu, cuv, cvv, x_high, x_low, sem, const_sem = refs[14:]
    w_high, w_low = kept[0], kept[1]
    odd = lax.rem(lax.axis_index("gx"), 2)
    levels, count_x = u_ref.shape[:2]

    def fine(level, part):
        source, held = ((u_hbm, u_ref), (v_hbm, v_ref))[part % 2]
        rows = (pl.ds(0, EDGE), pl.ds(count_x - EDGE, EDGE), pl.ds(EDGE, count_x - 2 * EDGE))[part // 2]
        return pltpu.make_async_copy(source.at[level, rows], held.at[level, rows], sem.at[part, level])

    copies = [
        pltpu.make_async_copy(source, held, const_sem.at[k])
        for k, (source, held) in enumerate(zip(consts, (wide, cuu, cuv, cvv) + kept))
    ]
    for part in range(4):
        fine(0, part).start()
    for copy in copies[:4]:
        copy.start()
    for level in range(1, levels):
        for part in range(4):
            fine(level, part).start()
    for copy in copies[4:]:
        copy.start()
    for level in range(levels):
        for part in range(4, 6):
            fine(level, part).start()
    for copy in copies[:4]:
        copy.wait()

    def rows_of(level):
        for part in range(4):
            fine(level, part).wait()
        u, v = (jnp.concatenate([r[level, :EDGE], r[level, count_x - EDGE :]], 0) for r in (u_ref, v_ref))
        _, _, uu, uv, vv = products(u, v)
        last = row_sums(cvv[odd], vv)
        sums = jnp.concatenate(
            [
                row_sums(wide[odd], u) + last[:16],
                row_sums(wide[odd], v) + last[16:],
                row_sums(cuu[odd], uu) + row_sums(cuv[odd], uv),
            ],
            0,
        )
        at = pl.ds(pl.multiple_of(level * 48, 16), 48)
        x_high[at], x_low[at] = split(sums)

    each(levels, EDGE_UNROLL, rows_of)
    for copy in copies[4:6]:
        copy.wait()
    sums = column_sums(x_high[...], x_low[...], w_high[...], w_low[...])
    lanes = e_ref.shape[2]
    for place, ref in ((0, e_ref), (8, o_ref)):
        strips = jnp.zeros((MSG, lanes), F32)
        for level in range(levels):
            part = jnp.concatenate(
                [sums[48 * level + 16 * t + place : 48 * level + 16 * t + place + 8] for t in range(3)], 0
            )
            ref[level] = part[:, :lanes]
            strips = strips + pltpu.roll(part[:, lanes:], WIDE * level, 1)
        ref[levels] = strips
    copies[6].wait()
    for level in range(levels):
        for part in range(4, 6):
            fine(level, part).wait()


def own_kernel(u_ref, v_ref, w_high, w_low, c_ref, p_ref, s_ref, x_high, x_low):
    levels = u_ref.shape[0]
    rows, lanes = s_ref.shape

    def rows_of(level):
        fields = products(u_ref[level], v_ref[level])
        sums = jnp.concatenate([row_sums(c_ref[...], f) for f in fields], 0)
        at = pl.ds(pl.multiple_of(level * rows, 16), rows)
        x_high[at], x_low[at] = split(sums)

    each(levels, OWN_UNROLL, rows_of)
    strips = jnp.zeros((rows, lanes), F32)
    for first in range(0, levels, OWN_CHUNK):
        at = slice(first * rows, (first + OWN_CHUNK) * rows)
        sums = column_sums(x_high[at], x_low[at], w_high[...], w_low[...])
        p_ref[at] = sums[:, :lanes]
        for level in range(first, first + OWN_CHUNK):
            part = sums[(level - first) * rows : (level - first + 1) * rows, lanes:]
            strips = strips + pltpu.roll(part, WIDE * level, 1)
    s_ref[...] = strips


def low_and_high(odd, e, o):
    return jnp.where(odd == 0, o, e), jnp.where(odd == 0, e, o)


def add_rows(wide_refs, short_refs, own_low, own_high, got_low, got_high):
    for k, ref in enumerate(wide_refs):
        count = ref.shape[0]
        at = 8 * k
        ref[0:RIM] = own_low[at + EXT - RIM : at + EXT]
        ref[count - RIM : count] = own_high[at + RIM : at + 2 * RIM]
        ref[0:WIDE] = ref[0:WIDE] + got_low[at : at + WIDE]
        ref[count - WIDE : count] = ref[count - WIDE : count] + got_high[at : at + WIDE]
    for k, ref in enumerate(short_refs):
        count = ref.shape[0]
        if k < 2:
            at = 16 + EXT * k
            ref[0:EXT] = ref[0:EXT] + got_low[at : at + EXT]
            ref[count - EXT : count] = ref[count - EXT : count] + got_high[at : at + EXT]
        else:
            for h in range(2):
                at = 8 * h + WIDE
                ref[2 * h : 2 * h + 2] = ref[2 * h : 2 * h + 2] + got_low[at : at + 2]
                back = count - EXT + 2 * h
                ref[back : back + 2] = ref[back : back + 2] + got_high[at : at + 2]


def strip_kernel(s_ref, own_e, own_o, got_e, got_o, e_ref, o_ref, us, vs, uus, uvs, vvs):
    odd_x = lax.rem(lax.axis_index("gx"), 2)
    odd_y = lax.rem(lax.axis_index("gy"), 2)
    coarse = uus.shape[0]
    us[RIM : RIM + coarse] = s_ref[0:coarse]
    vs[RIM : RIM + coarse] = s_ref[coarse : 2 * coarse]
    uus[...] = s_ref[2 * coarse : 3 * coarse]
    uvs[...] = s_ref[3 * coarse : 4 * coarse]
    vvs[...] = s_ref[4 * coarse : 5 * coarse]
    own_low, own_high = low_and_high(odd_x, own_e[own_e.shape[0] - 1], own_o[own_o.shape[0] - 1])
    got_low, got_high = low_and_high(odd_x, got_e[got_e.shape[0] - 1], got_o[got_o.shape[0] - 1])
    add_rows((us, vs), (uus, uvs, vvs), own_low, own_high, got_low, got_high)
    rim_rows = us.shape[0]
    start = -(-rim_rows // 8) * 8
    pairs = (
        (0, us[...], vs[...]),
        (start, uus[...], uvs[...]),
        (start + coarse, vvs[0 : coarse // 2], vvs[coarse // 2 : coarse]),
    )
    for at, a, b in pairs:
        lane = lax.broadcasted_iota(jnp.int32, a.shape, 1)
        low = jnp.where(lane < HALF, a, pltpu.roll(b, HALF, 1))
        high = jnp.where(lane < HALF, pltpu.roll(a, HALF, 1), b)
        e_ref[at : at + a.shape[0]] = jnp.where(odd_y == 0, high, low)
        o_ref[at : at + a.shape[0]] = jnp.where(odd_y == 0, low, high)


def first_form(plus_two, plus_one, minus_one, minus_two):
    return (8.0 * plus_one - plus_two - 8.0 * minus_one + minus_two) * (1.0 / 12.0)


def second_form(plus_two, plus_one, centre, minus_one, minus_two):
    return (16.0 * plus_one - plus_two - 30.0 * centre + 16.0 * minus_one - minus_two) * (1.0 / 12.0)


def final_kernel(
    p_ref, xe_own, xo_own, xe_got, xo_got, ye_own, yo_own, ye_got, yo_got, st_hbm, lib_hbm,
    us, vs, uus, uvs, vvs, low_side, high_side, slopes, st_ref, lib_ref, sem,
):
    odd_x = lax.rem(lax.axis_index("gx"), 2)
    odd_y = lax.rem(lax.axis_index("gy"), 2)
    levels, coarse, lanes = st_ref.shape[1:]
    rim_rows = us.shape[0]
    own_low, own_high = low_and_high(odd_y, ye_own[...], yo_own[...])
    got_low, got_high = low_and_high(odd_y, ye_got[...], yo_got[...])
    place = lax.rem(lax.rem(lax.broadcasted_iota(jnp.int32, own_low.shape, 1), HALF), WIDE)
    back = pltpu.roll(own_low, lanes - RIM, 1)
    ahead = pltpu.roll(own_high, RIM, 1)
    low_side[...] = got_low + jnp.where(place < RIM, back, 0.0)
    high_side[...] = got_high + jnp.where(place >= EXT, ahead, 0.0)

    def out(level):
        return (
            pltpu.make_async_copy(st_ref.at[:, level], st_hbm.at[:, level], sem.at[0, level]),
            pltpu.make_async_copy(lib_ref.at[:, level], lib_hbm.at[:, level], sem.at[1, level]),
        )

    def finish(level):
        def part_of(k):
            return p_ref[pl.ds(pl.multiple_of((5 * level + k) * coarse, 8), coarse)]

        us[RIM : RIM + coarse] = part_of(0)
        vs[RIM : RIM + coarse] = part_of(1)
        for k, ref in enumerate((uus, uvs, vvs)):
            ref[...] = part_of(2 + k)
        own_low, own_high = low_and_high(odd_x, xe_own[level], xo_own[level])
        got_low, got_high = low_and_high(odd_x, xe_got[level], xo_got[level])
        add_rows((us, vs), (uus, uvs, vvs), own_low, own_high, got_low, got_high)

        shift = WIDE * level

        def sides(at, count, second):
            base = HALF if second else 0
            low = pltpu.roll(low_side[at : at + count], lanes - RIM - base - shift, 1)
            high = pltpu.roll(high_side[at : at + count], lanes - EXT - base - shift, 1)
            return low, high

        def joined(field, low, high):
            lane = lax.broadcasted_iota(jnp.int32, field.shape, 1)
            return field + jnp.where(lane < EXT, low, 0.0) + jnp.where(lane >= lanes - EXT, high, 0.0)

        means = []
        found = []
        for k, ref in enumerate((us, vs)):
            low, high = sides(0, rim_rows, k == 1)
            f = joined(ref[...], low, high)
            ref[...] = f
            lane = lax.broadcasted_iota(jnp.int32, f.shape, 1)
            plus_one = pltpu.roll(jnp.where(lane < 1, high, f), lanes - 1, 1)
            plus_two = pltpu.roll(jnp.where(lane < 2, high, f), lanes - 2, 1)
            minus_one = pltpu.roll(jnp.where(lane >= lanes - 1, low, f), 1, 1)
            minus_two = pltpu.roll(jnp.where(lane >= lanes - 2, low, f), 2, 1)
            slopes[...] = first_form(plus_two, plus_one, minus_one, minus_two)

            def row(source, by):
                return source[RIM + by : RIM + by + coarse]

            curve_y = second_form(plus_two, plus_one, f, minus_one, minus_two)[RIM : RIM + coarse]
            centre = row(ref, 0)
            shifted = [row(ref, by) for by in (2, 1, -1, -2)]
            grad_x = first_form(*shifted)
            curve_x = second_form(shifted[0], shifted[1], centre, shifted[2], shifted[3])
            grad_y = row(slopes, 0)
            cross = first_form(*[row(slopes, by) for by in (2, 1, -1, -2)])
            means.append(centre)
            found.append((grad_x, grad_y, curve_x, cross, curve_y))

        u, v = means
        start = -(-rim_rows // 8) * 8
        low, high = sides(start, coarse, False)
        st_ref[0, level] = joined(uus[...], low, high) - u * u
        low, high = sides(start, coarse, True)
        st_ref[1, level] = joined(uvs[...], low, high) - u * v
        for h in range(2):
            part = slice(coarse // 2 * h, coarse // 2 * (h + 1))
            low, high = sides(start + coarse, coarse // 2, h == 1)
            st_ref[2, level, part] = joined(vvs[part], low, high) - v[part] * v[part]

        (ux, uy, uxx, uxy, uyy), (vx, vy, vxx, vxy, vyy) = found
        vorticity = vx - uy
        features = (ux, uy, vx, vy, uxx, uxy, uyy, vxx, vxy, vyy, vxx - uxy, vxy - uyy)
        for k, feature in enumerate(features):
            lib_ref[4 * k, level] = feature
            lib_ref[4 * k + 1, level] = u * feature
            lib_ref[4 * k + 2, level] = v * feature
            lib_ref[4 * k + 3, level] = vorticity * feature
        for copy in out(level):
            copy.start()

    each(levels, FINAL_UNROLL, finish)
    for level in range(levels):
        for copy in out(level):
            copy.wait()


def swapped(axis, even, odd):
    count = lax.axis_size(axis)
    assert count % 2 == 0
    pairs = [(i, i ^ 1) for i in range(count)]
    others = [(i, (i + 1) % count if i % 2 else (i - 1) % count) for i in range(count)]
    return lax.ppermute(even, axis, pairs), lax.ppermute(odd, axis, others)


def local_call(body, outs, scratch, name, *operands):
    in_vmem, in_hbm = pl.BlockSpec(memory_space=pltpu.VMEM), pl.BlockSpec(memory_space=pltpu.HBM)
    specs, arrays = [], []
    for operand, here in operands:
        specs.append(in_vmem if here else in_hbm)
        arrays.append(pltpu.with_memory_space_constraint(operand, pltpu.VMEM) if here else pltpu.with_memory_space_constraint(operand, pltpu.HBM))
    return pl.pallas_call(
        body,
        in_specs=specs,
        out_specs=[in_hbm if isinstance(o, jax.ShapeDtypeStruct) else in_vmem for o in outs],
        out_shape=outs,
        scratch_shapes=scratch,
        compiler_params=pltpu.CompilerParams(vmem_limit_bytes=VMEM_BYTES),
        name=name,
    )(*arrays)


def per_device(east_flow, north_flow):
    levels, count_x, count_y = east_flow.shape
    coarse, lanes = count_x // STEP, count_y // STEP
    assert lanes == 2 * HALF and WIDE * levels <= HALF and coarse % 16 == 0
    consts = message_rows(count_x) + column_weights(count_y) + (left_operand(taps(range(coarse), count_x)),)
    consts = [jnp.asarray(c) for c in consts]
    rim_rows = coarse + 2 * RIM
    start = -(-rim_rows // 8) * 8
    side = (start + coarse + coarse // 2, lanes)
    message = (levels + 1, MSG, lanes)
    held = [pltpu.VMEM(c.shape, BF16) for c in consts]
    f32 = functools.partial(pltpu.VMEM, dtype=F32)

    xe, xo, u, v, *kept = local_call(
        edge_kernel,
        [f32(message), f32(message), f32(east_flow.shape), f32(north_flow.shape)] + held[4:],
        held[:4]
        + [pltpu.VMEM((48 * levels, count_y), BF16)] * 2
        + [pltpu.SemaphoreType.DMA((6, levels)), pltpu.SemaphoreType.DMA((7,))],
        "edge",
        (east_flow, False),
        (north_flow, False),
        *[(c, False) for c in consts],
    )
    xe_got, xo_got = swapped("gx", xe, xo)
    partial_sums, strips = local_call(
        own_kernel,
        [f32((levels * 5 * coarse, lanes)), f32((5 * coarse, lanes))],
        [pltpu.VMEM((levels * 5 * coarse, count_y), BF16)] * 2,
        "own",
        *[(a, True) for a in (u, v, *kept)],
    )
    rows = [f32((rim_rows, lanes))] * 2 + [f32((coarse, lanes))] * 3
    along_x = [(a, True) for a in (xe, xo, xe_got, xo_got)]
    ye, yo = local_call(strip_kernel, [f32(side)] * 2, rows, "strips", (strips, True), *along_x)
    ye_got, yo_got = swapped("gy", ye, yo)
    outs = [jax.ShapeDtypeStruct((n, levels, coarse, lanes), F32) for n in (3, 48)]
    return local_call(
        final_kernel,
        outs,
        rows
        + [f32(side)] * 2
        + [f32((rim_rows, lanes))]
        + [f32(o.shape) for o in outs]
        + [pltpu.SemaphoreType.DMA((2, levels))],
        "final",
        (partial_sums, True),
        *along_x,
        *[(a, True) for a in (ye, yo, ye_got, yo_got)],
    )


def solution(mesh):
    return jax.shard_map(
        per_device,
        mesh=mesh,
        in_specs=(P(None, "gx", "gy"), P(None, "gx", "gy")),
        out_specs=(P(None, None, "gx", "gy"), P(None, None, "gx", "gy")),
        check_vma=False,
    )
```

```python
import functools

import jax
import jax.numpy as jnp
import numpy as np
from jax import lax
from jax.experimental import pallas as pl
from jax.experimental.pallas import tpu as pltpu
from jax.sharding import PartitionSpec as P

spread_cells = 5.5
REACH = 16
STEP = 4
EXT = REACH // STEP
RIM = 2
WIDE = EXT + RIM
EDGE = 24
SHORT = 16
SIDE = 128
HALF = 64
MSG = 24
F32, BF16 = jnp.float32, jnp.bfloat16
VMEM_BYTES = 24 << 20
SLAB_UNROLL, MAIN_UNROLL, OWN_UNROLL, FINAL_UNROLL = 2, 2, 4, 1


def taps(cells, count_in):
    offsets = np.arange(2 * REACH + 1) - REACH
    bumps = np.exp(-0.5 * (offsets / spread_cells) ** 2)
    lag = np.arange(count_in)[None, :] - STEP * np.asarray(cells)[:, None]
    inside = np.abs(lag) <= REACH
    return np.where(inside, np.exp(-0.5 * (lag / spread_cells) ** 2), 0.0) / bumps.sum()


def pieces(values):
    high = values.astype(BF16)
    low = (values - high.astype(np.float64)).astype(BF16)
    return high, low


def left_operand(*sources):
    tops, bottoms = [], []
    for rows in sources:
        high, low = pieces(rows)
        tops += [high, high]
        bottoms += [low, np.zeros_like(low)]
    return np.concatenate([np.concatenate(tops, 1), np.concatenate(bottoms, 1)], 0)


def message_rows(count_x):
    coarse = count_x // STEP

    def rows(cells, ends):
        full = taps(cells, count_x)
        return np.concatenate([full[:, :ends], full[:, count_x - ends :]], 1)

    wide = {"low": rows(range(-EXT, RIM), EDGE), "high": rows(range(coarse - RIM, coarse + EXT), EDGE)}
    short = {"low": rows(range(-EXT, 0), SHORT), "high": rows(range(coarse, coarse + EXT), SHORT)}

    def placed(at, parts):
        blocks = []
        for part in parts:
            block = np.zeros((8, part.shape[1]))
            block[at : at + part.shape[0]] = part
            blocks.append(block)
        return np.concatenate(blocks, 0)

    three, two = [], []
    for sides in (("high", "low"), ("low", "high")):
        w = placed(0, [wide[s] for s in sides])
        none = np.zeros_like(w)
        vv = [placed(WIDE, [short[s][2 * h : 2 * h + 2] for s in sides]) for h in range(2)]
        three.append(left_operand(np.concatenate([w, none]), np.concatenate([none, w]), np.concatenate(vv)))
        two.append(left_operand(*[placed(EXT * h, [short[s] for s in sides]) for h in range(2)]))
    return np.stack(three), np.stack(two)


def column_weights(count_y):
    coarse = count_y // STEP
    own = taps(range(coarse), count_y).T
    strips = np.zeros((count_y, 2 * HALF))
    strips[:, :WIDE] = taps(range(-EXT, RIM), count_y).T
    strips[:, HALF : HALF + WIDE] = taps(range(coarse - RIM, coarse + EXT), count_y).T

    def ends(w):
        return np.concatenate([w[:SIDE], w[count_y - SIDE :]], 0)

    return tuple(np.concatenate(pieces(w), 1) for w in (ends(strips), ends(own), own[SIDE : count_y - SIDE]))


def split(values):
    high = values.astype(BF16)
    return high, (values - high.astype(F32)).astype(BF16)


def row_sums(left, field):
    high, low = split(field)
    both = jnp.dot(left, jnp.concatenate([high, low], 0), preferred_element_type=F32)
    half = both.shape[0] // 2
    return both[:half] + both[half:]


def column_sums(high, low, weights):
    count = weights.shape[1] // 2
    both = jnp.dot(high, weights[...], preferred_element_type=F32)
    return both[:, :count] + both[:, count:] + jnp.dot(low, weights[:, :count], preferred_element_type=F32)


def products(u, v):
    return u, v, u * u, u * v, v * v


def each(count, unroll, body):
    lax.fori_loop(0, count, lambda i, _: (body(i), None)[1], None, unroll=unroll)


def message_sums(three, two, u, v):
    us, vs = (jnp.concatenate([f[:SHORT], f[2 * EDGE - SHORT :]], 0) for f in (u, v))
    first = jnp.concatenate([*split(u), *split(v), *split(vs * vs)], 0)
    second = jnp.concatenate([*split(us * us), *split(us * vs)], 0)
    first = jnp.dot(three, first, preferred_element_type=F32)
    second = jnp.dot(two, second, preferred_element_type=F32)
    return jnp.concatenate([first[:32] + first[32:], second[:16] + second[16:]], 0)


def slab_kernel(
    u_hbm, v_hbm, three_hbm, two_hbm, w_hbm, w_ends_hbm, w_rest_hbm, left_hbm,
    e_ref, o_ref, x_high, x_low, three, two, weights, w_ends, w_rest, left,
    u_ref, v_ref, sem, const_sem,
):
    odd = lax.rem(lax.axis_index("gx"), 2)
    levels = u_ref.shape[0]
    _, count_x, count_y = u_hbm.shape
    parts = sem.shape[0]
    batch = levels // parts

    def loads(part):
        some = pl.ds(part * batch, batch)
        copies = []
        for f, (source, held) in enumerate(((u_hbm, u_ref), (v_hbm, v_ref))):
            for r in range(2):
                for c in range(2):
                    copies.append(
                        pltpu.make_async_copy(
                            source.at[
                                some, pl.ds(r * (count_x - EDGE), EDGE), pl.ds(c * (count_y - SIDE), SIDE)
                            ],
                            held.at[some, pl.ds(r * EDGE, EDGE), pl.ds(c * SIDE, SIDE)],
                            sem.at[part, 4 * f + 2 * r + c],
                        )
                    )
        return copies

    consts = [
        pltpu.make_async_copy(source, held, const_sem.at[k])
        for k, (source, held) in enumerate(
            (
                (three_hbm, three),
                (two_hbm, two),
                (w_hbm, weights),
                (left_hbm, left),
                (w_ends_hbm, w_ends),
                (w_rest_hbm, w_rest),
            )
        )
    ]
    for copy in loads(0) + consts[:2]:
        copy.start()
    for part in range(1, parts):
        for copy in loads(part):
            copy.start()
    for copy in consts[2:]:
        copy.start()
    for copy in consts[:2]:
        copy.wait()
    for part in range(parts):
        for copy in loads(part):
            copy.wait()

        def rows_of(i, part=part):
            level = part * batch + i
            at = pl.ds(pl.multiple_of(level * 48, 16), 48)
            x_high[at], x_low[at] = split(message_sums(three[odd], two[odd], u_ref[level], v_ref[level]))

        each(batch, SLAB_UNROLL, rows_of)
    consts[2].wait()
    sums = column_sums(x_high[...], x_low[...], weights)
    for place, ref in ((0, e_ref), (8, o_ref)):
        strips = jnp.zeros(ref.shape, F32)
        for level in range(levels):
            strips = strips + pltpu.roll(message_of(sums, level, place), WIDE * level, 1)
        ref[...] = strips
    for copy in consts[3:]:
        copy.wait()


def message_of(sums, level, place):
    return jnp.concatenate([sums[48 * level + 16 * t + place : 48 * level + 16 * t + place + 8] for t in range(3)], 0)


def middle(ref):
    count_y = ref.shape[-1]
    return pl.ds(SIDE, count_y - 2 * SIDE)


def main_kernel(u_ref, v_ref, three, two, ends_high, ends_low, w_ends, w_rest, e_ref, o_ref, x_high, x_low):
    odd = lax.rem(lax.axis_index("gx"), 2)
    levels, count_x = u_ref.shape[:2]

    def rows_of(level):
        u, v = (
            jnp.concatenate([r[level, :EDGE, middle(r)], r[level, count_x - EDGE :, middle(r)]], 0)
            for r in (u_ref, v_ref)
        )
        at = pl.ds(pl.multiple_of(level * 48, 16), 48)
        x_high[at], x_low[at] = split(message_sums(three[odd], two[odd], u, v))

    each(levels, MAIN_UNROLL, rows_of)
    sums = column_sums(ends_high[...], ends_low[...], w_ends) + column_sums(x_high[...], x_low[...], w_rest)
    for place, ref in ((0, e_ref), (8, o_ref)):
        for level in range(levels):
            ref[level] = message_of(sums, level, place)


def own_rows_of(left, u, v):
    return split(jnp.concatenate([row_sums(left, f) for f in products(u, v)], 0))


def ends_kernel(u_ref, v_ref, left, weights, s_ref, x_high, x_low):
    levels, _, count_y = u_ref.shape
    rows, lanes = s_ref.shape

    def rows_of(level):
        u, v = (
            jnp.concatenate([r[level, :, :SIDE], r[level, :, count_y - SIDE :]], 1) for r in (u_ref, v_ref)
        )
        at = pl.ds(pl.multiple_of(level * rows, 16), rows)
        x_high[at], x_low[at] = own_rows_of(left[...], u, v)

    each(levels, OWN_UNROLL, rows_of)
    strips = jnp.zeros((rows, lanes), F32)
    for level in range(levels):
        at = slice(level * rows, (level + 1) * rows)
        strips = strips + pltpu.roll(column_sums(x_high[at], x_low[at], weights), WIDE * level, 1)
    s_ref[...] = strips


def own_kernel(u_ref, v_ref, left, ends_high, ends_low, w_ends, w_rest, p_ref, x_high, x_low):
    levels = u_ref.shape[0]
    rows = p_ref.shape[0] // levels

    def rows_of(level):
        at = pl.ds(pl.multiple_of(level * rows, 16), rows)
        x_high[at], x_low[at] = own_rows_of(left[...], u_ref[level, :, middle(u_ref)], v_ref[level, :, middle(v_ref)])

    each(levels, OWN_UNROLL, rows_of)
    for level in range(0, levels, 2):
        at = slice(level * rows, (level + 2) * rows)
        p_ref[at] = column_sums(ends_high[at], ends_low[at], w_ends) + column_sums(x_high[at], x_low[at], w_rest)


def low_and_high(odd, e, o):
    return jnp.where(odd == 0, o, e), jnp.where(odd == 0, e, o)


def add_rows(wide_refs, short_refs, own_low, own_high, got_low, got_high):
    for k, ref in enumerate(wide_refs):
        count = ref.shape[0]
        at = 8 * k
        ref[0:RIM] = own_low[at + EXT - RIM : at + EXT]
        ref[count - RIM : count] = own_high[at + RIM : at + 2 * RIM]
        ref[0:WIDE] = ref[0:WIDE] + got_low[at : at + WIDE]
        ref[count - WIDE : count] = ref[count - WIDE : count] + got_high[at : at + WIDE]
    for k, ref in enumerate(short_refs):
        count = ref.shape[0]
        if k < 2:
            at = 16 + EXT * k
            ref[0:EXT] = ref[0:EXT] + got_low[at : at + EXT]
            ref[count - EXT : count] = ref[count - EXT : count] + got_high[at : at + EXT]
        else:
            for h in range(2):
                at = 8 * h + WIDE
                ref[2 * h : 2 * h + 2] = ref[2 * h : 2 * h + 2] + got_low[at : at + 2]
                back = count - EXT + 2 * h
                ref[back : back + 2] = ref[back : back + 2] + got_high[at : at + 2]


def strip_kernel(s_ref, own_e, own_o, got_e, got_o, e_ref, o_ref, us, vs, uus, uvs, vvs):
    odd_x = lax.rem(lax.axis_index("gx"), 2)
    odd_y = lax.rem(lax.axis_index("gy"), 2)
    coarse = uus.shape[0]
    us[RIM : RIM + coarse] = s_ref[0:coarse]
    vs[RIM : RIM + coarse] = s_ref[coarse : 2 * coarse]
    uus[...] = s_ref[2 * coarse : 3 * coarse]
    uvs[...] = s_ref[3 * coarse : 4 * coarse]
    vvs[...] = s_ref[4 * coarse : 5 * coarse]
    own_low, own_high = low_and_high(odd_x, own_e[...], own_o[...])
    got_low, got_high = low_and_high(odd_x, got_e[...], got_o[...])
    add_rows((us, vs), (uus, uvs, vvs), own_low, own_high, got_low, got_high)
    rim_rows = us.shape[0]
    start = -(-rim_rows // 8) * 8
    pairs = (
        (0, us[...], vs[...]),
        (start, uus[...], uvs[...]),
        (start + coarse, vvs[0 : coarse // 2], vvs[coarse // 2 : coarse]),
    )
    for at, a, b in pairs:
        lane = lax.broadcasted_iota(jnp.int32, a.shape, 1)
        low = jnp.where(lane < HALF, a, pltpu.roll(b, HALF, 1))
        high = jnp.where(lane < HALF, pltpu.roll(a, HALF, 1), b)
        e_ref[at : at + a.shape[0]] = jnp.where(odd_y == 0, high, low)
        o_ref[at : at + a.shape[0]] = jnp.where(odd_y == 0, low, high)


def first_form(plus_two, plus_one, minus_one, minus_two):
    return (8.0 * plus_one - plus_two - 8.0 * minus_one + minus_two) * (1.0 / 12.0)


def second_form(plus_two, plus_one, centre, minus_one, minus_two):
    return (16.0 * plus_one - plus_two - 30.0 * centre + 16.0 * minus_one - minus_two) * (1.0 / 12.0)


def final_kernel(
    p_ref, xe_own, xo_own, xe_got, xo_got, ye_own, yo_own, ye_got, yo_got, st_hbm, lib_hbm,
    us, vs, uus, uvs, vvs, low_side, high_side, slopes, st_ref, lib_ref, sem,
):
    odd_x = lax.rem(lax.axis_index("gx"), 2)
    odd_y = lax.rem(lax.axis_index("gy"), 2)
    levels, coarse, lanes = st_ref.shape[1:]
    rim_rows = us.shape[0]
    own_low, own_high = low_and_high(odd_y, ye_own[...], yo_own[...])
    got_low, got_high = low_and_high(odd_y, ye_got[...], yo_got[...])
    place = lax.rem(lax.rem(lax.broadcasted_iota(jnp.int32, own_low.shape, 1), HALF), WIDE)
    back = pltpu.roll(own_low, lanes - RIM, 1)
    ahead = pltpu.roll(own_high, RIM, 1)
    low_side[...] = got_low + jnp.where(place < RIM, back, 0.0)
    high_side[...] = got_high + jnp.where(place >= EXT, ahead, 0.0)

    def out(level):
        return (
            pltpu.make_async_copy(st_ref.at[:, level], st_hbm.at[:, level], sem.at[0, level]),
            pltpu.make_async_copy(lib_ref.at[:, level], lib_hbm.at[:, level], sem.at[1, level]),
        )

    def finish(level):
        def part_of(k):
            return p_ref[pl.ds(pl.multiple_of((5 * level + k) * coarse, 8), coarse)]

        us[RIM : RIM + coarse] = part_of(0)
        vs[RIM : RIM + coarse] = part_of(1)
        for k, ref in enumerate((uus, uvs, vvs)):
            ref[...] = part_of(2 + k)
        own_low, own_high = low_and_high(odd_x, xe_own[level], xo_own[level])
        got_low, got_high = low_and_high(odd_x, xe_got[level], xo_got[level])
        add_rows((us, vs), (uus, uvs, vvs), own_low, own_high, got_low, got_high)

        shift = WIDE * level

        def sides(at, count, second):
            base = HALF if second else 0
            low = pltpu.roll(low_side[at : at + count], lanes - RIM - base - shift, 1)
            high = pltpu.roll(high_side[at : at + count], lanes - EXT - base - shift, 1)
            return low, high

        def joined(field, low, high):
            lane = lax.broadcasted_iota(jnp.int32, field.shape, 1)
            return field + jnp.where(lane < EXT, low, 0.0) + jnp.where(lane >= lanes - EXT, high, 0.0)

        means = []
        found = []
        for k, ref in enumerate((us, vs)):
            low, high = sides(0, rim_rows, k == 1)
            f = joined(ref[...], low, high)
            ref[...] = f
            lane = lax.broadcasted_iota(jnp.int32, f.shape, 1)
            plus_one = pltpu.roll(jnp.where(lane < 1, high, f), lanes - 1, 1)
            plus_two = pltpu.roll(jnp.where(lane < 2, high, f), lanes - 2, 1)
            minus_one = pltpu.roll(jnp.where(lane >= lanes - 1, low, f), 1, 1)
            minus_two = pltpu.roll(jnp.where(lane >= lanes - 2, low, f), 2, 1)
            slopes[...] = first_form(plus_two, plus_one, minus_one, minus_two)

            def row(source, by):
                return source[RIM + by : RIM + by + coarse]

            curve_y = second_form(plus_two, plus_one, f, minus_one, minus_two)[RIM : RIM + coarse]
            centre = row(ref, 0)
            shifted = [row(ref, by) for by in (2, 1, -1, -2)]
            grad_x = first_form(*shifted)
            curve_x = second_form(shifted[0], shifted[1], centre, shifted[2], shifted[3])
            grad_y = row(slopes, 0)
            cross = first_form(*[row(slopes, by) for by in (2, 1, -1, -2)])
            means.append(centre)
            found.append((grad_x, grad_y, curve_x, cross, curve_y))

        u, v = means
        start = -(-rim_rows // 8) * 8
        low, high = sides(start, coarse, False)
        st_ref[0, level] = joined(uus[...], low, high) - u * u
        low, high = sides(start, coarse, True)
        st_ref[1, level] = joined(uvs[...], low, high) - u * v
        for h in range(2):
            part = slice(coarse // 2 * h, coarse // 2 * (h + 1))
            low, high = sides(start + coarse, coarse // 2, h == 1)
            st_ref[2, level, part] = joined(vvs[part], low, high) - v[part] * v[part]

        (ux, uy, uxx, uxy, uyy), (vx, vy, vxx, vxy, vyy) = found
        vorticity = vx - uy
        features = (ux, uy, vx, vy, uxx, uxy, uyy, vxx, vxy, vyy, vxx - uxy, vxy - uyy)
        for k, feature in enumerate(features):
            lib_ref[4 * k, level] = feature
            lib_ref[4 * k + 1, level] = u * feature
            lib_ref[4 * k + 2, level] = v * feature
            lib_ref[4 * k + 3, level] = vorticity * feature
        for copy in out(level):
            copy.start()

    each(levels, FINAL_UNROLL, finish)
    for level in range(levels):
        for copy in out(level):
            copy.wait()


def swapped(axis, even, odd):
    count = lax.axis_size(axis)
    assert count % 2 == 0
    pairs = [(i, i ^ 1) for i in range(count)]
    others = [(i, (i + 1) % count if i % 2 else (i - 1) % count) for i in range(count)]
    return lax.ppermute(even, axis, pairs), lax.ppermute(odd, axis, others)


def local_call(body, outs, scratch, *operands):
    in_vmem, in_hbm = pl.BlockSpec(memory_space=pltpu.VMEM), pl.BlockSpec(memory_space=pltpu.HBM)
    specs, arrays = [], []
    for operand, here in operands:
        specs.append(in_vmem if here else in_hbm)
        arrays.append(pltpu.with_memory_space_constraint(operand, pltpu.VMEM) if here else pltpu.with_memory_space_constraint(operand, pltpu.HBM))
    return pl.pallas_call(
        body,
        in_specs=specs,
        out_specs=[in_hbm if isinstance(o, jax.ShapeDtypeStruct) else in_vmem for o in outs],
        out_shape=outs,
        scratch_shapes=scratch,
        compiler_params=pltpu.CompilerParams(vmem_limit_bytes=VMEM_BYTES),
    )(*arrays)


def in_order(east_flow, north_flow):
    levels, count_x, count_y = east_flow.shape
    coarse, lanes = count_x // STEP, count_y // STEP
    assert lanes == 2 * HALF and WIDE * levels <= HALF and coarse % 16 == 0
    assert count_x >= 2 * EDGE and count_y > 2 * SIDE
    three, two = (jnp.asarray(c) for c in message_rows(count_x))
    w_strips, w_ends, w_rest = (jnp.asarray(c) for c in column_weights(count_y))
    left = jnp.asarray(left_operand(taps(range(coarse), count_x)))
    rim_rows = coarse + 2 * RIM
    start = -(-rim_rows // 8) * 8
    side = (start + coarse + coarse // 2, lanes)
    own_count = 5 * coarse
    f32, bf16 = functools.partial(pltpu.VMEM, dtype=F32), functools.partial(pltpu.VMEM, dtype=BF16)

    def held(*arrays):
        return [(a, True) for a in arrays]

    parts = 2
    consts = (three, two, w_strips, w_ends, w_rest, left)
    se, so, ends_high, ends_low, *kept = local_call(
        slab_kernel,
        [f32((MSG, lanes))] * 2 + [bf16((48 * levels, 2 * SIDE))] * 2 + [bf16(c.shape) for c in consts],
        [f32((levels, 2 * EDGE, 2 * SIDE))] * 2
        + [pltpu.SemaphoreType.DMA((parts, 8)), pltpu.SemaphoreType.DMA((len(consts),))],
        *[(a, False) for a in (east_flow, north_flow) + consts],
    )
    message_ends = (ends_high, ends_low)
    three, two, w_strips, w_ends, w_rest, left = kept
    se_got, so_got = swapped("gx", se, so)
    fine = held(east_flow, north_flow)
    xe, xo = local_call(
        main_kernel,
        [f32((levels, MSG, lanes))] * 2,
        [bf16((48 * levels, count_y - 2 * SIDE))] * 2,
        *fine,
        *held(three, two, *message_ends, w_ends, w_rest),
    )
    xe_got, xo_got = swapped("gx", xe, xo)
    strips, *own_ends = local_call(
        ends_kernel,
        [f32((own_count, lanes))] + [bf16((own_count * levels, 2 * SIDE))] * 2,
        [],
        *fine,
        *held(left, w_strips),
    )
    rows = [f32((rim_rows, lanes))] * 2 + [f32((coarse, lanes))] * 3
    ye, yo = local_call(strip_kernel, [f32(side)] * 2, rows, *held(strips, se, so, se_got, so_got))
    ye_got, yo_got = swapped("gy", ye, yo)
    (partial_sums,) = local_call(
        own_kernel,
        [f32((own_count * levels, lanes))],
        [bf16((own_count * levels, count_y - 2 * SIDE))] * 2,
        *fine,
        *held(left, *own_ends, w_ends, w_rest),
    )
    outs = [jax.ShapeDtypeStruct((n, levels, coarse, lanes), F32) for n in (3, 48)]
    return local_call(
        final_kernel,
        outs,
        rows
        + [f32(side)] * 2
        + [f32((rim_rows, lanes))]
        + [f32(o.shape) for o in outs]
        + [pltpu.SemaphoreType.DMA((2, levels))],
        *held(partial_sums, xe, xo, xe_got, xo_got, ye, yo, ye_got, yo_got),
    )


def solution(mesh):
    return jax.shard_map(
        in_order,
        mesh=mesh,
        in_specs=(P(None, "gx", "gy"), P(None, "gx", "gy")),
        out_specs=(P(None, None, "gx", "gy"), P(None, None, "gx", "gy")),
        check_vma=False,
    )
```

```python
import functools

import jax
import jax.numpy as jnp
import numpy as np
from jax import lax
from jax.experimental import pallas as pl
from jax.experimental.pallas import tpu as pltpu
from jax.sharding import PartitionSpec as P

spread_cells = 5.5
REACH = 16
STEP = 4
EXT = REACH // STEP
RIM = 2
WIDE = EXT + RIM
EDGE = 24
SHORT = 16
SIDE = 128
HALF = 64
MSG = 24
F32, BF16 = jnp.float32, jnp.bfloat16
VMEM_BYTES = 24 << 20
MAIN_UNROLL, OWN_UNROLL, FINAL_UNROLL = 8, 8, 1


def taps(cells, count_in):
    offsets = np.arange(2 * REACH + 1) - REACH
    bumps = np.exp(-0.5 * (offsets / spread_cells) ** 2)
    lag = np.arange(count_in)[None, :] - STEP * np.asarray(cells)[:, None]
    inside = np.abs(lag) <= REACH
    return np.where(inside, np.exp(-0.5 * (lag / spread_cells) ** 2), 0.0) / bumps.sum()


def pieces(values):
    high = values.astype(BF16)
    low = (values - high.astype(np.float64)).astype(BF16)
    return high, low


def left_operand(*sources):
    tops, bottoms = [], []
    for rows in sources:
        high, low = pieces(rows)
        tops += [high, high]
        bottoms += [low, np.zeros_like(low)]
    return np.concatenate([np.concatenate(tops, 1), np.concatenate(bottoms, 1)], 0)


def message_rows(count_x):
    coarse = count_x // STEP

    def rows(cells, ends):
        full = taps(cells, count_x)
        return np.concatenate([full[:, :ends], full[:, count_x - ends :]], 1)

    wide = {"low": rows(range(-EXT, RIM), EDGE), "high": rows(range(coarse - RIM, coarse + EXT), EDGE)}
    short = {"low": rows(range(-EXT, 0), SHORT), "high": rows(range(coarse, coarse + EXT), SHORT)}

    def placed(at, parts):
        blocks = []
        for part in parts:
            block = np.zeros((8, part.shape[1]))
            block[at : at + part.shape[0]] = part
            blocks.append(block)
        return np.concatenate(blocks, 0)

    three, two = [], []
    for sides in (("high", "low"), ("low", "high")):
        w = placed(0, [wide[s] for s in sides])
        none = np.zeros_like(w)
        vv = [placed(WIDE, [short[s][2 * h : 2 * h + 2] for s in sides]) for h in range(2)]
        three.append(left_operand(np.concatenate([w, none]), np.concatenate([none, w]), np.concatenate(vv)))
        two.append(left_operand(*[placed(EXT * h, [short[s] for s in sides]) for h in range(2)]))
    return np.stack(three), np.stack(two)


def column_weights(count_y):
    coarse = count_y // STEP
    own = taps(range(coarse), count_y).T
    strips = np.zeros((count_y, 2 * HALF))
    strips[:, :WIDE] = taps(range(-EXT, RIM), count_y).T
    strips[:, HALF : HALF + WIDE] = taps(range(coarse - RIM, coarse + EXT), count_y).T

    def ends(w):
        return np.concatenate([w[:SIDE], w[count_y - SIDE :]], 0)

    return tuple(np.concatenate(pieces(w), 1) for w in (ends(strips), ends(own), own[SIDE : count_y - SIDE]))


def split(values):
    high = values.astype(BF16)
    return high, (values - high.astype(F32)).astype(BF16)


def row_sums(left, field):
    high, low = split(field)
    both = jnp.dot(left, jnp.concatenate([high, low], 0), preferred_element_type=F32)
    half = both.shape[0] // 2
    return both[:half] + both[half:]


def column_sums(high, low, weights):
    count = weights.shape[1] // 2
    both = jnp.dot(high, weights[...], preferred_element_type=F32)
    return both[:, :count] + both[:, count:] + jnp.dot(low, weights[:, :count], preferred_element_type=F32)


def products(u, v):
    return u, v, u * u, u * v, v * v


def each(count, unroll, body):
    lax.fori_loop(0, count, lambda i, _: (body(i), None)[1], None, unroll=unroll)


def message_sums(three, two, u, v):
    us, vs = (jnp.concatenate([f[:SHORT], f[2 * EDGE - SHORT :]], 0) for f in (u, v))
    first = jnp.concatenate([*split(u), *split(v), *split(vs * vs)], 0)
    second = jnp.concatenate([*split(us * us), *split(us * vs)], 0)
    first = jnp.dot(three, first, preferred_element_type=F32)
    second = jnp.dot(two, second, preferred_element_type=F32)
    return jnp.concatenate([first[:32] + first[32:], second[:16] + second[16:]], 0)


def slab_kernel(
    u_hbm, v_hbm, three_hbm, two_hbm, w_hbm, w_ends_hbm, w_rest_hbm, left_hbm,
    e_ref, o_ref, x_high, x_low, three, two, weights, w_ends, w_rest, left,
    u_ref, v_ref, sem, const_sem,
):
    odd = lax.rem(lax.axis_index("gx"), 2)
    levels = u_ref.shape[0]
    _, count_x, count_y = u_hbm.shape
    parts = sem.shape[0]
    batch = levels // parts

    def loads(part):
        some = pl.ds(part * batch, batch)
        copies = []
        for f, (source, held) in enumerate(((u_hbm, u_ref), (v_hbm, v_ref))):
            for r in range(2):
                for c in range(2):
                    copies.append(
                        pltpu.make_async_copy(
                            source.at[
                                some, pl.ds(r * (count_x - EDGE), EDGE), pl.ds(c * (count_y - SIDE), SIDE)
                            ],
                            held.at[some, pl.ds(r * EDGE, EDGE), pl.ds(c * SIDE, SIDE)],
                            sem.at[part, 4 * f + 2 * r + c],
                        )
                    )
        return copies

    consts = [
        pltpu.make_async_copy(source, held, const_sem.at[k])
        for k, (source, held) in enumerate(
            (
                (three_hbm, three),
                (two_hbm, two),
                (w_hbm, weights),
                (left_hbm, left),
                (w_ends_hbm, w_ends),
                (w_rest_hbm, w_rest),
            )
        )
    ]
    for copy in loads(0) + consts[:3]:
        copy.start()
    for part in range(1, parts):
        for copy in loads(part):
            copy.start()
    for copy in consts[3:]:
        copy.start()
    for copy in consts[:3]:
        copy.wait()
    for part in range(parts):
        for copy in loads(part):
            copy.wait()

        for level in range(part * batch, (part + 1) * batch):
            at = slice(level * 48, (level + 1) * 48)
            x_high[at], x_low[at] = split(message_sums(three[odd], two[odd], u_ref[level], v_ref[level]))
    sums = column_sums(x_high[...], x_low[...], weights)
    for place, ref in ((0, e_ref), (8, o_ref)):
        strips = [pltpu.roll(message_of(sums, level, place), WIDE * level, 1) for level in range(levels)]
        ref[...] = added(strips)
    for copy in consts[3:]:
        copy.wait()


def added(terms):
    while len(terms) > 1:
        terms = [a + b for a, b in zip(terms[::2], terms[1::2])] + terms[len(terms) & ~1 :]
    return terms[0]


def message_of(sums, level, place):
    return jnp.concatenate([sums[48 * level + 16 * t + place : 48 * level + 16 * t + place + 8] for t in range(3)], 0)


def middle(ref):
    count_y = ref.shape[-1]
    return pl.ds(SIDE, count_y - 2 * SIDE)


def main_kernel(
    u_ref, v_ref, three, two, ends_high, ends_low, w_ends, w_rest, slab_ref, e_ref, o_ref, x_high, x_low
):
    odd = lax.rem(lax.axis_index("gx"), 2)
    levels, count_x = u_ref.shape[:2]

    def rows_of(level):
        u, v = (
            jnp.concatenate([r[level, :EDGE, middle(r)], r[level, count_x - EDGE :, middle(r)]], 0)
            for r in (u_ref, v_ref)
        )
        at = pl.ds(pl.multiple_of(level * 48, 16), 48)
        x_high[at], x_low[at] = split(message_sums(three[odd], two[odd], u, v))

    each(levels, MAIN_UNROLL, rows_of)
    sums = column_sums(ends_high[...], ends_low[...], w_ends) + column_sums(x_high[...], x_low[...], w_rest)
    for place, ref in ((0, e_ref), (8, o_ref)):
        for level in range(levels):
            ref[level] = message_of(sums, level, place)
    e_ref[levels] = slab_ref[...]


def own_rows_of(left, u, v):
    return split(jnp.concatenate([row_sums(left, f) for f in products(u, v)], 0))


def ends_kernel(u_ref, v_ref, left, weights, s_ref, x_high, x_low):
    levels, _, count_y = u_ref.shape
    rows, lanes = s_ref.shape

    for level in range(levels):
        u, v = (
            jnp.concatenate([r[level, :, :SIDE], r[level, :, count_y - SIDE :]], 1) for r in (u_ref, v_ref)
        )
        at = slice(level * rows, (level + 1) * rows)
        x_high[at], x_low[at] = own_rows_of(left[...], u, v)
    strips = jnp.zeros((rows, lanes), F32)
    for level in range(levels):
        at = slice(level * rows, (level + 1) * rows)
        strips = strips + pltpu.roll(column_sums(x_high[at], x_low[at], weights), WIDE * level, 1)
    s_ref[...] = strips


def own_kernel(u_ref, v_ref, left, ends_high, ends_low, w_ends, w_rest, p_ref, x_high, x_low):
    levels = u_ref.shape[0]
    rows = p_ref.shape[0] // levels

    def rows_of(level):
        at = pl.ds(pl.multiple_of(level * rows, 16), rows)
        x_high[at], x_low[at] = own_rows_of(left[...], u_ref[level, :, middle(u_ref)], v_ref[level, :, middle(v_ref)])

    each(levels, OWN_UNROLL, rows_of)
    for level in range(0, levels, 2):
        at = slice(level * rows, (level + 2) * rows)
        p_ref[at] = column_sums(ends_high[at], ends_low[at], w_ends) + column_sums(x_high[at], x_low[at], w_rest)


def low_and_high(odd, e, o):
    return jnp.where(odd == 0, o, e), jnp.where(odd == 0, e, o)


def add_rows(wide_refs, short_refs, own_low, own_high, got_low, got_high):
    for k, ref in enumerate(wide_refs):
        count = ref.shape[0]
        at = 8 * k
        ref[0:RIM] = own_low[at + EXT - RIM : at + EXT]
        ref[count - RIM : count] = own_high[at + RIM : at + 2 * RIM]
        ref[0:WIDE] = ref[0:WIDE] + got_low[at : at + WIDE]
        ref[count - WIDE : count] = ref[count - WIDE : count] + got_high[at : at + WIDE]
    for k, ref in enumerate(short_refs):
        count = ref.shape[0]
        if k < 2:
            at = 16 + EXT * k
            ref[0:EXT] = ref[0:EXT] + got_low[at : at + EXT]
            ref[count - EXT : count] = ref[count - EXT : count] + got_high[at : at + EXT]
        else:
            for h in range(2):
                at = 8 * h + WIDE
                ref[2 * h : 2 * h + 2] = ref[2 * h : 2 * h + 2] + got_low[at : at + 2]
                back = count - EXT + 2 * h
                ref[back : back + 2] = ref[back : back + 2] + got_high[at : at + 2]


def strip_kernel(s_ref, own_e, own_o, got_e, got_o, e_ref, o_ref, us, vs, uus, uvs, vvs):
    odd_x = lax.rem(lax.axis_index("gx"), 2)
    odd_y = lax.rem(lax.axis_index("gy"), 2)
    coarse = uus.shape[0]
    us[RIM : RIM + coarse] = s_ref[0:coarse]
    vs[RIM : RIM + coarse] = s_ref[coarse : 2 * coarse]
    uus[...] = s_ref[2 * coarse : 3 * coarse]
    uvs[...] = s_ref[3 * coarse : 4 * coarse]
    vvs[...] = s_ref[4 * coarse : 5 * coarse]
    own_low, own_high = low_and_high(odd_x, own_e[...], own_o[...])
    got_low, got_high = low_and_high(odd_x, got_e[got_e.shape[0] - 1], got_o[...])
    add_rows((us, vs), (uus, uvs, vvs), own_low, own_high, got_low, got_high)
    rim_rows = us.shape[0]
    start = -(-rim_rows // 8) * 8
    pairs = (
        (0, us[...], vs[...]),
        (start, uus[...], uvs[...]),
        (start + coarse, vvs[0 : coarse // 2], vvs[coarse // 2 : coarse]),
    )
    for at, a, b in pairs:
        lane = lax.broadcasted_iota(jnp.int32, a.shape, 1)
        low = jnp.where(lane < HALF, a, pltpu.roll(b, HALF, 1))
        high = jnp.where(lane < HALF, pltpu.roll(a, HALF, 1), b)
        e_ref[at : at + a.shape[0]] = jnp.where(odd_y == 0, high, low)
        o_ref[at : at + a.shape[0]] = jnp.where(odd_y == 0, low, high)


def first_form(plus_two, plus_one, minus_one, minus_two):
    return (8.0 * plus_one - plus_two - 8.0 * minus_one + minus_two) * (1.0 / 12.0)


def second_form(plus_two, plus_one, centre, minus_one, minus_two):
    return (16.0 * plus_one - plus_two - 30.0 * centre + 16.0 * minus_one - minus_two) * (1.0 / 12.0)


def final_kernel(
    p_ref, xe_own, xo_own, xe_got, xo_got, ye_own, yo_own, ye_got, yo_got, st_hbm, lib_hbm,
    us, vs, uus, uvs, vvs, low_side, high_side, slopes, st_ref, lib_ref, sem,
):
    odd_x = lax.rem(lax.axis_index("gx"), 2)
    odd_y = lax.rem(lax.axis_index("gy"), 2)
    levels, coarse, lanes = st_ref.shape[1:]
    rim_rows = us.shape[0]
    own_low, own_high = low_and_high(odd_y, ye_own[...], yo_own[...])
    got_low, got_high = low_and_high(odd_y, ye_got[...], yo_got[...])
    place = lax.rem(lax.rem(lax.broadcasted_iota(jnp.int32, own_low.shape, 1), HALF), WIDE)
    back = pltpu.roll(own_low, lanes - RIM, 1)
    ahead = pltpu.roll(own_high, RIM, 1)
    low_side[...] = got_low + jnp.where(place < RIM, back, 0.0)
    high_side[...] = got_high + jnp.where(place >= EXT, ahead, 0.0)

    def out(level):
        return (
            pltpu.make_async_copy(st_ref.at[:, level], st_hbm.at[:, level], sem.at[0, level]),
            pltpu.make_async_copy(lib_ref.at[:, level], lib_hbm.at[:, level], sem.at[1, level]),
        )

    def finish(level):
        def part_of(k):
            return p_ref[pl.ds(pl.multiple_of((5 * level + k) * coarse, 8), coarse)]

        us[RIM : RIM + coarse] = part_of(0)
        vs[RIM : RIM + coarse] = part_of(1)
        for k, ref in enumerate((uus, uvs, vvs)):
            ref[...] = part_of(2 + k)
        own_low, own_high = low_and_high(odd_x, xe_own[level], xo_own[level])
        got_low, got_high = low_and_high(odd_x, xe_got[level], xo_got[level])
        add_rows((us, vs), (uus, uvs, vvs), own_low, own_high, got_low, got_high)

        shift = WIDE * level

        def sides(at, count, second):
            base = HALF if second else 0
            low = pltpu.roll(low_side[at : at + count], lanes - RIM - base - shift, 1)
            high = pltpu.roll(high_side[at : at + count], lanes - EXT - base - shift, 1)
            return low, high

        def joined(field, low, high):
            lane = lax.broadcasted_iota(jnp.int32, field.shape, 1)
            return field + jnp.where(lane < EXT, low, 0.0) + jnp.where(lane >= lanes - EXT, high, 0.0)

        means = []
        found = []
        for k, ref in enumerate((us, vs)):
            low, high = sides(0, rim_rows, k == 1)
            f = joined(ref[...], low, high)
            ref[...] = f
            lane = lax.broadcasted_iota(jnp.int32, f.shape, 1)
            plus_one = pltpu.roll(jnp.where(lane < 1, high, f), lanes - 1, 1)
            plus_two = pltpu.roll(jnp.where(lane < 2, high, f), lanes - 2, 1)
            minus_one = pltpu.roll(jnp.where(lane >= lanes - 1, low, f), 1, 1)
            minus_two = pltpu.roll(jnp.where(lane >= lanes - 2, low, f), 2, 1)
            slopes[...] = first_form(plus_two, plus_one, minus_one, minus_two)

            def row(source, by):
                return source[RIM + by : RIM + by + coarse]

            curve_y = second_form(plus_two, plus_one, f, minus_one, minus_two)[RIM : RIM + coarse]
            centre = row(ref, 0)
            shifted = [row(ref, by) for by in (2, 1, -1, -2)]
            grad_x = first_form(*shifted)
            curve_x = second_form(shifted[0], shifted[1], centre, shifted[2], shifted[3])
            grad_y = row(slopes, 0)
            cross = first_form(*[row(slopes, by) for by in (2, 1, -1, -2)])
            means.append(centre)
            found.append((grad_x, grad_y, curve_x, cross, curve_y))

        u, v = means
        start = -(-rim_rows // 8) * 8
        low, high = sides(start, coarse, False)
        st_ref[0, level] = joined(uus[...], low, high) - u * u
        low, high = sides(start, coarse, True)
        st_ref[1, level] = joined(uvs[...], low, high) - u * v
        for h in range(2):
            part = slice(coarse // 2 * h, coarse // 2 * (h + 1))
            low, high = sides(start + coarse, coarse // 2, h == 1)
            st_ref[2, level, part] = joined(vvs[part], low, high) - v[part] * v[part]

        (ux, uy, uxx, uxy, uyy), (vx, vy, vxx, vxy, vyy) = found
        vorticity = vx - uy
        features = (ux, uy, vx, vy, uxx, uxy, uyy, vxx, vxy, vyy, vxx - uxy, vxy - uyy)
        for k, feature in enumerate(features):
            lib_ref[4 * k, level] = feature
            lib_ref[4 * k + 1, level] = u * feature
            lib_ref[4 * k + 2, level] = v * feature
            lib_ref[4 * k + 3, level] = vorticity * feature
        for copy in out(level):
            copy.start()

    each(levels, FINAL_UNROLL, finish)
    for level in range(levels):
        for copy in out(level):
            copy.wait()


def pairs_of(axis):
    count = lax.axis_size(axis)
    assert count % 2 == 0
    even = [(i, i ^ 1) for i in range(count)]
    odd = [(i, (i + 1) % count if i % 2 else (i - 1) % count) for i in range(count)]
    return even, odd


def local_call(body, outs, scratch, *operands):
    in_vmem, in_hbm = pl.BlockSpec(memory_space=pltpu.VMEM), pl.BlockSpec(memory_space=pltpu.HBM)
    specs, arrays = [], []
    for operand, here in operands:
        specs.append(in_vmem if here else in_hbm)
        arrays.append(pltpu.with_memory_space_constraint(operand, pltpu.VMEM) if here else pltpu.with_memory_space_constraint(operand, pltpu.HBM))
    return pl.pallas_call(
        body,
        in_specs=specs,
        out_specs=[in_hbm if isinstance(o, jax.ShapeDtypeStruct) else in_vmem for o in outs],
        out_shape=outs,
        scratch_shapes=scratch,
        compiler_params=pltpu.CompilerParams(vmem_limit_bytes=VMEM_BYTES),
    )(*arrays)


def in_order(east_flow, north_flow):
    levels, count_x, count_y = east_flow.shape
    coarse, lanes = count_x // STEP, count_y // STEP
    assert lanes == 2 * HALF and WIDE * levels <= HALF and coarse % 16 == 0
    assert count_x >= 2 * EDGE and count_y > 2 * SIDE
    three, two = (jnp.asarray(c) for c in message_rows(count_x))
    w_strips, w_ends, w_rest = (jnp.asarray(c) for c in column_weights(count_y))
    left = jnp.asarray(left_operand(taps(range(coarse), count_x)))
    rim_rows = coarse + 2 * RIM
    start = -(-rim_rows // 8) * 8
    side = (start + coarse + coarse // 2, lanes)
    own_count = 5 * coarse
    f32, bf16 = functools.partial(pltpu.VMEM, dtype=F32), functools.partial(pltpu.VMEM, dtype=BF16)

    def held(*arrays):
        return [(a, True) for a in arrays]

    (even_x, odd_x), (even_y, odd_y) = pairs_of("gx"), pairs_of("gy")
    parts = 1
    consts = (three, two, w_strips, w_ends, w_rest, left)
    se, so, ends_high, ends_low, *kept = local_call(
        slab_kernel,
        [f32((MSG, lanes))] * 2 + [bf16((48 * levels, 2 * SIDE))] * 2 + [bf16(c.shape) for c in consts],
        [f32((levels, 2 * EDGE, 2 * SIDE))] * 2
        + [pltpu.SemaphoreType.DMA((parts, 8)), pltpu.SemaphoreType.DMA((len(consts),))],
        *[(a, False) for a in (east_flow, north_flow) + consts],
    )
    message_ends = (ends_high, ends_low)
    three, two, w_strips, w_ends, w_rest, left = kept
    so_got = lax.ppermute(so, "gx", odd_x)
    fine = held(east_flow, north_flow)
    xe, xo = local_call(
        main_kernel,
        [f32((levels + 1, MSG, lanes)), f32((levels, MSG, lanes))],
        [bf16((48 * levels, count_y - 2 * SIDE))] * 2,
        *fine,
        *held(three, two, *message_ends, w_ends, w_rest, se),
    )
    xe_got, xo_got = lax.ppermute(xe, "gx", even_x), lax.ppermute(xo, "gx", odd_x)
    strips, *own_ends = local_call(
        ends_kernel,
        [f32((own_count, lanes))] + [bf16((own_count * levels, 2 * SIDE))] * 2,
        [],
        *fine,
        *held(left, w_strips),
    )
    rows = [f32((rim_rows, lanes))] * 2 + [f32((coarse, lanes))] * 3
    ye, yo = local_call(strip_kernel, [f32(side)] * 2, rows, *held(strips, se, so, xe_got, so_got))
    ye_got, yo_got = lax.ppermute(ye, "gy", even_y), lax.ppermute(yo, "gy", odd_y)
    (partial_sums,) = local_call(
        own_kernel,
        [f32((own_count * levels, lanes))],
        [bf16((own_count * levels, count_y - 2 * SIDE))] * 2,
        *fine,
        *held(left, *own_ends, w_ends, w_rest),
    )
    outs = [jax.ShapeDtypeStruct((n, levels, coarse, lanes), F32) for n in (3, 48)]
    return local_call(
        final_kernel,
        outs,
        rows
        + [f32(side)] * 2
        + [f32((rim_rows, lanes))]
        + [f32(o.shape) for o in outs]
        + [pltpu.SemaphoreType.DMA((2, levels))],
        *held(partial_sums, xe, xo, xe_got, xo_got, ye, yo, ye_got, yo_got),
    )


def solution(mesh):
    return jax.shard_map(
        in_order,
        mesh=mesh,
        in_specs=(P(None, "gx", "gy"), P(None, "gx", "gy")),
        out_specs=(P(None, None, "gx", "gy"), P(None, None, "gx", "gy")),
        check_vma=False,
    )
```

```python
import functools

import jax
import jax.numpy as jnp
import numpy as np
from jax import lax
from jax.experimental import pallas as pl
from jax.experimental.pallas import tpu as pltpu
from jax.sharding import PartitionSpec as P

spread_cells = 5.5
REACH = 16
STEP = 4
EXT = REACH // STEP
RIM = 2
WIDE = EXT + RIM
EDGE = 24
SHORT = 16
SIDE = 128
HALF = 64
MSG = 24
F32, BF16 = jnp.float32, jnp.bfloat16
VMEM_BYTES = 24 << 20
MAIN_UNROLL, OWN_UNROLL, FINAL_UNROLL = 8, 8, 1


def taps(cells, count_in):
    offsets = np.arange(2 * REACH + 1) - REACH
    bumps = np.exp(-0.5 * (offsets / spread_cells) ** 2)
    lag = np.arange(count_in)[None, :] - STEP * np.asarray(cells)[:, None]
    inside = np.abs(lag) <= REACH
    return np.where(inside, np.exp(-0.5 * (lag / spread_cells) ** 2), 0.0) / bumps.sum()


def pieces(values):
    high = values.astype(BF16)
    low = (values - high.astype(np.float64)).astype(BF16)
    return high, low


def left_operand(*sources):
    tops, bottoms = [], []
    for rows in sources:
        high, low = pieces(rows)
        tops += [high, high]
        bottoms += [low, np.zeros_like(low)]
    return np.concatenate([np.concatenate(tops, 1), np.concatenate(bottoms, 1)], 0)


def message_rows(count_x):
    coarse = count_x // STEP

    def rows(cells, ends):
        full = taps(cells, count_x)
        return np.concatenate([full[:, :ends], full[:, count_x - ends :]], 1)

    wide = {"low": rows(range(-EXT, RIM), EDGE), "high": rows(range(coarse - RIM, coarse + EXT), EDGE)}
    short = {"low": rows(range(-EXT, 0), SHORT), "high": rows(range(coarse, coarse + EXT), SHORT)}

    def placed(at, parts):
        blocks = []
        for part in parts:
            block = np.zeros((8, part.shape[1]))
            block[at : at + part.shape[0]] = part
            blocks.append(block)
        return np.concatenate(blocks, 0)

    three, two = [], []
    for sides in (("high", "low"), ("low", "high")):
        w = placed(0, [wide[s] for s in sides])
        none = np.zeros_like(w)
        vv = [placed(WIDE, [short[s][2 * h : 2 * h + 2] for s in sides]) for h in range(2)]
        three.append(left_operand(np.concatenate([w, none]), np.concatenate([none, w]), np.concatenate(vv)))
        two.append(left_operand(*[placed(EXT * h, [short[s] for s in sides]) for h in range(2)]))
    return np.stack(three), np.stack(two)


def column_weights(count_y):
    coarse = count_y // STEP
    own = taps(range(coarse), count_y).T
    strips = np.zeros((count_y, 2 * HALF))
    strips[:, :WIDE] = taps(range(-EXT, RIM), count_y).T
    high = list(range(coarse, coarse + EXT)) + list(range(coarse - RIM, coarse))
    strips[:, HALF : HALF + WIDE] = taps(high, count_y).T

    def ends(w):
        return np.concatenate([w[:SIDE], w[count_y - SIDE :]], 0)

    return tuple(np.concatenate(pieces(w), 1) for w in (ends(strips), ends(own), own[SIDE : count_y - SIDE]))


def split(values):
    high = values.astype(BF16)
    return high, (values - high.astype(F32)).astype(BF16)


def row_sums(left, field):
    high, low = split(field)
    both = jnp.dot(left, jnp.concatenate([high, low], 0), preferred_element_type=F32)
    half = both.shape[0] // 2
    return both[:half] + both[half:]


def column_sums(high, low, weights):
    count = weights.shape[1] // 2
    both = jnp.dot(high, weights[...], preferred_element_type=F32)
    return both[:, :count] + both[:, count:] + jnp.dot(low, weights[:, :count], preferred_element_type=F32)


def products(u, v):
    return u, v, u * u, u * v, v * v


def each(count, unroll, body):
    lax.fori_loop(0, count, lambda i, _: (body(i), None)[1], None, unroll=unroll)


def message_sums(three, two, u, v):
    us, vs = (jnp.concatenate([f[:SHORT], f[2 * EDGE - SHORT :]], 0) for f in (u, v))
    first = jnp.concatenate([*split(u), *split(v), *split(vs * vs)], 0)
    second = jnp.concatenate([*split(us * us), *split(us * vs)], 0)
    first = jnp.dot(three, first, preferred_element_type=F32)
    second = jnp.dot(two, second, preferred_element_type=F32)
    return jnp.concatenate([first[:32] + first[32:], second[:16] + second[16:]], 0)


def slab_kernel(
    u_hbm, v_hbm, three_hbm, two_hbm, w_hbm, w_ends_hbm, w_rest_hbm, left_hbm,
    e_ref, o_ref, x_high, x_low, three, two, weights, w_ends, w_rest, left,
    u_ref, v_ref, sem, const_sem,
):
    odd = lax.rem(lax.axis_index("gx"), 2)
    levels = u_ref.shape[0]
    _, count_x, count_y = u_hbm.shape
    parts = sem.shape[0]
    batch = levels // parts

    def loads(part):
        some = pl.ds(part * batch, batch)
        copies = []
        for f, (source, held) in enumerate(((u_hbm, u_ref), (v_hbm, v_ref))):
            for r in range(2):
                for c in range(2):
                    copies.append(
                        pltpu.make_async_copy(
                            source.at[
                                some, pl.ds(r * (count_x - EDGE), EDGE), pl.ds(c * (count_y - SIDE), SIDE)
                            ],
                            held.at[some, pl.ds(r * EDGE, EDGE), pl.ds(c * SIDE, SIDE)],
                            sem.at[part, 4 * f + 2 * r + c],
                        )
                    )
        return copies

    consts = [
        pltpu.make_async_copy(source, held, const_sem.at[k])
        for k, (source, held) in enumerate(
            (
                (three_hbm, three),
                (two_hbm, two),
                (w_hbm, weights),
                (left_hbm, left),
                (w_ends_hbm, w_ends),
                (w_rest_hbm, w_rest),
            )
        )
    ]
    for copy in loads(0) + consts[:3]:
        copy.start()
    for part in range(1, parts):
        for copy in loads(part):
            copy.start()
    for copy in consts[3:]:
        copy.start()
    for copy in consts[:3]:
        copy.wait()
    for part in range(parts):
        for copy in loads(part):
            copy.wait()

        for level in range(part * batch, (part + 1) * batch):
            at = slice(level * 48, (level + 1) * 48)
            x_high[at], x_low[at] = split(message_sums(three[odd], two[odd], u_ref[level], v_ref[level]))
    sums = column_sums(x_high[...], x_low[...], weights)
    row = lax.broadcasted_iota(jnp.int32, e_ref.shape, 0)
    wide = (row < 16) & (lax.rem(row, 8) < WIDE)
    for place, ref in ((0, e_ref), (8, o_ref)):
        parts = [message_of(sums, level, place) for level in range(levels)]
        ref[...] = jnp.where(wide, packed(parts, WIDE), packed([short_only(p) for p in parts], EXT))
    for copy in consts[3:]:
        copy.wait()


def short_only(strips):
    lane = lax.broadcasted_iota(jnp.int32, strips.shape, 1)
    return jnp.where(lax.rem(lane, HALF) < EXT, strips, 0.0)


def packed(parts, cells):
    return added([pltpu.roll(part, cells * level, 1) for level, part in enumerate(parts)])


def added(terms):
    while len(terms) > 1:
        terms = [a + b for a, b in zip(terms[::2], terms[1::2])] + terms[len(terms) & ~1 :]
    return terms[0]


def message_of(sums, level, place):
    return jnp.concatenate([sums[48 * level + 16 * t + place : 48 * level + 16 * t + place + 8] for t in range(3)], 0)


def middle(ref):
    count_y = ref.shape[-1]
    return pl.ds(SIDE, count_y - 2 * SIDE)


def main_kernel(
    u_ref, v_ref, three, two, ends_high, ends_low, w_ends, w_rest, slab_ref, e_ref, o_ref, x_high, x_low
):
    odd = lax.rem(lax.axis_index("gx"), 2)
    levels, count_x = u_ref.shape[:2]

    def rows_of(level):
        u, v = (
            jnp.concatenate([r[level, :EDGE, middle(r)], r[level, count_x - EDGE :, middle(r)]], 0)
            for r in (u_ref, v_ref)
        )
        at = pl.ds(pl.multiple_of(level * 48, 16), 48)
        x_high[at], x_low[at] = split(message_sums(three[odd], two[odd], u, v))

    each(levels, MAIN_UNROLL, rows_of)
    sums = column_sums(ends_high[...], ends_low[...], w_ends) + column_sums(x_high[...], x_low[...], w_rest)
    for place, ref in ((0, e_ref), (8, o_ref)):
        for level in range(levels):
            ref[level] = message_of(sums, level, place)
    e_ref[levels] = slab_ref[...]


def own_rows_of(left, u, v):
    return split(jnp.concatenate([row_sums(left, f) for f in products(u, v)], 0))


def ends_kernel(u_ref, v_ref, left, weights, s_ref, x_high, x_low):
    levels, _, count_y = u_ref.shape
    rows, lanes = s_ref.shape

    for level in range(levels):
        u, v = (
            jnp.concatenate([r[level, :, :SIDE], r[level, :, count_y - SIDE :]], 1) for r in (u_ref, v_ref)
        )
        at = slice(level * rows, (level + 1) * rows)
        x_high[at], x_low[at] = own_rows_of(left[...], u, v)
    wide = rows // 5 * 2
    strips, short = jnp.zeros((wide, lanes), F32), jnp.zeros((rows - wide, lanes), F32)
    for level in range(levels):
        at = slice(level * rows, (level + 1) * rows)
        sums = column_sums(x_high[at], x_low[at], weights)
        strips = strips + pltpu.roll(sums[:wide], WIDE * level, 1)
        short = short + pltpu.roll(short_only(sums[wide:]), EXT * level, 1)
    s_ref[:wide] = strips
    s_ref[wide:] = short


def own_kernel(u_ref, v_ref, left, ends_high, ends_low, w_ends, w_rest, p_ref, x_high, x_low):
    levels = u_ref.shape[0]
    rows = p_ref.shape[0] // levels

    def rows_of(level):
        at = pl.ds(pl.multiple_of(level * rows, 16), rows)
        x_high[at], x_low[at] = own_rows_of(left[...], u_ref[level, :, middle(u_ref)], v_ref[level, :, middle(v_ref)])

    each(levels, OWN_UNROLL, rows_of)
    for level in range(0, levels, 2):
        at = slice(level * rows, (level + 2) * rows)
        p_ref[at] = column_sums(ends_high[at], ends_low[at], w_ends) + column_sums(x_high[at], x_low[at], w_rest)


def low_and_high(odd, e, o):
    return jnp.where(odd == 0, o, e), jnp.where(odd == 0, e, o)


def add_rows(wide_refs, short_refs, own_low, own_high, got_low, got_high):
    for k, ref in enumerate(wide_refs):
        count = ref.shape[0]
        at = 8 * k
        ref[0:RIM] = own_low[at + EXT - RIM : at + EXT]
        ref[count - RIM : count] = own_high[at + RIM : at + 2 * RIM]
        ref[0:WIDE] = ref[0:WIDE] + got_low[at : at + WIDE]
        ref[count - WIDE : count] = ref[count - WIDE : count] + got_high[at : at + WIDE]
    for k, ref in enumerate(short_refs):
        count = ref.shape[0]
        if k < 2:
            at = 16 + EXT * k
            ref[0:EXT] = ref[0:EXT] + got_low[at : at + EXT]
            ref[count - EXT : count] = ref[count - EXT : count] + got_high[at : at + EXT]
        else:
            for h in range(2):
                at = 8 * h + WIDE
                ref[2 * h : 2 * h + 2] = ref[2 * h : 2 * h + 2] + got_low[at : at + 2]
                back = count - EXT + 2 * h
                ref[back : back + 2] = ref[back : back + 2] + got_high[at : at + 2]


def strip_kernel(levels, s_ref, own_e, own_o, got_e, got_o, e_ref, o_ref, us, vs, uus, uvs, vvs):
    odd_x = lax.rem(lax.axis_index("gx"), 2)
    odd_y = lax.rem(lax.axis_index("gy"), 2)
    coarse = uus.shape[0]
    us[RIM : RIM + coarse] = s_ref[0:coarse]
    vs[RIM : RIM + coarse] = s_ref[coarse : 2 * coarse]
    uus[...] = s_ref[2 * coarse : 3 * coarse]
    uvs[...] = s_ref[3 * coarse : 4 * coarse]
    vvs[...] = s_ref[4 * coarse : 5 * coarse]
    own_low, own_high = low_and_high(odd_x, own_e[...], own_o[...])
    got_low, got_high = low_and_high(odd_x, got_e[got_e.shape[0] - 1], got_o[...])
    add_rows((us, vs), (uus, uvs, vvs), own_low, own_high, got_low, got_high)
    start = e_ref.shape[0] - coarse // 2
    lanes = e_ref.shape[1]
    wide, short = WIDE * levels, EXT * levels

    def laid(fields, ends, from_lane):
        lane = lax.broadcasted_iota(jnp.int32, fields[0].shape, 1)
        total, begin = None, 0
        for field, end in zip(fields, ends):
            there = pltpu.roll(field, (lanes + begin - from_lane) % lanes, 1) if begin != from_lane else field
            total = there if total is None else jnp.where(lane < begin, total, there)
            begin = end
        return total

    h = coarse // 2
    sides = []
    for from_lane in (0, HALF):
        both = laid((us[...], vs[...]), (wide, 2 * wide), from_lane)
        lane = lax.broadcasted_iota(jnp.int32, (coarse, lanes), 1)
        uu = pltpu.roll(uus[...], (lanes + 2 * wide - from_lane) % lanes, 1)
        first = jnp.where(lane < 2 * wide, both[:coarse], uu)
        quarters = (uvs[:h], uvs[h:], vvs[:h], vvs[h:])
        second = laid(quarters, [short * n for n in range(1, 5)], from_lane)
        sides.append((first, both[coarse:], second))
    for low, high, at in zip(*sides, (0, coarse, start)):
        here = slice(at, at + low.shape[0])
        e_ref[here] = jnp.where(odd_y == 0, high, low)
        o_ref[here] = jnp.where(odd_y == 0, low, high)


def first_form(plus_two, plus_one, minus_one, minus_two):
    return (8.0 * plus_one - plus_two - 8.0 * minus_one + minus_two) * (1.0 / 12.0)


def second_form(plus_two, plus_one, centre, minus_one, minus_two):
    return (16.0 * plus_one - plus_two - 30.0 * centre + 16.0 * minus_one - minus_two) * (1.0 / 12.0)


def final_kernel(
    p_ref, xe_own, xo_own, xe_got, xo_got, ye_own, yo_own, ye_got, yo_got, st_hbm, lib_hbm,
    us, vs, uus, uvs, vvs, low_side, high_side, slopes, st_ref, lib_ref, sem,
):
    odd_x = lax.rem(lax.axis_index("gx"), 2)
    odd_y = lax.rem(lax.axis_index("gy"), 2)
    levels, coarse, lanes = st_ref.shape[1:]
    rim_rows = us.shape[0]
    own_low, own_high = low_and_high(odd_y, ye_own[...], yo_own[...])
    got_low, got_high = low_and_high(odd_y, ye_got[...], yo_got[...])
    lane = lax.broadcasted_iota(jnp.int32, own_low.shape, 1)
    row = lax.broadcasted_iota(jnp.int32, own_low.shape, 0)
    wide, short = WIDE * levels, EXT * levels
    start = own_low.shape[0] - coarse // 2
    is_wide = (lane < 2 * wide) & (row < start)
    place = lax.rem(lane, WIDE)
    rim = pltpu.roll(got_low, lanes - EXT, 1) + pltpu.roll(own_low, lanes - RIM, 1)
    ordered = jnp.where(place < RIM, rim, pltpu.roll(got_low, RIM, 1))
    low_side[...] = jnp.where(is_wide, ordered, got_low)
    ahead = pltpu.roll(own_high, EXT, 1)
    high_side[...] = got_high + jnp.where(is_wide & (place >= EXT), ahead, 0.0)

    def out(level):
        return (
            pltpu.make_async_copy(st_ref.at[:, level], st_hbm.at[:, level], sem.at[0, level]),
            pltpu.make_async_copy(lib_ref.at[:, level], lib_hbm.at[:, level], sem.at[1, level]),
        )

    def finish(level):
        def part_of(k):
            return p_ref[pl.ds(pl.multiple_of((5 * level + k) * coarse, 8), coarse)]

        us[RIM : RIM + coarse] = part_of(0)
        vs[RIM : RIM + coarse] = part_of(1)
        for k, ref in enumerate((uus, uvs, vvs)):
            ref[...] = part_of(2 + k)
        own_low, own_high = low_and_high(odd_x, xe_own[level], xo_own[level])
        got_low, got_high = low_and_high(odd_x, xe_got[level], xo_got[level])
        add_rows((us, vs), (uus, uvs, vvs), own_low, own_high, got_low, got_high)

        def sides(at, count, base, cells):
            rim = RIM if cells == WIDE else 0
            first = base + cells * level
            low = pltpu.roll(low_side[at : at + count], lax.rem(2 * lanes - rim - first, lanes), 1)
            high = pltpu.roll(high_side[at : at + count], lanes - EXT - first, 1)
            return low, high

        def joined(field, low, high):
            lane = lax.broadcasted_iota(jnp.int32, field.shape, 1)
            return field + jnp.where(lane < EXT, low, 0.0) + jnp.where(lane >= lanes - EXT, high, 0.0)

        means = []
        found = []
        for k, ref in enumerate((us, vs)):
            low, high = sides(0, rim_rows, k * wide, WIDE)
            f = joined(ref[...], low, high)
            ref[...] = f
            lane = lax.broadcasted_iota(jnp.int32, f.shape, 1)
            plus_one = pltpu.roll(jnp.where(lane < 1, high, f), lanes - 1, 1)
            plus_two = pltpu.roll(jnp.where(lane < 2, high, f), lanes - 2, 1)
            minus_one = pltpu.roll(jnp.where(lane >= lanes - 1, low, f), 1, 1)
            minus_two = pltpu.roll(jnp.where(lane >= lanes - 2, low, f), 2, 1)
            slopes[...] = first_form(plus_two, plus_one, minus_one, minus_two)

            def row(source, by):
                return source[RIM + by : RIM + by + coarse]

            curve_y = second_form(plus_two, plus_one, f, minus_one, minus_two)[RIM : RIM + coarse]
            centre = row(ref, 0)
            shifted = [row(ref, by) for by in (2, 1, -1, -2)]
            grad_x = first_form(*shifted)
            curve_x = second_form(shifted[0], shifted[1], centre, shifted[2], shifted[3])
            grad_y = row(slopes, 0)
            cross = first_form(*[row(slopes, by) for by in (2, 1, -1, -2)])
            means.append(centre)
            found.append((grad_x, grad_y, curve_x, cross, curve_y))

        u, v = means
        low, high = sides(0, coarse, 2 * wide, EXT)
        st_ref[0, level] = joined(uus[...], low, high) - u * u
        for k, (ref, other) in enumerate(((uvs, u), (vvs, v))):
            for h in range(2):
                part = slice(coarse // 2 * h, coarse // 2 * (h + 1))
                low, high = sides(start, coarse // 2, (2 * k + h) * short, EXT)
                st_ref[1 + k, level, part] = joined(ref[part], low, high) - other[part] * v[part]

        (ux, uy, uxx, uxy, uyy), (vx, vy, vxx, vxy, vyy) = found
        vorticity = vx - uy
        features = (ux, uy, vx, vy, uxx, uxy, uyy, vxx, vxy, vyy, vxx - uxy, vxy - uyy)
        for k, feature in enumerate(features):
            lib_ref[4 * k, level] = feature
            lib_ref[4 * k + 1, level] = u * feature
            lib_ref[4 * k + 2, level] = v * feature
            lib_ref[4 * k + 3, level] = vorticity * feature
        for copy in out(level):
            copy.start()

    each(levels, FINAL_UNROLL, finish)
    for level in range(levels):
        for copy in out(level):
            copy.wait()


def pairs_of(axis):
    count = lax.axis_size(axis)
    assert count % 2 == 0
    even = [(i, i ^ 1) for i in range(count)]
    odd = [(i, (i + 1) % count if i % 2 else (i - 1) % count) for i in range(count)]
    return even, odd


def local_call(body, outs, scratch, *operands):
    in_vmem, in_hbm = pl.BlockSpec(memory_space=pltpu.VMEM), pl.BlockSpec(memory_space=pltpu.HBM)
    specs, arrays = [], []
    for operand, here in operands:
        specs.append(in_vmem if here else in_hbm)
        arrays.append(pltpu.with_memory_space_constraint(operand, pltpu.VMEM) if here else pltpu.with_memory_space_constraint(operand, pltpu.HBM))
    return pl.pallas_call(
        body,
        in_specs=specs,
        out_specs=[in_hbm if isinstance(o, jax.ShapeDtypeStruct) else in_vmem for o in outs],
        out_shape=outs,
        scratch_shapes=scratch,
        compiler_params=pltpu.CompilerParams(vmem_limit_bytes=VMEM_BYTES),
    )(*arrays)


def in_order(east_flow, north_flow):
    levels, count_x, count_y = east_flow.shape
    coarse, lanes = count_x // STEP, count_y // STEP
    assert lanes == 2 * HALF and (2 * WIDE + EXT) * levels <= lanes and coarse % 16 == 0
    assert count_x >= 2 * EDGE and count_y > 2 * SIDE
    three, two = (jnp.asarray(c) for c in message_rows(count_x))
    w_strips, w_ends, w_rest = (jnp.asarray(c) for c in column_weights(count_y))
    left = jnp.asarray(left_operand(taps(range(coarse), count_x)))
    rim_rows = coarse + 2 * RIM
    start = -(-rim_rows // 8) * 8
    side = (start + coarse // 2, lanes)
    own_count = 5 * coarse
    f32, bf16 = functools.partial(pltpu.VMEM, dtype=F32), functools.partial(pltpu.VMEM, dtype=BF16)

    def held(*arrays):
        return [(a, True) for a in arrays]

    (even_x, odd_x), (even_y, odd_y) = pairs_of("gx"), pairs_of("gy")
    parts = 1
    consts = (three, two, w_strips, w_ends, w_rest, left)
    se, so, ends_high, ends_low, *kept = local_call(
        slab_kernel,
        [f32((MSG, lanes))] * 2 + [bf16((48 * levels, 2 * SIDE))] * 2 + [bf16(c.shape) for c in consts],
        [f32((levels, 2 * EDGE, 2 * SIDE))] * 2
        + [pltpu.SemaphoreType.DMA((parts, 8)), pltpu.SemaphoreType.DMA((len(consts),))],
        *[(a, False) for a in (east_flow, north_flow) + consts],
    )
    message_ends = (ends_high, ends_low)
    three, two, w_strips, w_ends, w_rest, left = kept
    so_got = lax.ppermute(so, "gx", odd_x)
    fine = held(east_flow, north_flow)
    xe, xo = local_call(
        main_kernel,
        [f32((levels + 1, MSG, lanes)), f32((levels, MSG, lanes))],
        [bf16((48 * levels, count_y - 2 * SIDE))] * 2,
        *fine,
        *held(three, two, *message_ends, w_ends, w_rest, se),
    )
    xe_got, xo_got = lax.ppermute(xe, "gx", even_x), lax.ppermute(xo, "gx", odd_x)
    strips, *own_ends = local_call(
        ends_kernel,
        [f32((own_count, lanes))] + [bf16((own_count * levels, 2 * SIDE))] * 2,
        [],
        *fine,
        *held(left, w_strips),
    )
    rows = [f32((rim_rows, lanes))] * 2 + [f32((coarse, lanes))] * 3
    ye, yo = local_call(functools.partial(strip_kernel, levels), [f32(side)] * 2, rows, *held(strips, se, so, xe_got, so_got))
    ye_got, yo_got = lax.ppermute(ye, "gy", even_y), lax.ppermute(yo, "gy", odd_y)
    (partial_sums,) = local_call(
        own_kernel,
        [f32((own_count * levels, lanes))],
        [bf16((own_count * levels, count_y - 2 * SIDE))] * 2,
        *fine,
        *held(left, *own_ends, w_ends, w_rest),
    )
    outs = [jax.ShapeDtypeStruct((n, levels, coarse, lanes), F32) for n in (3, 48)]
    return local_call(
        final_kernel,
        outs,
        rows
        + [f32(side)] * 2
        + [f32((rim_rows, lanes))]
        + [f32(o.shape) for o in outs]
        + [pltpu.SemaphoreType.DMA((2, levels))],
        *held(partial_sums, xe, xo, xe_got, xo_got, ye, yo, ye_got, yo_got),
    )


def solution(mesh):
    return jax.shard_map(
        in_order,
        mesh=mesh,
        in_specs=(P(None, "gx", "gy"), P(None, "gx", "gy")),
        out_specs=(P(None, None, "gx", "gy"), P(None, None, "gx", "gy")),
        check_vma=False,
    )
```

```python
import functools

import jax
import jax.numpy as jnp
import numpy as np
from jax import lax
from jax.experimental import pallas as pl
from jax.experimental.pallas import tpu as pltpu
from jax.sharding import PartitionSpec as P

spread_cells = 5.5
REACH = 16
STEP = 4
EXT = REACH // STEP
RIM = 2
WIDE = EXT + RIM
EDGE = 24
SHORT = 16
SIDE = 128
HALF = 64
MSG = 24
F32, BF16 = jnp.float32, jnp.bfloat16
VMEM_BYTES = 24 << 20
MAIN_UNROLL, OWN_UNROLL, FINAL_UNROLL = 8, 8, 1


def taps(cells, count_in):
    offsets = np.arange(2 * REACH + 1) - REACH
    bumps = np.exp(-0.5 * (offsets / spread_cells) ** 2)
    lag = np.arange(count_in)[None, :] - STEP * np.asarray(cells)[:, None]
    inside = np.abs(lag) <= REACH
    return np.where(inside, np.exp(-0.5 * (lag / spread_cells) ** 2), 0.0) / bumps.sum()


def pieces(values):
    high = values.astype(BF16)
    low = (values - high.astype(np.float64)).astype(BF16)
    return high, low


def left_operand(*sources):
    tops, bottoms = [], []
    for rows in sources:
        high, low = pieces(rows)
        tops += [high, high]
        bottoms += [low, np.zeros_like(low)]
    return np.concatenate([np.concatenate(tops, 1), np.concatenate(bottoms, 1)], 0)


def message_rows(count_x):
    coarse = count_x // STEP

    def rows(cells, ends):
        full = taps(cells, count_x)
        return np.concatenate([full[:, :ends], full[:, count_x - ends :]], 1)

    wide = {"low": rows(range(-EXT, RIM), EDGE), "high": rows(range(coarse - RIM, coarse + EXT), EDGE)}
    short = {"low": rows(range(-EXT, 0), SHORT), "high": rows(range(coarse, coarse + EXT), SHORT)}

    def placed(at, parts):
        blocks = []
        for part in parts:
            block = np.zeros((8, part.shape[1]))
            block[at : at + part.shape[0]] = part
            blocks.append(block)
        return np.concatenate(blocks, 0)

    three, two = [], []
    for sides in (("high", "low"), ("low", "high")):
        w = placed(0, [wide[s] for s in sides])
        none = np.zeros_like(w)
        vv = [placed(WIDE, [short[s][2 * h : 2 * h + 2] for s in sides]) for h in range(2)]
        three.append(left_operand(np.concatenate([w, none]), np.concatenate([none, w]), np.concatenate(vv)))
        two.append(left_operand(*[placed(EXT * h, [short[s] for s in sides]) for h in range(2)]))
    return np.stack(three), np.stack(two)


def column_weights(count_y):
    coarse = count_y // STEP
    own = taps(range(coarse), count_y).T
    strips = np.zeros((count_y, 2 * HALF))
    strips[:, :WIDE] = taps(range(-EXT, RIM), count_y).T
    high = list(range(coarse, coarse + EXT)) + list(range(coarse - RIM, coarse))
    strips[:, HALF : HALF + WIDE] = taps(high, count_y).T

    def ends(w):
        return np.concatenate([w[:SIDE], w[count_y - SIDE :]], 0)

    return tuple(np.concatenate(pieces(w), 1) for w in (ends(strips), ends(own), own[SIDE : count_y - SIDE]))


def split(values):
    high = values.astype(BF16)
    return high, (values - high.astype(F32)).astype(BF16)


def row_sums(left, field):
    high, low = split(field)
    both = jnp.dot(left, jnp.concatenate([high, low], 0), preferred_element_type=F32)
    half = both.shape[0] // 2
    return both[:half] + both[half:]


def column_sums(high, low, weights):
    count = weights.shape[1] // 2
    both = jnp.dot(high, weights[...], preferred_element_type=F32)
    return both[:, :count] + both[:, count:] + jnp.dot(low, weights[:, :count], preferred_element_type=F32)


def products(u, v):
    return u, v, u * u, u * v, v * v


def each(count, unroll, body):
    lax.fori_loop(0, count, lambda i, _: (body(i), None)[1], None, unroll=unroll)


def message_sums(three, two, u, v):
    us, vs = (jnp.concatenate([f[:SHORT], f[2 * EDGE - SHORT :]], 0) for f in (u, v))
    first = jnp.concatenate([*split(u), *split(v), *split(vs * vs)], 0)
    second = jnp.concatenate([*split(us * us), *split(us * vs)], 0)
    first = jnp.dot(three, first, preferred_element_type=F32)
    second = jnp.dot(two, second, preferred_element_type=F32)
    return jnp.concatenate([first[:32] + first[32:], second[:16] + second[16:]], 0)


def slab_kernel(
    u_hbm, v_hbm, three_hbm, two_hbm, w_hbm, w_ends_hbm, w_rest_hbm, left_hbm,
    e_ref, o_ref, x_high, x_low, three, two, weights, w_ends, w_rest, left,
    u_ref, v_ref, sem, const_sem,
):
    odd = lax.rem(lax.axis_index("gx"), 2)
    levels = u_ref.shape[0]
    _, count_x, count_y = u_hbm.shape
    parts = sem.shape[0]
    batch = levels // parts

    def loads(part):
        some = pl.ds(part * batch, batch)
        copies = []
        for f, (source, held) in enumerate(((u_hbm, u_ref), (v_hbm, v_ref))):
            for r in range(2):
                for c in range(2):
                    copies.append(
                        pltpu.make_async_copy(
                            source.at[
                                some, pl.ds(r * (count_x - EDGE), EDGE), pl.ds(c * (count_y - SIDE), SIDE)
                            ],
                            held.at[some, pl.ds(r * EDGE, EDGE), pl.ds(c * SIDE, SIDE)],
                            sem.at[part, 4 * f + 2 * r + c],
                        )
                    )
        return copies

    consts = [
        pltpu.make_async_copy(source, held, const_sem.at[k])
        for k, (source, held) in enumerate(
            (
                (three_hbm, three),
                (two_hbm, two),
                (w_hbm, weights),
                (left_hbm, left),
                (w_ends_hbm, w_ends),
                (w_rest_hbm, w_rest),
            )
        )
    ]
    for copy in loads(0) + consts[:3]:
        copy.start()
    for part in range(1, parts):
        for copy in loads(part):
            copy.start()
    for copy in consts[3:]:
        copy.start()
    for copy in consts[:3]:
        copy.wait()
    for part in range(parts):
        for copy in loads(part):
            copy.wait()

        for level in range(part * batch, (part + 1) * batch):
            at = slice(level * 48, (level + 1) * 48)
            x_high[at], x_low[at] = split(message_sums(three[odd], two[odd], u_ref[level], v_ref[level]))
    sums = column_sums(x_high[...], x_low[...], weights)
    row = lax.broadcasted_iota(jnp.int32, e_ref.shape, 0)
    wide = (row < 16) & (lax.rem(row, 8) < WIDE)
    for place, ref in ((0, e_ref), (8, o_ref)):
        parts = [message_of(sums, level, place) for level in range(levels)]
        ref[...] = jnp.where(wide, packed(parts, WIDE), packed([short_only(p) for p in parts], EXT))
    for copy in consts[3:]:
        copy.wait()


def short_only(strips):
    lane = lax.broadcasted_iota(jnp.int32, strips.shape, 1)
    return jnp.where(lax.rem(lane, HALF) < EXT, strips, 0.0)


def packed(parts, cells):
    return added([pltpu.roll(part, cells * level, 1) for level, part in enumerate(parts)])


def added(terms):
    while len(terms) > 1:
        terms = [a + b for a, b in zip(terms[::2], terms[1::2])] + terms[len(terms) & ~1 :]
    return terms[0]


def message_of(sums, level, place):
    return jnp.concatenate([sums[48 * level + 16 * t + place : 48 * level + 16 * t + place + 8] for t in range(3)], 0)


def middle(ref):
    count_y = ref.shape[-1]
    return pl.ds(SIDE, count_y - 2 * SIDE)


def main_kernel(
    u_ref, v_ref, three, two, ends_high, ends_low, w_ends, w_rest, slab_ref, e_ref, o_ref, x_high, x_low
):
    odd = lax.rem(lax.axis_index("gx"), 2)
    levels, count_x = u_ref.shape[:2]

    def rows_of(level):
        u, v = (
            jnp.concatenate([r[level, :EDGE, middle(r)], r[level, count_x - EDGE :, middle(r)]], 0)
            for r in (u_ref, v_ref)
        )
        at = pl.ds(pl.multiple_of(level * 48, 16), 48)
        x_high[at], x_low[at] = split(message_sums(three[odd], two[odd], u, v))

    each(levels, MAIN_UNROLL, rows_of)
    sums = column_sums(ends_high[...], ends_low[...], w_ends) + column_sums(x_high[...], x_low[...], w_rest)
    for place, ref in ((0, e_ref), (8, o_ref)):
        for level in range(levels):
            ref[level] = message_of(sums, level, place)
    e_ref[levels] = slab_ref[...]


def own_rows_of(left, u, v):
    return split(jnp.concatenate([row_sums(left, f) for f in products(u, v)], 0))


def ends_kernel(u_ref, v_ref, left, weights, s_ref, x_high, x_low):
    levels, _, count_y = u_ref.shape
    rows, lanes = s_ref.shape

    for level in range(levels):
        u, v = (
            jnp.concatenate([r[level, :, :SIDE], r[level, :, count_y - SIDE :]], 1) for r in (u_ref, v_ref)
        )
        at = slice(level * rows, (level + 1) * rows)
        x_high[at], x_low[at] = own_rows_of(left[...], u, v)
    wide = rows // 5 * 2
    strips, short = jnp.zeros((wide, lanes), F32), jnp.zeros((rows - wide, lanes), F32)
    for level in range(levels):
        at = slice(level * rows, (level + 1) * rows)
        sums = column_sums(x_high[at], x_low[at], weights)
        strips = strips + pltpu.roll(sums[:wide], WIDE * level, 1)
        short = short + pltpu.roll(short_only(sums[wide:]), EXT * level, 1)
    s_ref[:wide] = strips
    s_ref[wide:] = short


def own_kernel(u_ref, v_ref, left, ends_high, ends_low, w_ends, w_rest, p_ref, x_high, x_low):
    levels = u_ref.shape[0]
    rows = p_ref.shape[0] // levels

    def rows_of(level):
        at = pl.ds(pl.multiple_of(level * rows, 16), rows)
        x_high[at], x_low[at] = own_rows_of(left[...], u_ref[level, :, middle(u_ref)], v_ref[level, :, middle(v_ref)])

    each(levels, OWN_UNROLL, rows_of)
    for level in range(0, levels, 2):
        at = slice(level * rows, (level + 2) * rows)
        p_ref[at] = column_sums(ends_high[at], ends_low[at], w_ends) + column_sums(x_high[at], x_low[at], w_rest)


def low_and_high(odd, e, o):
    return jnp.where(odd == 0, o, e), jnp.where(odd == 0, e, o)


def add_rows(wide_refs, short_refs, own_low, own_high, got_low, got_high):
    for k, ref in enumerate(wide_refs):
        count = ref.shape[0]
        at = 8 * k
        ref[0:RIM] = own_low[at + EXT - RIM : at + EXT]
        ref[count - RIM : count] = own_high[at + RIM : at + 2 * RIM]
        ref[0:WIDE] = ref[0:WIDE] + got_low[at : at + WIDE]
        ref[count - WIDE : count] = ref[count - WIDE : count] + got_high[at : at + WIDE]
    for k, ref in enumerate(short_refs):
        count = ref.shape[0]
        if k < 2:
            at = 16 + EXT * k
            ref[0:EXT] = ref[0:EXT] + got_low[at : at + EXT]
            ref[count - EXT : count] = ref[count - EXT : count] + got_high[at : at + EXT]
        else:
            for h in range(2):
                at = 8 * h + WIDE
                ref[2 * h : 2 * h + 2] = ref[2 * h : 2 * h + 2] + got_low[at : at + 2]
                back = count - EXT + 2 * h
                ref[back : back + 2] = ref[back : back + 2] + got_high[at : at + 2]


def strip_kernel(levels, s_ref, own_e, own_o, got_e, got_o, e_ref, o_ref, us, vs, uus, uvs, vvs):
    odd_x = lax.rem(lax.axis_index("gx"), 2)
    odd_y = lax.rem(lax.axis_index("gy"), 2)
    coarse = uus.shape[0]
    us[RIM : RIM + coarse] = s_ref[0:coarse]
    vs[RIM : RIM + coarse] = s_ref[coarse : 2 * coarse]
    uus[...] = s_ref[2 * coarse : 3 * coarse]
    uvs[...] = s_ref[3 * coarse : 4 * coarse]
    vvs[...] = s_ref[4 * coarse : 5 * coarse]
    own_low, own_high = low_and_high(odd_x, own_e[...], own_o[...])
    got_low, got_high = low_and_high(odd_x, got_e[got_e.shape[0] - 1], got_o[...])
    add_rows((us, vs), (uus, uvs, vvs), own_low, own_high, got_low, got_high)
    start = e_ref.shape[0] - coarse // 2
    lanes = e_ref.shape[1]
    wide, short = WIDE * levels, EXT * levels

    def laid(fields, ends, from_lane):
        lane = lax.broadcasted_iota(jnp.int32, fields[0].shape, 1)
        total, begin = None, 0
        for field, end in zip(fields, ends):
            there = pltpu.roll(field, (lanes + begin - from_lane) % lanes, 1) if begin != from_lane else field
            total = there if total is None else jnp.where(lane < begin, total, there)
            begin = end
        return total

    h = coarse // 2
    sides = []
    for from_lane in (0, HALF):
        both = laid((us[...], vs[...]), (wide, 2 * wide), from_lane)
        lane = lax.broadcasted_iota(jnp.int32, (coarse, lanes), 1)
        uu = pltpu.roll(uus[...], (lanes + 2 * wide - from_lane) % lanes, 1)
        first = jnp.where(lane < 2 * wide, both[:coarse], uu)
        quarters = (uvs[:h], uvs[h:], vvs[:h], vvs[h:])
        second = laid(quarters, [short * n for n in range(1, 5)], from_lane)
        sides.append((first, both[coarse:], second))
    for low, high, at in zip(*sides, (0, coarse, start)):
        here = slice(at, at + low.shape[0])
        e_ref[here] = jnp.where(odd_y == 0, high, low)
        o_ref[here] = jnp.where(odd_y == 0, low, high)


def first_form(plus_two, plus_one, minus_one, minus_two):
    return (8.0 * plus_one - plus_two - 8.0 * minus_one + minus_two) * (1.0 / 12.0)


def second_form(plus_two, plus_one, centre, minus_one, minus_two):
    return (16.0 * plus_one - plus_two - 30.0 * centre + 16.0 * minus_one - minus_two) * (1.0 / 12.0)


def final_kernel(
    p_ref, xe_own, xo_own, xe_got, xo_got, ye_own, yo_own, ye_got, yo_got, st_hbm, lib_hbm,
    us, vs, uus, uvs, vvs, low_side, high_side, slopes, st_ref, lib_ref, sem,
):
    odd_x = lax.rem(lax.axis_index("gx"), 2)
    odd_y = lax.rem(lax.axis_index("gy"), 2)
    levels, coarse, lanes = st_ref.shape[1:]
    rim_rows = us.shape[0]
    own_low, own_high = low_and_high(odd_y, ye_own[...], yo_own[...])
    got_low, got_high = low_and_high(odd_y, ye_got[...], yo_got[...])
    lane = lax.broadcasted_iota(jnp.int32, own_low.shape, 1)
    row = lax.broadcasted_iota(jnp.int32, own_low.shape, 0)
    wide, short = WIDE * levels, EXT * levels
    start = own_low.shape[0] - coarse // 2
    is_wide = (lane < 2 * wide) & (row < start)
    place = lax.rem(lane, WIDE)
    rim = pltpu.roll(got_low, lanes - EXT, 1) + pltpu.roll(own_low, lanes - RIM, 1)
    ordered = jnp.where(place < RIM, rim, pltpu.roll(got_low, RIM, 1))
    low_side[...] = jnp.where(is_wide, ordered, got_low)
    ahead = pltpu.roll(own_high, EXT, 1)
    high_side[...] = got_high + jnp.where(is_wide & (place >= EXT), ahead, 0.0)

    def out(level):
        return (
            pltpu.make_async_copy(st_ref.at[:, level], st_hbm.at[:, level], sem.at[0, level]),
            pltpu.make_async_copy(lib_ref.at[:, level], lib_hbm.at[:, level], sem.at[1, level]),
        )

    def finish(level):
        def part_of(k):
            return p_ref[pl.ds(pl.multiple_of((5 * level + k) * coarse, 8), coarse)]

        us[RIM : RIM + coarse] = part_of(0)
        vs[RIM : RIM + coarse] = part_of(1)
        for k, ref in enumerate((uus, uvs, vvs)):
            ref[...] = part_of(2 + k)
        own_low, own_high = low_and_high(odd_x, xe_own[level], xo_own[level])
        got_low, got_high = low_and_high(odd_x, xe_got[level], xo_got[level])
        add_rows((us, vs), (uus, uvs, vvs), own_low, own_high, got_low, got_high)

        def sides(at, count, base, cells):
            rim = RIM if cells == WIDE else 0
            first = base + cells * level
            low = pltpu.roll(low_side[at : at + count], lax.rem(2 * lanes - rim - first, lanes), 1)
            high = pltpu.roll(high_side[at : at + count], lanes - EXT - first, 1)
            return low, high

        def joined(field, low, high):
            lane = lax.broadcasted_iota(jnp.int32, field.shape, 1)
            return field + jnp.where(lane < EXT, low, 0.0) + jnp.where(lane >= lanes - EXT, high, 0.0)

        means = []
        found = []
        for k, ref in enumerate((us, vs)):
            low, high = sides(0, rim_rows, k * wide, WIDE)
            f = joined(ref[...], low, high)
            ref[...] = f
            lane = lax.broadcasted_iota(jnp.int32, f.shape, 1)
            plus_one = pltpu.roll(jnp.where(lane < 1, high, f), lanes - 1, 1)
            plus_two = pltpu.roll(jnp.where(lane < 2, high, f), lanes - 2, 1)
            minus_one = pltpu.roll(jnp.where(lane >= lanes - 1, low, f), 1, 1)
            minus_two = pltpu.roll(jnp.where(lane >= lanes - 2, low, f), 2, 1)
            slopes[...] = first_form(plus_two, plus_one, minus_one, minus_two)

            def row(source, by):
                return source[RIM + by : RIM + by + coarse]

            curve_y = second_form(plus_two, plus_one, f, minus_one, minus_two)[RIM : RIM + coarse]
            centre = row(ref, 0)
            shifted = [row(ref, by) for by in (2, 1, -1, -2)]
            grad_x = first_form(*shifted)
            curve_x = second_form(shifted[0], shifted[1], centre, shifted[2], shifted[3])
            grad_y = row(slopes, 0)
            cross = first_form(*[row(slopes, by) for by in (2, 1, -1, -2)])
            means.append(centre)
            found.append((grad_x, grad_y, curve_x, cross, curve_y))

        u, v = means
        low, high = sides(0, coarse, 2 * wide, EXT)
        st_ref[0, level] = joined(uus[...], low, high) - u * u
        for k, (ref, other) in enumerate(((uvs, u), (vvs, v))):
            for h in range(2):
                part = slice(coarse // 2 * h, coarse // 2 * (h + 1))
                low, high = sides(start, coarse // 2, (2 * k + h) * short, EXT)
                st_ref[1 + k, level, part] = joined(ref[part], low, high) - other[part] * v[part]

        (ux, uy, uxx, uxy, uyy), (vx, vy, vxx, vxy, vyy) = found
        vorticity = vx - uy
        features = (ux, uy, vx, vy, uxx, uxy, uyy, vxx, vxy, vyy, vxx - uxy, vxy - uyy)
        for k, feature in enumerate(features):
            lib_ref[4 * k, level] = feature
            lib_ref[4 * k + 1, level] = u * feature
            lib_ref[4 * k + 2, level] = v * feature
            lib_ref[4 * k + 3, level] = vorticity * feature
        for copy in out(level):
            copy.start()

    each(levels, FINAL_UNROLL, finish)
    for level in range(levels):
        for copy in out(level):
            copy.wait()


def pairs_of(axis):
    count = lax.axis_size(axis)
    assert count % 2 == 0
    even = [(i, i ^ 1) for i in range(count)]
    odd = [(i, (i + 1) % count if i % 2 else (i - 1) % count) for i in range(count)]
    return even, odd


def local_call(body, outs, scratch, *operands):
    in_vmem, in_hbm = pl.BlockSpec(memory_space=pltpu.VMEM), pl.BlockSpec(memory_space=pltpu.HBM)
    specs, arrays = [], []
    for operand, here in operands:
        specs.append(in_vmem if here else in_hbm)
        arrays.append(pltpu.with_memory_space_constraint(operand, pltpu.VMEM) if here else pltpu.with_memory_space_constraint(operand, pltpu.HBM))
    return pl.pallas_call(
        body,
        in_specs=specs,
        out_specs=[in_hbm if isinstance(o, jax.ShapeDtypeStruct) else in_vmem for o in outs],
        out_shape=outs,
        scratch_shapes=scratch,
        compiler_params=pltpu.CompilerParams(vmem_limit_bytes=VMEM_BYTES),
    )(*arrays)


def in_order(east_flow, north_flow):
    levels, count_x, count_y = east_flow.shape
    coarse, lanes = count_x // STEP, count_y // STEP
    assert lanes == 2 * HALF and (2 * WIDE + EXT) * levels <= lanes and coarse % 16 == 0
    assert count_x >= 2 * EDGE and count_y > 2 * SIDE
    three, two = (jnp.asarray(c) for c in message_rows(count_x))
    w_strips, w_ends, w_rest = (jnp.asarray(c) for c in column_weights(count_y))
    left = jnp.asarray(left_operand(taps(range(coarse), count_x)))
    rim_rows = coarse + 2 * RIM
    start = -(-rim_rows // 8) * 8
    side = (start + coarse // 2, lanes)
    own_count = 5 * coarse
    f32, bf16 = functools.partial(pltpu.VMEM, dtype=F32), functools.partial(pltpu.VMEM, dtype=BF16)

    def held(*arrays):
        return [(a, True) for a in arrays]

    (even_x, odd_x), (even_y, odd_y) = pairs_of("gx"), pairs_of("gy")
    parts = 1
    consts = (three, two, w_strips, w_ends, w_rest, left)
    se, so, ends_high, ends_low, *kept = local_call(
        slab_kernel,
        [f32((MSG, lanes))] * 2 + [bf16((48 * levels, 2 * SIDE))] * 2 + [bf16(c.shape) for c in consts],
        [f32((levels, 2 * EDGE, 2 * SIDE))] * 2
        + [pltpu.SemaphoreType.DMA((parts, 8)), pltpu.SemaphoreType.DMA((len(consts),))],
        *[(a, False) for a in (east_flow, north_flow) + consts],
    )
    message_ends = (ends_high, ends_low)
    three, two, w_strips, w_ends, w_rest, left = kept
    so_got = lax.ppermute(so, "gx", odd_x)
    fine = held(east_flow, north_flow)
    xe, xo = local_call(
        main_kernel,
        [f32((levels + 1, MSG, lanes)), f32((levels, MSG, lanes))],
        [bf16((48 * levels, count_y - 2 * SIDE))] * 2,
        *fine,
        *held(three, two, *message_ends, w_ends, w_rest, se),
    )
    xo_got = lax.ppermute(xo, "gx", odd_x)
    xe_got = lax.ppermute(xe, "gx", even_x)
    strips, *own_ends = local_call(
        ends_kernel,
        [f32((own_count, lanes))] + [bf16((own_count * levels, 2 * SIDE))] * 2,
        [],
        *fine,
        *held(left, w_strips),
    )
    rows = [f32((rim_rows, lanes))] * 2 + [f32((coarse, lanes))] * 3
    ye, yo = local_call(functools.partial(strip_kernel, levels), [f32(side)] * 2, rows, *held(strips, se, so, xe_got, so_got))
    yo_got = lax.ppermute(yo, "gy", odd_y)
    ye_got = lax.ppermute(ye, "gy", even_y)
    (partial_sums,) = local_call(
        own_kernel,
        [f32((own_count * levels, lanes))],
        [bf16((own_count * levels, count_y - 2 * SIDE))] * 2,
        *fine,
        *held(left, *own_ends, w_ends, w_rest),
    )
    outs = [jax.ShapeDtypeStruct((n, levels, coarse, lanes), F32) for n in (3, 48)]
    return local_call(
        final_kernel,
        outs,
        rows
        + [f32(side)] * 2
        + [f32((rim_rows, lanes))]
        + [f32(o.shape) for o in outs]
        + [pltpu.SemaphoreType.DMA((2, levels))],
        *held(partial_sums, xe, xo, xe_got, xo_got, ye, yo, ye_got, yo_got),
    )


def solution(mesh):
    return jax.shard_map(
        in_order,
        mesh=mesh,
        in_specs=(P(None, "gx", "gy"), P(None, "gx", "gy")),
        out_specs=(P(None, None, "gx", "gy"), P(None, None, "gx", "gy")),
        check_vma=False,
    )
```

```python
import functools

import jax
import jax.numpy as jnp
import numpy as np
from jax import lax
from jax.experimental import pallas as pl
from jax.experimental.pallas import tpu as pltpu
from jax.sharding import PartitionSpec as P

spread_cells = 5.5
REACH = 16
STEP = 4
EXT = REACH // STEP
RIM = 2
WIDE = EXT + RIM
EDGE = 24
SHORT = 16
SIDE = 128
HALF = 64
MSG = 24
F32, BF16 = jnp.float32, jnp.bfloat16
VMEM_BYTES = 24 << 20
MAIN_UNROLL, FINAL_UNROLL = 8, 1


def taps(cells, count_in):
    offsets = np.arange(2 * REACH + 1) - REACH
    bumps = np.exp(-0.5 * (offsets / spread_cells) ** 2)
    lag = np.arange(count_in)[None, :] - STEP * np.asarray(cells)[:, None]
    inside = np.abs(lag) <= REACH
    return np.where(inside, np.exp(-0.5 * (lag / spread_cells) ** 2), 0.0) / bumps.sum()


def pieces(values):
    high = values.astype(BF16)
    low = (values - high.astype(np.float64)).astype(BF16)
    return high, low


def left_operand(*sources):
    tops, bottoms = [], []
    for rows in sources:
        high, low = pieces(rows)
        tops += [high, high]
        bottoms += [low, np.zeros_like(low)]
    return np.concatenate([np.concatenate(tops, 1), np.concatenate(bottoms, 1)], 0)


def message_rows(count_x):
    coarse = count_x // STEP

    def rows(cells, ends):
        full = taps(cells, count_x)
        return np.concatenate([full[:, :ends], full[:, count_x - ends :]], 1)

    wide = {"low": rows(range(-EXT, RIM), EDGE), "high": rows(range(coarse - RIM, coarse + EXT), EDGE)}
    short = {"low": rows(range(-EXT, 0), SHORT), "high": rows(range(coarse, coarse + EXT), SHORT)}

    def placed(at, parts):
        blocks = []
        for part in parts:
            block = np.zeros((8, part.shape[1]))
            block[at : at + part.shape[0]] = part
            blocks.append(block)
        return np.concatenate(blocks, 0)

    three, two = [], []
    for sides in (("high", "low"), ("low", "high")):
        w = placed(0, [wide[s] for s in sides])
        none = np.zeros_like(w)
        vv = [placed(WIDE, [short[s][2 * h : 2 * h + 2] for s in sides]) for h in range(2)]
        three.append(left_operand(np.concatenate([w, none]), np.concatenate([none, w]), np.concatenate(vv)))
        two.append(left_operand(*[placed(EXT * h, [short[s] for s in sides]) for h in range(2)]))
    return np.stack(three), np.stack(two)


def column_weights(count_y):
    coarse = count_y // STEP
    own = taps(range(coarse), count_y).T
    strips = np.zeros((count_y, 2 * HALF))
    strips[:, :WIDE] = taps(range(-EXT, RIM), count_y).T
    high = list(range(coarse, coarse + EXT)) + list(range(coarse - RIM, coarse))
    strips[:, HALF : HALF + WIDE] = taps(high, count_y).T

    def ends(w):
        return np.concatenate([w[:SIDE], w[count_y - SIDE :]], 0)

    return tuple(np.concatenate(pieces(w), 1) for w in (ends(strips), ends(own), own[SIDE : count_y - SIDE]))


def split(values):
    high = values.astype(BF16)
    return high, (values - high.astype(F32)).astype(BF16)


def row_sums(left, field):
    high, low = split(field)
    both = jnp.dot(left, jnp.concatenate([high, low], 0), preferred_element_type=F32)
    half = both.shape[0] // 2
    return both[:half] + both[half:]


def column_sums(high, low, weights):
    count = weights.shape[1] // 2
    both = jnp.dot(high, weights[...], preferred_element_type=F32)
    return both[:, :count] + both[:, count:] + jnp.dot(low, weights[:, :count], preferred_element_type=F32)


def products(u, v):
    return u, v, u * u, u * v, v * v


def each(count, unroll, body):
    lax.fori_loop(0, count, lambda i, _: (body(i), None)[1], None, unroll=unroll)


def message_sums(three, two, u, v):
    us, vs = (jnp.concatenate([f[:SHORT], f[2 * EDGE - SHORT :]], 0) for f in (u, v))
    first = jnp.concatenate([*split(u), *split(v), *split(vs * vs)], 0)
    second = jnp.concatenate([*split(us * us), *split(us * vs)], 0)
    first = jnp.dot(three, first, preferred_element_type=F32)
    second = jnp.dot(two, second, preferred_element_type=F32)
    return jnp.concatenate([first[:32] + first[32:], second[:16] + second[16:]], 0)


def slab_kernel(
    u_hbm, v_hbm, three_hbm, two_hbm, w_hbm, w_ends_hbm, w_rest_hbm, left_hbm,
    e_ref, o_ref, x_high, x_low, three, two, weights, w_ends, w_rest, left,
    u_ref, v_ref, sem, const_sem,
):
    odd = lax.rem(lax.axis_index("gx"), 2)
    levels = u_ref.shape[0]
    _, count_x, count_y = u_hbm.shape
    parts = sem.shape[0]
    batch = levels // parts

    def loads(part):
        some = pl.ds(part * batch, batch)
        copies = []
        for f, (source, held) in enumerate(((u_hbm, u_ref), (v_hbm, v_ref))):
            for r in range(2):
                for c in range(2):
                    copies.append(
                        pltpu.make_async_copy(
                            source.at[
                                some, pl.ds(r * (count_x - EDGE), EDGE), pl.ds(c * (count_y - SIDE), SIDE)
                            ],
                            held.at[some, pl.ds(r * EDGE, EDGE), pl.ds(c * SIDE, SIDE)],
                            sem.at[part, 4 * f + 2 * r + c],
                        )
                    )
        return copies

    consts = [
        pltpu.make_async_copy(source, held, const_sem.at[k])
        for k, (source, held) in enumerate(
            (
                (three_hbm, three),
                (two_hbm, two),
                (w_hbm, weights),
                (left_hbm, left),
                (w_ends_hbm, w_ends),
                (w_rest_hbm, w_rest),
            )
        )
    ]
    for copy in loads(0) + consts[:3]:
        copy.start()
    for part in range(1, parts):
        for copy in loads(part):
            copy.start()
    for copy in consts[3:]:
        copy.start()
    for copy in consts[:3]:
        copy.wait()
    for part in range(parts):
        for copy in loads(part):
            copy.wait()

        for level in range(part * batch, (part + 1) * batch):
            at = slice(level * 48, (level + 1) * 48)
            x_high[at], x_low[at] = split(message_sums(three[odd], two[odd], u_ref[level], v_ref[level]))
    sums = column_sums(x_high[...], x_low[...], weights)
    row = lax.broadcasted_iota(jnp.int32, e_ref.shape, 0)
    wide = (row < 16) & (lax.rem(row, 8) < WIDE)
    for place, ref in ((0, e_ref), (8, o_ref)):
        parts = [message_of(sums, level, place) for level in range(levels)]
        ref[...] = jnp.where(wide, packed(parts, WIDE), packed([short_only(p) for p in parts], EXT))
    for copy in consts[3:]:
        copy.wait()


def short_only(strips):
    lane = lax.broadcasted_iota(jnp.int32, strips.shape, 1)
    return jnp.where(lax.rem(lane, HALF) < EXT, strips, 0.0)


def packed(parts, cells):
    return added([pltpu.roll(part, cells * level, 1) for level, part in enumerate(parts)])


def added(terms):
    while len(terms) > 1:
        terms = [a + b for a, b in zip(terms[::2], terms[1::2])] + terms[len(terms) & ~1 :]
    return terms[0]


def message_of(sums, level, place):
    return jnp.concatenate([sums[48 * level + 16 * t + place : 48 * level + 16 * t + place + 8] for t in range(3)], 0)


def middle(ref):
    count_y = ref.shape[-1]
    return pl.ds(SIDE, count_y - 2 * SIDE)


def main_kernel(
    u_ref, v_ref, three, two, ends_high, ends_low, w_ends, w_rest, slab_ref, e_ref, o_ref, x_high, x_low
):
    odd = lax.rem(lax.axis_index("gx"), 2)
    levels, count_x = u_ref.shape[:2]

    def rows_of(level):
        u, v = (
            jnp.concatenate([r[level, :EDGE, middle(r)], r[level, count_x - EDGE :, middle(r)]], 0)
            for r in (u_ref, v_ref)
        )
        at = pl.ds(pl.multiple_of(level * 48, 16), 48)
        x_high[at], x_low[at] = split(message_sums(three[odd], two[odd], u, v))

    each(levels, MAIN_UNROLL, rows_of)
    sums = column_sums(ends_high[...], ends_low[...], w_ends) + column_sums(x_high[...], x_low[...], w_rest)
    for place, ref in ((0, e_ref), (8, o_ref)):
        for level in range(levels):
            ref[level] = message_of(sums, level, place)
    e_ref[levels] = slab_ref[...]


def own_rows_of(left, u, v):
    return split(jnp.concatenate([row_sums(left, f) for f in products(u, v)], 0))


def ends_kernel(u_ref, v_ref, left, weights, s_ref, x_high, x_low, y_high, y_low):
    levels, _, count_y = u_ref.shape
    rows, lanes = s_ref.shape

    few = levels - x_high.shape[0] // rows
    lane = lax.broadcasted_iota(jnp.int32, (u_ref.shape[1], SIDE), 1)
    for level in range(levels):
        ends = [(r[level, :, :SIDE], r[level, :, count_y - SIDE :]) for r in (u_ref, v_ref)]
        if level < few:
            u, v = (jnp.where(lane < HALF, first, last) for first, last in ends)
            at = slice(level * rows, (level + 1) * rows)
            y_high[at], y_low[at] = own_rows_of(left[...], u, v)
        else:
            u, v = (jnp.concatenate(pair, 1) for pair in ends)
            at = slice((level - few) * rows, (level - few + 1) * rows)
            x_high[at], x_low[at] = own_rows_of(left[...], u, v)
    packed_weights = jnp.concatenate([weights[:HALF], weights[2 * SIDE - HALF :]], 0)
    wide = rows // 5 * 2
    strips, short = jnp.zeros((wide, lanes), F32), jnp.zeros((rows - wide, lanes), F32)
    for level in range(levels):
        if level < few:
            at = slice(level * rows, (level + 1) * rows)
            sums = column_sums(y_high[at], y_low[at], packed_weights)
        else:
            at = slice((level - few) * rows, (level - few + 1) * rows)
            sums = column_sums(x_high[at], x_low[at], weights)
        strips = strips + pltpu.roll(sums[:wide], WIDE * level, 1)
        short = short + pltpu.roll(short_only(sums[wide:]), EXT * level, 1)
    s_ref[:wide] = strips
    s_ref[wide:] = short


def own_kernel(
    u_ref, v_ref, left, ends_high, ends_low, w_ends, w_rest, p_ref, x_high, x_low, y_high, y_low
):
    levels, _, count_y = u_ref.shape
    rows = p_ref.shape[0] // levels
    few = y_high.shape[0] // rows
    for level in range(levels):
        at = slice(level * rows, (level + 1) * rows)
        if level < few:
            high, low = own_rows_of(left[...], u_ref[level], v_ref[level])
            for whole, rest, ends in ((high, x_high, y_high), (low, x_low, y_low)):
                rest[at] = whole[:, SIDE : count_y - SIDE]
                ends[at] = jnp.concatenate([whole[:, :SIDE], whole[:, count_y - SIDE :]], 1)
        else:
            x_high[at], x_low[at] = own_rows_of(
                left[...], u_ref[level, :, middle(u_ref)], v_ref[level, :, middle(v_ref)]
            )
    for level in range(0, levels, 2):
        at = slice(level * rows, (level + 2) * rows)
        if level < few:
            ends = column_sums(y_high[at], y_low[at], w_ends)
        else:
            kept = slice((level - few) * rows, (level - few + 2) * rows)
            ends = column_sums(ends_high[kept], ends_low[kept], w_ends)
        p_ref[at] = ends + column_sums(x_high[at], x_low[at], w_rest)


def low_and_high(odd, e, o):
    return jnp.where(odd == 0, o, e), jnp.where(odd == 0, e, o)


def add_rows(wide_refs, short_refs, own_low, own_high, got_low, got_high):
    for k, ref in enumerate(wide_refs):
        count = ref.shape[0]
        at = 8 * k
        ref[0:RIM] = own_low[at + EXT - RIM : at + EXT]
        ref[count - RIM : count] = own_high[at + RIM : at + 2 * RIM]
        ref[0:WIDE] = ref[0:WIDE] + got_low[at : at + WIDE]
        ref[count - WIDE : count] = ref[count - WIDE : count] + got_high[at : at + WIDE]
    for k, ref in enumerate(short_refs):
        count = ref.shape[0]
        if k < 2:
            at = 16 + EXT * k
            ref[0:EXT] = ref[0:EXT] + got_low[at : at + EXT]
            ref[count - EXT : count] = ref[count - EXT : count] + got_high[at : at + EXT]
        else:
            for h in range(2):
                at = 8 * h + WIDE
                ref[2 * h : 2 * h + 2] = ref[2 * h : 2 * h + 2] + got_low[at : at + 2]
                back = count - EXT + 2 * h
                ref[back : back + 2] = ref[back : back + 2] + got_high[at : at + 2]


def strip_kernel(levels, s_ref, own_e, own_o, got_e, got_o, e_ref, o_ref, us, vs, uus, uvs, vvs):
    odd_x = lax.rem(lax.axis_index("gx"), 2)
    odd_y = lax.rem(lax.axis_index("gy"), 2)
    coarse = uus.shape[0]
    us[RIM : RIM + coarse] = s_ref[0:coarse]
    vs[RIM : RIM + coarse] = s_ref[coarse : 2 * coarse]
    uus[...] = s_ref[2 * coarse : 3 * coarse]
    uvs[...] = s_ref[3 * coarse : 4 * coarse]
    vvs[...] = s_ref[4 * coarse : 5 * coarse]
    own_low, own_high = low_and_high(odd_x, own_e[...], own_o[...])
    got_low, got_high = low_and_high(odd_x, got_e[got_e.shape[0] - 1], got_o[...])
    add_rows((us, vs), (uus, uvs, vvs), own_low, own_high, got_low, got_high)
    start = e_ref.shape[0] - coarse // 2
    lanes = e_ref.shape[1]
    wide, short = WIDE * levels, EXT * levels

    def laid(fields, ends, from_lane):
        lane = lax.broadcasted_iota(jnp.int32, fields[0].shape, 1)
        total, begin = None, 0
        for field, end in zip(fields, ends):
            there = pltpu.roll(field, (lanes + begin - from_lane) % lanes, 1) if begin != from_lane else field
            total = there if total is None else jnp.where(lane < begin, total, there)
            begin = end
        return total

    h = coarse // 2
    sides = []
    for from_lane in (0, HALF):
        both = laid((us[...], vs[...]), (wide, 2 * wide), from_lane)
        lane = lax.broadcasted_iota(jnp.int32, (coarse, lanes), 1)
        uu = pltpu.roll(uus[...], (lanes + 2 * wide - from_lane) % lanes, 1)
        first = jnp.where(lane < 2 * wide, both[:coarse], uu)
        quarters = (uvs[:h], uvs[h:], vvs[:h], vvs[h:])
        second = laid(quarters, [short * n for n in range(1, 5)], from_lane)
        sides.append((first, both[coarse:], second))
    for low, high, at in zip(*sides, (0, coarse, start)):
        here = slice(at, at + low.shape[0])
        e_ref[here] = jnp.where(odd_y == 0, high, low)
        o_ref[here] = jnp.where(odd_y == 0, low, high)


def first_form(plus_two, plus_one, minus_one, minus_two):
    return (8.0 * plus_one - plus_two - 8.0 * minus_one + minus_two) * (1.0 / 12.0)


def second_form(plus_two, plus_one, centre, minus_one, minus_two):
    return (16.0 * plus_one - plus_two - 30.0 * centre + 16.0 * minus_one - minus_two) * (1.0 / 12.0)


def final_kernel(
    p_ref, xe_own, xo_own, xe_got, xo_got, ye_own, yo_own, ye_got, yo_got, st_hbm, lib_hbm,
    us, vs, uus, uvs, vvs, low_side, high_side, slopes, st_ref, lib_ref, sem,
):
    odd_x = lax.rem(lax.axis_index("gx"), 2)
    odd_y = lax.rem(lax.axis_index("gy"), 2)
    levels, coarse, lanes = st_ref.shape[1:]
    rim_rows = us.shape[0]
    own_low, own_high = low_and_high(odd_y, ye_own[...], yo_own[...])
    got_low, got_high = low_and_high(odd_y, ye_got[...], yo_got[...])
    lane = lax.broadcasted_iota(jnp.int32, own_low.shape, 1)
    row = lax.broadcasted_iota(jnp.int32, own_low.shape, 0)
    wide, short = WIDE * levels, EXT * levels
    start = own_low.shape[0] - coarse // 2
    is_wide = (lane < 2 * wide) & (row < start)
    place = lax.rem(lane, WIDE)
    rim = pltpu.roll(got_low, lanes - EXT, 1) + pltpu.roll(own_low, lanes - RIM, 1)
    ordered = jnp.where(place < RIM, rim, pltpu.roll(got_low, RIM, 1))
    low_side[...] = jnp.where(is_wide, ordered, got_low)
    ahead = pltpu.roll(own_high, EXT, 1)
    high_side[...] = got_high + jnp.where(is_wide & (place >= EXT), ahead, 0.0)

    def out(level):
        return (
            pltpu.make_async_copy(st_ref.at[:, level], st_hbm.at[:, level], sem.at[0, level]),
            pltpu.make_async_copy(lib_ref.at[:, level], lib_hbm.at[:, level], sem.at[1, level]),
        )

    def finish(level):
        def part_of(k):
            return p_ref[pl.ds(pl.multiple_of((5 * level + k) * coarse, 8), coarse)]

        us[RIM : RIM + coarse] = part_of(0)
        vs[RIM : RIM + coarse] = part_of(1)
        for k, ref in enumerate((uus, uvs, vvs)):
            ref[...] = part_of(2 + k)
        own_low, own_high = low_and_high(odd_x, xe_own[level], xo_own[level])
        got_low, got_high = low_and_high(odd_x, xe_got[level], xo_got[level])
        add_rows((us, vs), (uus, uvs, vvs), own_low, own_high, got_low, got_high)

        def sides(at, count, base, cells):
            rim = RIM if cells == WIDE else 0
            first = base + cells * level
            low = pltpu.roll(low_side[at : at + count], lax.rem(2 * lanes - rim - first, lanes), 1)
            high = pltpu.roll(high_side[at : at + count], lanes - EXT - first, 1)
            return low, high

        def joined(field, low, high):
            lane = lax.broadcasted_iota(jnp.int32, field.shape, 1)
            return field + jnp.where(lane < EXT, low, 0.0) + jnp.where(lane >= lanes - EXT, high, 0.0)

        means = []
        found = []
        for k, ref in enumerate((us, vs)):
            low, high = sides(0, rim_rows, k * wide, WIDE)
            f = joined(ref[...], low, high)
            ref[...] = f
            lane = lax.broadcasted_iota(jnp.int32, f.shape, 1)
            plus_one = pltpu.roll(jnp.where(lane < 1, high, f), lanes - 1, 1)
            plus_two = pltpu.roll(jnp.where(lane < 2, high, f), lanes - 2, 1)
            minus_one = pltpu.roll(jnp.where(lane >= lanes - 1, low, f), 1, 1)
            minus_two = pltpu.roll(jnp.where(lane >= lanes - 2, low, f), 2, 1)
            slopes[...] = first_form(plus_two, plus_one, minus_one, minus_two)

            def row(source, by):
                return source[RIM + by : RIM + by + coarse]

            curve_y = second_form(plus_two, plus_one, f, minus_one, minus_two)[RIM : RIM + coarse]
            centre = row(ref, 0)
            shifted = [row(ref, by) for by in (2, 1, -1, -2)]
            grad_x = first_form(*shifted)
            curve_x = second_form(shifted[0], shifted[1], centre, shifted[2], shifted[3])
            grad_y = row(slopes, 0)
            cross = first_form(*[row(slopes, by) for by in (2, 1, -1, -2)])
            means.append(centre)
            found.append((grad_x, grad_y, curve_x, cross, curve_y))

        u, v = means
        low, high = sides(0, coarse, 2 * wide, EXT)
        st_ref[0, level] = joined(uus[...], low, high) - u * u
        for k, (ref, other) in enumerate(((uvs, u), (vvs, v))):
            for h in range(2):
                part = slice(coarse // 2 * h, coarse // 2 * (h + 1))
                low, high = sides(start, coarse // 2, (2 * k + h) * short, EXT)
                st_ref[1 + k, level, part] = joined(ref[part], low, high) - other[part] * v[part]

        (ux, uy, uxx, uxy, uyy), (vx, vy, vxx, vxy, vyy) = found
        vorticity = vx - uy
        features = (ux, uy, vx, vy, uxx, uxy, uyy, vxx, vxy, vyy, vxx - uxy, vxy - uyy)
        for k, feature in enumerate(features):
            lib_ref[4 * k, level] = feature
            lib_ref[4 * k + 1, level] = u * feature
            lib_ref[4 * k + 2, level] = v * feature
            lib_ref[4 * k + 3, level] = vorticity * feature
        for copy in out(level):
            copy.start()

    each(levels, FINAL_UNROLL, finish)
    for level in range(levels):
        for copy in out(level):
            copy.wait()


def pairs_of(axis):
    count = lax.axis_size(axis)
    assert count % 2 == 0
    even = [(i, i ^ 1) for i in range(count)]
    odd = [(i, (i + 1) % count if i % 2 else (i - 1) % count) for i in range(count)]
    return even, odd


def local_call(body, outs, scratch, *operands):
    in_vmem, in_hbm = pl.BlockSpec(memory_space=pltpu.VMEM), pl.BlockSpec(memory_space=pltpu.HBM)
    specs, arrays = [], []
    for operand, here in operands:
        specs.append(in_vmem if here else in_hbm)
        arrays.append(pltpu.with_memory_space_constraint(operand, pltpu.VMEM) if here else pltpu.with_memory_space_constraint(operand, pltpu.HBM))
    return pl.pallas_call(
        body,
        in_specs=specs,
        out_specs=[in_hbm if isinstance(o, jax.ShapeDtypeStruct) else in_vmem for o in outs],
        out_shape=outs,
        scratch_shapes=scratch,
        compiler_params=pltpu.CompilerParams(vmem_limit_bytes=VMEM_BYTES),
    )(*arrays)


def in_order(east_flow, north_flow):
    levels, count_x, count_y = east_flow.shape
    coarse, lanes = count_x // STEP, count_y // STEP
    assert lanes == 2 * HALF and (2 * WIDE + EXT) * levels <= lanes and coarse % 16 == 0
    assert count_x >= 2 * EDGE and count_y > 2 * SIDE
    three, two = (jnp.asarray(c) for c in message_rows(count_x))
    w_strips, w_ends, w_rest = (jnp.asarray(c) for c in column_weights(count_y))
    left = jnp.asarray(left_operand(taps(range(coarse), count_x)))
    rim_rows = coarse + 2 * RIM
    start = -(-rim_rows // 8) * 8
    side = (start + coarse // 2, lanes)
    own_count = 5 * coarse
    f32, bf16 = functools.partial(pltpu.VMEM, dtype=F32), functools.partial(pltpu.VMEM, dtype=BF16)

    def held(*arrays):
        return [(a, True) for a in arrays]

    (even_x, odd_x), (even_y, odd_y) = pairs_of("gx"), pairs_of("gy")
    parts, few = 1, levels // 4 * 3
    consts = (three, two, w_strips, w_ends, w_rest, left)
    se, so, ends_high, ends_low, *kept = local_call(
        slab_kernel,
        [f32((MSG, lanes))] * 2 + [bf16((48 * levels, 2 * SIDE))] * 2 + [bf16(c.shape) for c in consts],
        [f32((levels, 2 * EDGE, 2 * SIDE))] * 2
        + [pltpu.SemaphoreType.DMA((parts, 8)), pltpu.SemaphoreType.DMA((len(consts),))],
        *[(a, False) for a in (east_flow, north_flow) + consts],
    )
    message_ends = (ends_high, ends_low)
    three, two, w_strips, w_ends, w_rest, left = kept
    so_got = lax.ppermute(so, "gx", odd_x)
    fine = held(east_flow, north_flow)
    xe, xo = local_call(
        main_kernel,
        [f32((levels + 1, MSG, lanes)), f32((levels, MSG, lanes))],
        [bf16((48 * levels, count_y - 2 * SIDE))] * 2,
        *fine,
        *held(three, two, *message_ends, w_ends, w_rest, se),
    )
    xo_got = lax.ppermute(xo, "gx", odd_x)
    xe_got = lax.ppermute(xe, "gx", even_x)
    strips, *own_ends = local_call(
        ends_kernel,
        [f32((own_count, lanes))] + [bf16((own_count * (levels - few), 2 * SIDE))] * 2,
        [bf16((own_count * few, SIDE))] * 2,
        *fine,
        *held(left, w_strips),
    )
    rows = [f32((rim_rows, lanes))] * 2 + [f32((coarse, lanes))] * 3
    ye, yo = local_call(functools.partial(strip_kernel, levels), [f32(side)] * 2, rows, *held(strips, se, so, xe_got, so_got))
    yo_got = lax.ppermute(yo, "gy", odd_y)
    ye_got = lax.ppermute(ye, "gy", even_y)
    (partial_sums,) = local_call(
        own_kernel,
        [f32((own_count * levels, lanes))],
        [bf16((own_count * levels, count_y - 2 * SIDE))] * 2 + [bf16((own_count * few, 2 * SIDE))] * 2,
        *fine,
        *held(left, *own_ends, w_ends, w_rest),
    )
    outs = [jax.ShapeDtypeStruct((n, levels, coarse, lanes), F32) for n in (3, 48)]
    return local_call(
        final_kernel,
        outs,
        rows
        + [f32(side)] * 2
        + [f32((rim_rows, lanes))]
        + [f32(o.shape) for o in outs]
        + [pltpu.SemaphoreType.DMA((2, levels))],
        *held(partial_sums, xe, xo, xe_got, xo_got, ye, yo, ye_got, yo_got),
    )


def solution(mesh):
    return jax.shard_map(
        in_order,
        mesh=mesh,
        in_specs=(P(None, "gx", "gy"), P(None, "gx", "gy")),
        out_specs=(P(None, None, "gx", "gy"), P(None, None, "gx", "gy")),
        check_vma=False,
    )
```

```python
import functools

import jax
import jax.numpy as jnp
import numpy as np
from jax import lax
from jax.experimental import pallas as pl
from jax.experimental.pallas import tpu as pltpu
from jax.sharding import PartitionSpec as P

spread_cells = 5.5
REACH = 16
STEP = 4
EXT = REACH // STEP
RIM = 2
WIDE = EXT + RIM
EDGE = 24
SHORT = 16
SIDE = 128
HALF = 64
MSG = 24
F32, BF16 = jnp.float32, jnp.bfloat16
VMEM_BYTES = 24 << 20
MAIN_UNROLL, FINAL_UNROLL = 8, 1


def taps(cells, count_in):
    offsets = np.arange(2 * REACH + 1) - REACH
    bumps = np.exp(-0.5 * (offsets / spread_cells) ** 2)
    lag = np.arange(count_in)[None, :] - STEP * np.asarray(cells)[:, None]
    inside = np.abs(lag) <= REACH
    return np.where(inside, np.exp(-0.5 * (lag / spread_cells) ** 2), 0.0) / bumps.sum()


def pieces(values):
    high = values.astype(BF16)
    low = (values - high.astype(np.float64)).astype(BF16)
    return high, low


def left_operand(*sources):
    tops, bottoms = [], []
    for rows in sources:
        high, low = pieces(rows)
        tops += [high, high]
        bottoms += [low, np.zeros_like(low)]
    return np.concatenate([np.concatenate(tops, 1), np.concatenate(bottoms, 1)], 0)


def message_rows(count_x):
    coarse = count_x // STEP

    def rows(cells, ends):
        full = taps(cells, count_x)
        return np.concatenate([full[:, :ends], full[:, count_x - ends :]], 1)

    wide = {"low": rows(range(-EXT, RIM), EDGE), "high": rows(range(coarse - RIM, coarse + EXT), EDGE)}
    short = {"low": rows(range(-EXT, 0), SHORT), "high": rows(range(coarse, coarse + EXT), SHORT)}

    def placed(at, parts):
        blocks = []
        for part in parts:
            block = np.zeros((8, part.shape[1]))
            block[at : at + part.shape[0]] = part
            blocks.append(block)
        return np.concatenate(blocks, 0)

    three, two = [], []
    for sides in (("high", "low"), ("low", "high")):
        w = placed(0, [wide[s] for s in sides])
        none = np.zeros_like(w)
        vv = [placed(WIDE, [short[s][2 * h : 2 * h + 2] for s in sides]) for h in range(2)]
        three.append(left_operand(np.concatenate([w, none]), np.concatenate([none, w]), np.concatenate(vv)))
        two.append(left_operand(*[placed(EXT * h, [short[s] for s in sides]) for h in range(2)]))
    return np.stack(three), np.stack(two)


def column_weights(count_y):
    coarse = count_y // STEP
    own = taps(range(coarse), count_y).T
    strips = np.zeros((count_y, 2 * HALF))
    strips[:, :WIDE] = taps(range(-EXT, RIM), count_y).T
    high = list(range(coarse, coarse + EXT)) + list(range(coarse - RIM, coarse))
    strips[:, HALF : HALF + WIDE] = taps(high, count_y).T

    def ends(w):
        return np.concatenate([w[:SIDE], w[count_y - SIDE :]], 0)

    return tuple(np.concatenate(pieces(w), 1) for w in (ends(strips), ends(own), own[SIDE : count_y - SIDE]))


def split(values):
    high = values.astype(BF16)
    return high, (values - high.astype(F32)).astype(BF16)


def row_sums(left, field):
    high, low = split(field)
    both = jnp.dot(left, jnp.concatenate([high, low], 0), preferred_element_type=F32)
    half = both.shape[0] // 2
    return both[:half] + both[half:]


def column_sums(high, low, weights):
    count = weights.shape[1] // 2
    both = jnp.dot(high, weights[...], preferred_element_type=F32)
    return both[:, :count] + both[:, count:] + jnp.dot(low, weights[:, :count], preferred_element_type=F32)


def products(u, v):
    return u, v, u * u, u * v, v * v


def each(count, unroll, body):
    lax.fori_loop(0, count, lambda i, _: (body(i), None)[1], None, unroll=unroll)


def message_sums(three, two, u, v):
    us, vs = (jnp.concatenate([f[:SHORT], f[2 * EDGE - SHORT :]], 0) for f in (u, v))
    first = jnp.concatenate([*split(u), *split(v), *split(vs * vs)], 0)
    second = jnp.concatenate([*split(us * us), *split(us * vs)], 0)
    first = jnp.dot(three, first, preferred_element_type=F32)
    second = jnp.dot(two, second, preferred_element_type=F32)
    return jnp.concatenate([first[:32] + first[32:], second[:16] + second[16:]], 0)


def slab_kernel(
    u_hbm, v_hbm, three_hbm, two_hbm, w_hbm, w_ends_hbm, w_rest_hbm, left_hbm,
    e_ref, o_ref, x_high, x_low, three, two, weights, w_ends, w_rest, left,
    u_ref, v_ref, sem, const_sem,
):
    odd = lax.rem(lax.axis_index("gx"), 2)
    levels = u_ref.shape[0]
    _, count_x, count_y = u_hbm.shape
    parts = sem.shape[0]
    batch = levels // parts

    def loads(part):
        some = pl.ds(part * batch, batch)
        copies = []
        for f, (source, held) in enumerate(((u_hbm, u_ref), (v_hbm, v_ref))):
            for r in range(2):
                for c in range(2):
                    copies.append(
                        pltpu.make_async_copy(
                            source.at[
                                some, pl.ds(r * (count_x - EDGE), EDGE), pl.ds(c * (count_y - SIDE), SIDE)
                            ],
                            held.at[some, pl.ds(r * EDGE, EDGE), pl.ds(c * SIDE, SIDE)],
                            sem.at[part, 4 * f + 2 * r + c],
                        )
                    )
        return copies

    consts = [
        pltpu.make_async_copy(source, held, const_sem.at[k])
        for k, (source, held) in enumerate(
            (
                (three_hbm, three),
                (two_hbm, two),
                (w_hbm, weights),
                (left_hbm, left),
                (w_ends_hbm, w_ends),
                (w_rest_hbm, w_rest),
            )
        )
    ]
    for copy in loads(0) + consts[:3]:
        copy.start()
    for part in range(1, parts):
        for copy in loads(part):
            copy.start()
    for copy in consts[3:]:
        copy.start()
    for copy in consts[:3]:
        copy.wait()
    for part in range(parts):
        for copy in loads(part):
            copy.wait()

        for level in range(part * batch, (part + 1) * batch):
            at = slice(level * 48, (level + 1) * 48)
            x_high[at], x_low[at] = split(message_sums(three[odd], two[odd], u_ref[level], v_ref[level]))
    sums = column_sums(x_high[...], x_low[...], weights)
    row = lax.broadcasted_iota(jnp.int32, e_ref.shape, 0)
    wide = (row < 16) & (lax.rem(row, 8) < WIDE)
    for place, ref in ((0, e_ref), (8, o_ref)):
        parts = [message_of(sums, level, place) for level in range(levels)]
        ref[...] = jnp.where(wide, packed(parts, WIDE), packed([short_only(p) for p in parts], EXT))
    for copy in consts[3:]:
        copy.wait()


def short_only(strips):
    lane = lax.broadcasted_iota(jnp.int32, strips.shape, 1)
    return jnp.where(lax.rem(lane, HALF) < EXT, strips, 0.0)


def packed(parts, cells):
    return added([pltpu.roll(part, cells * level, 1) for level, part in enumerate(parts)])


def added(terms):
    while len(terms) > 1:
        terms = [a + b for a, b in zip(terms[::2], terms[1::2])] + terms[len(terms) & ~1 :]
    return terms[0]


def message_of(sums, level, place):
    return jnp.concatenate([sums[48 * level + 16 * t + place : 48 * level + 16 * t + place + 8] for t in range(3)], 0)


def middle(ref):
    count_y = ref.shape[-1]
    return pl.ds(SIDE, count_y - 2 * SIDE)


def main_kernel(
    u_ref, v_ref, three, two, ends_high, ends_low, w_ends, w_rest, e_ref, o_ref, x_high, x_low
):
    odd = lax.rem(lax.axis_index("gx"), 2)
    levels, count_x = u_ref.shape[:2]

    def rows_of(level):
        u, v = (
            jnp.concatenate([r[level, :EDGE, middle(r)], r[level, count_x - EDGE :, middle(r)]], 0)
            for r in (u_ref, v_ref)
        )
        at = pl.ds(pl.multiple_of(level * 48, 16), 48)
        x_high[at], x_low[at] = split(message_sums(three[odd], two[odd], u, v))

    each(levels, MAIN_UNROLL, rows_of)
    sums = column_sums(ends_high[...], ends_low[...], w_ends) + column_sums(x_high[...], x_low[...], w_rest)
    for place, ref in ((0, e_ref), (8, o_ref)):
        for level in range(levels):
            ref[level] = message_of(sums, level, place)


def own_rows_of(left, u, v):
    return split(jnp.concatenate([row_sums(left, f) for f in products(u, v)], 0))


def ends_kernel(u_ref, v_ref, left, weights, s_ref, x_high, x_low):
    levels, count_x, count_y = u_ref.shape
    rows, lanes = s_ref.shape
    lane = lax.broadcasted_iota(jnp.int32, (count_x, SIDE), 1)
    for level in range(levels):
        u, v = (
            jnp.where(lane < HALF, r[level, :, :SIDE], r[level, :, count_y - SIDE :]) for r in (u_ref, v_ref)
        )
        at = slice(level * rows, (level + 1) * rows)
        x_high[at], x_low[at] = own_rows_of(left[...], u, v)
    read = jnp.concatenate([weights[:HALF], weights[2 * SIDE - HALF :]], 0)
    wide = rows // 5 * 2
    strips, short = jnp.zeros((wide, lanes), F32), jnp.zeros((rows - wide, lanes), F32)
    for level in range(levels):
        at = slice(level * rows, (level + 1) * rows)
        sums = column_sums(x_high[at], x_low[at], read)
        strips = strips + pltpu.roll(sums[:wide], WIDE * level, 1)
        short = short + pltpu.roll(short_only(sums[wide:]), EXT * level, 1)
    s_ref[:wide] = strips
    s_ref[wide:] = short


def own_kernel(u_ref, v_ref, left, w_ends, w_rest, p_ref, x_high, x_low):
    levels = u_ref.shape[0]
    rows = p_ref.shape[0] // levels
    for level in range(levels):
        at = slice(level * rows, (level + 1) * rows)
        x_high[at], x_low[at] = own_rows_of(left[...], u_ref[level], v_ref[level])
    weights = jnp.concatenate([w_ends[:SIDE], w_rest[...], w_ends[SIDE:]], 0)
    for level in range(0, levels, 2):
        at = slice(level * rows, (level + 2) * rows)
        p_ref[at] = column_sums(x_high[at], x_low[at], weights)


def low_and_high(odd, e, o):
    return jnp.where(odd == 0, o, e), jnp.where(odd == 0, e, o)


def add_rows(wide_refs, short_refs, own_low, own_high, got_low, got_high):
    for k, ref in enumerate(wide_refs):
        count = ref.shape[0]
        at = 8 * k
        ref[0:RIM] = own_low[at + EXT - RIM : at + EXT]
        ref[count - RIM : count] = own_high[at + RIM : at + 2 * RIM]
        ref[0:WIDE] = ref[0:WIDE] + got_low[at : at + WIDE]
        ref[count - WIDE : count] = ref[count - WIDE : count] + got_high[at : at + WIDE]
    for k, ref in enumerate(short_refs):
        count = ref.shape[0]
        if k < 2:
            at = 16 + EXT * k
            ref[0:EXT] = ref[0:EXT] + got_low[at : at + EXT]
            ref[count - EXT : count] = ref[count - EXT : count] + got_high[at : at + EXT]
        else:
            for h in range(2):
                at = 8 * h + WIDE
                ref[2 * h : 2 * h + 2] = ref[2 * h : 2 * h + 2] + got_low[at : at + 2]
                back = count - EXT + 2 * h
                ref[back : back + 2] = ref[back : back + 2] + got_high[at : at + 2]


def strip_kernel(levels, s_ref, own_e, own_o, got_e, got_o, e_ref, o_ref, us, vs, uus, uvs, vvs):
    odd_x = lax.rem(lax.axis_index("gx"), 2)
    odd_y = lax.rem(lax.axis_index("gy"), 2)
    coarse = uus.shape[0]
    us[RIM : RIM + coarse] = s_ref[0:coarse]
    vs[RIM : RIM + coarse] = s_ref[coarse : 2 * coarse]
    uus[...] = s_ref[2 * coarse : 3 * coarse]
    uvs[...] = s_ref[3 * coarse : 4 * coarse]
    vvs[...] = s_ref[4 * coarse : 5 * coarse]
    own_low, own_high = low_and_high(odd_x, own_e[...], own_o[...])
    got_low, got_high = low_and_high(odd_x, got_e[...], got_o[...])
    add_rows((us, vs), (uus, uvs, vvs), own_low, own_high, got_low, got_high)
    start = e_ref.shape[0] - coarse // 2
    lanes = e_ref.shape[1]
    wide, short = WIDE * levels, EXT * levels

    def laid(fields, ends, from_lane):
        lane = lax.broadcasted_iota(jnp.int32, fields[0].shape, 1)
        total, begin = None, 0
        for field, end in zip(fields, ends):
            there = pltpu.roll(field, (lanes + begin - from_lane) % lanes, 1) if begin != from_lane else field
            total = there if total is None else jnp.where(lane < begin, total, there)
            begin = end
        return total

    h = coarse // 2
    sides = []
    for from_lane in (0, HALF):
        both = laid((us[...], vs[...]), (wide, 2 * wide), from_lane)
        lane = lax.broadcasted_iota(jnp.int32, (coarse, lanes), 1)
        uu = pltpu.roll(uus[...], (lanes + 2 * wide - from_lane) % lanes, 1)
        first = jnp.where(lane < 2 * wide, both[:coarse], uu)
        quarters = (uvs[:h], uvs[h:], vvs[:h], vvs[h:])
        second = laid(quarters, [short * n for n in range(1, 5)], from_lane)
        sides.append((first, both[coarse:], second))
    for low, high, at in zip(*sides, (0, coarse, start)):
        here = slice(at, at + low.shape[0])
        e_ref[here] = jnp.where(odd_y == 0, high, low)
        o_ref[here] = jnp.where(odd_y == 0, low, high)


def first_form(plus_two, plus_one, minus_one, minus_two):
    return (8.0 * plus_one - plus_two - 8.0 * minus_one + minus_two) * (1.0 / 12.0)


def second_form(plus_two, plus_one, centre, minus_one, minus_two):
    return (16.0 * plus_one - plus_two - 30.0 * centre + 16.0 * minus_one - minus_two) * (1.0 / 12.0)


def final_kernel(
    p_ref, xe_own, xo_own, xe_got, xo_got, ye_own, yo_own, ye_got, yo_got, st_hbm, lib_hbm,
    us, vs, uus, uvs, vvs, low_side, high_side, slopes, st_ref, lib_ref, sem,
):
    odd_x = lax.rem(lax.axis_index("gx"), 2)
    odd_y = lax.rem(lax.axis_index("gy"), 2)
    levels, coarse, lanes = st_ref.shape[1:]
    rim_rows = us.shape[0]
    own_low, own_high = low_and_high(odd_y, ye_own[...], yo_own[...])
    got_low, got_high = low_and_high(odd_y, ye_got[...], yo_got[...])
    lane = lax.broadcasted_iota(jnp.int32, own_low.shape, 1)
    row = lax.broadcasted_iota(jnp.int32, own_low.shape, 0)
    wide, short = WIDE * levels, EXT * levels
    start = own_low.shape[0] - coarse // 2
    is_wide = (lane < 2 * wide) & (row < start)
    place = lax.rem(lane, WIDE)
    rim = pltpu.roll(got_low, lanes - EXT, 1) + pltpu.roll(own_low, lanes - RIM, 1)
    ordered = jnp.where(place < RIM, rim, pltpu.roll(got_low, RIM, 1))
    low_side[...] = jnp.where(is_wide, ordered, got_low)
    ahead = pltpu.roll(own_high, EXT, 1)
    high_side[...] = got_high + jnp.where(is_wide & (place >= EXT), ahead, 0.0)

    def out(level):
        return (
            pltpu.make_async_copy(st_ref.at[:, level], st_hbm.at[:, level], sem.at[0, level]),
            pltpu.make_async_copy(lib_ref.at[:, level], lib_hbm.at[:, level], sem.at[1, level]),
        )

    def finish(level):
        def part_of(k):
            return p_ref[pl.ds(pl.multiple_of((5 * level + k) * coarse, 8), coarse)]

        us[RIM : RIM + coarse] = part_of(0)
        vs[RIM : RIM + coarse] = part_of(1)
        for k, ref in enumerate((uus, uvs, vvs)):
            ref[...] = part_of(2 + k)
        own_low, own_high = low_and_high(odd_x, xe_own[level], xo_own[level])
        got_low, got_high = low_and_high(odd_x, xe_got[level], xo_got[level])
        add_rows((us, vs), (uus, uvs, vvs), own_low, own_high, got_low, got_high)

        def sides(at, count, base, cells):
            rim = RIM if cells == WIDE else 0
            first = base + cells * level
            low = pltpu.roll(low_side[at : at + count], lax.rem(2 * lanes - rim - first, lanes), 1)
            high = pltpu.roll(high_side[at : at + count], lanes - EXT - first, 1)
            return low, high

        def joined(field, low, high):
            lane = lax.broadcasted_iota(jnp.int32, field.shape, 1)
            return field + jnp.where(lane < EXT, low, 0.0) + jnp.where(lane >= lanes - EXT, high, 0.0)

        means = []
        found = []
        for k, ref in enumerate((us, vs)):
            low, high = sides(0, rim_rows, k * wide, WIDE)
            f = joined(ref[...], low, high)
            ref[...] = f
            lane = lax.broadcasted_iota(jnp.int32, f.shape, 1)
            plus_one = pltpu.roll(jnp.where(lane < 1, high, f), lanes - 1, 1)
            plus_two = pltpu.roll(jnp.where(lane < 2, high, f), lanes - 2, 1)
            minus_one = pltpu.roll(jnp.where(lane >= lanes - 1, low, f), 1, 1)
            minus_two = pltpu.roll(jnp.where(lane >= lanes - 2, low, f), 2, 1)
            slopes[...] = first_form(plus_two, plus_one, minus_one, minus_two)

            def row(source, by):
                return source[RIM + by : RIM + by + coarse]

            curve_y = second_form(plus_two, plus_one, f, minus_one, minus_two)[RIM : RIM + coarse]
            centre = row(ref, 0)
            shifted = [row(ref, by) for by in (2, 1, -1, -2)]
            grad_x = first_form(*shifted)
            curve_x = second_form(shifted[0], shifted[1], centre, shifted[2], shifted[3])
            grad_y = row(slopes, 0)
            cross = first_form(*[row(slopes, by) for by in (2, 1, -1, -2)])
            means.append(centre)
            found.append((grad_x, grad_y, curve_x, cross, curve_y))

        u, v = means
        low, high = sides(0, coarse, 2 * wide, EXT)
        st_ref[0, level] = joined(uus[...], low, high) - u * u
        for k, (ref, other) in enumerate(((uvs, u), (vvs, v))):
            for h in range(2):
                part = slice(coarse // 2 * h, coarse // 2 * (h + 1))
                low, high = sides(start, coarse // 2, (2 * k + h) * short, EXT)
                st_ref[1 + k, level, part] = joined(ref[part], low, high) - other[part] * v[part]

        (ux, uy, uxx, uxy, uyy), (vx, vy, vxx, vxy, vyy) = found
        vorticity = vx - uy
        features = (ux, uy, vx, vy, uxx, uxy, uyy, vxx, vxy, vyy, vxx - uxy, vxy - uyy)
        for k, feature in enumerate(features):
            lib_ref[4 * k, level] = feature
            lib_ref[4 * k + 1, level] = u * feature
            lib_ref[4 * k + 2, level] = v * feature
            lib_ref[4 * k + 3, level] = vorticity * feature
        for copy in out(level):
            copy.start()

    each(levels, FINAL_UNROLL, finish)
    for level in range(levels):
        for copy in out(level):
            copy.wait()


def pairs_of(axis):
    count = lax.axis_size(axis)
    assert count % 2 == 0
    even = [(i, i ^ 1) for i in range(count)]
    odd = [(i, (i + 1) % count if i % 2 else (i - 1) % count) for i in range(count)]
    return even, odd


def local_call(body, outs, scratch, *operands):
    in_vmem, in_hbm = pl.BlockSpec(memory_space=pltpu.VMEM), pl.BlockSpec(memory_space=pltpu.HBM)
    specs, arrays = [], []
    for operand, here in operands:
        specs.append(in_vmem if here else in_hbm)
        arrays.append(pltpu.with_memory_space_constraint(operand, pltpu.VMEM) if here else pltpu.with_memory_space_constraint(operand, pltpu.HBM))
    return pl.pallas_call(
        body,
        in_specs=specs,
        out_specs=[in_hbm if isinstance(o, jax.ShapeDtypeStruct) else in_vmem for o in outs],
        out_shape=outs,
        scratch_shapes=scratch,
        compiler_params=pltpu.CompilerParams(vmem_limit_bytes=VMEM_BYTES),
    )(*arrays)


def in_order(east_flow, north_flow):
    levels, count_x, count_y = east_flow.shape
    coarse, lanes = count_x // STEP, count_y // STEP
    assert lanes == 2 * HALF and (2 * WIDE + EXT) * levels <= lanes and coarse % 16 == 0
    assert count_x >= 2 * EDGE and count_y > 2 * SIDE
    three, two = (jnp.asarray(c) for c in message_rows(count_x))
    w_strips, w_ends, w_rest = (jnp.asarray(c) for c in column_weights(count_y))
    left = jnp.asarray(left_operand(taps(range(coarse), count_x)))
    rim_rows = coarse + 2 * RIM
    start = -(-rim_rows // 8) * 8
    side = (start + coarse // 2, lanes)
    own_count = 5 * coarse
    f32, bf16 = functools.partial(pltpu.VMEM, dtype=F32), functools.partial(pltpu.VMEM, dtype=BF16)

    def held(*arrays):
        return [(a, True) for a in arrays]

    (even_x, odd_x), (even_y, odd_y) = pairs_of("gx"), pairs_of("gy")
    parts = 1
    consts = (three, two, w_strips, w_ends, w_rest, left)
    se, so, ends_high, ends_low, *kept = local_call(
        slab_kernel,
        [f32((MSG, lanes))] * 2 + [bf16((48 * levels, 2 * SIDE))] * 2 + [bf16(c.shape) for c in consts],
        [f32((levels, 2 * EDGE, 2 * SIDE))] * 2
        + [pltpu.SemaphoreType.DMA((parts, 8)), pltpu.SemaphoreType.DMA((len(consts),))],
        *[(a, False) for a in (east_flow, north_flow) + consts],
    )
    message_ends = (ends_high, ends_low)
    three, two, w_strips, w_ends, w_rest, left = kept
    so_got = lax.ppermute(so, "gx", odd_x)
    se_got = lax.ppermute(se, "gx", even_x)
    fine = held(east_flow, north_flow)
    xe, xo = local_call(
        main_kernel,
        [f32((levels, MSG, lanes))] * 2,
        [bf16((48 * levels, count_y - 2 * SIDE))] * 2,
        *fine,
        *held(three, two, *message_ends, w_ends, w_rest),
    )
    xo_got = lax.ppermute(xo, "gx", odd_x)
    xe_got = lax.ppermute(xe, "gx", even_x)
    (strips,) = local_call(
        ends_kernel, [f32((own_count, lanes))], [bf16((own_count * levels, SIDE))] * 2, *fine, *held(left, w_strips)
    )
    rows = [f32((rim_rows, lanes))] * 2 + [f32((coarse, lanes))] * 3
    ye, yo = local_call(functools.partial(strip_kernel, levels), [f32(side)] * 2, rows, *held(strips, se, so, se_got, so_got))
    yo_got = lax.ppermute(yo, "gy", odd_y)
    ye_got = lax.ppermute(ye, "gy", even_y)
    (partial_sums,) = local_call(
        own_kernel,
        [f32((own_count * levels, lanes))],
        [bf16((own_count * levels, count_y))] * 2,
        *fine,
        *held(left, w_ends, w_rest),
    )
    outs = [jax.ShapeDtypeStruct((n, levels, coarse, lanes), F32) for n in (3, 48)]
    return local_call(
        final_kernel,
        outs,
        rows
        + [f32(side)] * 2
        + [f32((rim_rows, lanes))]
        + [f32(o.shape) for o in outs]
        + [pltpu.SemaphoreType.DMA((2, levels))],
        *held(partial_sums, xe, xo, xe_got, xo_got, ye, yo, ye_got, yo_got),
    )


def solution(mesh):
    return jax.shard_map(
        in_order,
        mesh=mesh,
        in_specs=(P(None, "gx", "gy"), P(None, "gx", "gy")),
        out_specs=(P(None, None, "gx", "gy"), P(None, None, "gx", "gy")),
        check_vma=False,
    )
```

```python
import functools

import jax
import jax.numpy as jnp
import numpy as np
from jax import lax
from jax.experimental import pallas as pl
from jax.experimental.pallas import tpu as pltpu
from jax.sharding import PartitionSpec as P

spread_cells = 5.5
REACH = 16
STEP = 4
EXT = REACH // STEP
RIM = 2
WIDE = EXT + RIM
EDGE = 24
SHORT = 16
SIDE = 128
HALF = 64
MSG = 24
F32, BF16 = jnp.float32, jnp.bfloat16
VMEM_BYTES = 24 << 20
MAIN_UNROLL, FINAL_UNROLL = 8, 1


def taps(cells, count_in):
    offsets = np.arange(2 * REACH + 1) - REACH
    bumps = np.exp(-0.5 * (offsets / spread_cells) ** 2)
    lag = np.arange(count_in)[None, :] - STEP * np.asarray(cells)[:, None]
    inside = np.abs(lag) <= REACH
    return np.where(inside, np.exp(-0.5 * (lag / spread_cells) ** 2), 0.0) / bumps.sum()


def pieces(values):
    high = values.astype(BF16)
    low = (values - high.astype(np.float64)).astype(BF16)
    return high, low


def left_operand(*sources):
    tops, bottoms = [], []
    for rows in sources:
        high, low = pieces(rows)
        tops += [high, high]
        bottoms += [low, np.zeros_like(low)]
    return np.concatenate([np.concatenate(tops, 1), np.concatenate(bottoms, 1)], 0)


def message_rows(count_x):
    coarse = count_x // STEP

    def rows(cells, ends):
        full = taps(cells, count_x)
        return np.concatenate([full[:, :ends], full[:, count_x - ends :]], 1)

    wide = {"low": rows(range(-EXT, RIM), EDGE), "high": rows(range(coarse - RIM, coarse + EXT), EDGE)}
    short = {"low": rows(range(-EXT, 0), SHORT), "high": rows(range(coarse, coarse + EXT), SHORT)}

    def placed(at, parts):
        blocks = []
        for part in parts:
            block = np.zeros((8, part.shape[1]))
            block[at : at + part.shape[0]] = part
            blocks.append(block)
        return np.concatenate(blocks, 0)

    three, two = [], []
    for sides in (("high", "low"), ("low", "high")):
        w = placed(0, [wide[s] for s in sides])
        none = np.zeros_like(w)
        vv = [placed(WIDE, [short[s][2 * h : 2 * h + 2] for s in sides]) for h in range(2)]
        three.append(left_operand(np.concatenate([w, none]), np.concatenate([none, w]), np.concatenate(vv)))
        two.append(left_operand(*[placed(EXT * h, [short[s] for s in sides]) for h in range(2)]))
    return np.stack(three), np.stack(two)


def column_weights(count_y):
    coarse = count_y // STEP
    own = taps(range(coarse), count_y).T
    strips = np.zeros((count_y, 2 * HALF))
    strips[:, :WIDE] = taps(range(-EXT, RIM), count_y).T
    high = list(range(coarse, coarse + EXT)) + list(range(coarse - RIM, coarse))
    strips[:, HALF : HALF + WIDE] = taps(high, count_y).T

    def ends(w):
        return np.concatenate([w[:SIDE], w[count_y - SIDE :]], 0)

    return tuple(np.concatenate(pieces(w), 1) for w in (ends(strips), ends(own), own[SIDE : count_y - SIDE]))


def split(values):
    high = values.astype(BF16)
    return high, (values - high.astype(F32)).astype(BF16)


def row_sums(left, field):
    high, low = split(field)
    both = jnp.dot(left, jnp.concatenate([high, low], 0), preferred_element_type=F32)
    half = both.shape[0] // 2
    return both[:half] + both[half:]


def column_sums(high, low, weights):
    count = weights.shape[1] // 2
    both = jnp.dot(high, weights[...], preferred_element_type=F32)
    return both[:, :count] + both[:, count:] + jnp.dot(low, weights[:, :count], preferred_element_type=F32)


def products(u, v):
    return u, v, u * u, u * v, v * v


def each(count, unroll, body):
    lax.fori_loop(0, count, lambda i, _: (body(i), None)[1], None, unroll=unroll)


def message_sums(three, two, u, v):
    us, vs = (jnp.concatenate([f[:SHORT], f[2 * EDGE - SHORT :]], 0) for f in (u, v))
    first = jnp.concatenate([*split(u), *split(v), *split(vs * vs)], 0)
    second = jnp.concatenate([*split(us * us), *split(us * vs)], 0)
    first = jnp.dot(three, first, preferred_element_type=F32)
    second = jnp.dot(two, second, preferred_element_type=F32)
    return jnp.concatenate([first[:32] + first[32:], second[:16] + second[16:]], 0)


def slab_kernel(
    u_hbm, v_hbm, three_hbm, two_hbm, w_hbm, w_ends_hbm, w_rest_hbm, left_hbm,
    e_ref, o_ref, x_high, x_low, three, two, weights, w_ends, w_rest, left,
    u_ref, v_ref, sem, const_sem,
):
    odd = lax.rem(lax.axis_index("gx"), 2)
    levels = u_ref.shape[0]
    _, count_x, count_y = u_hbm.shape
    parts = sem.shape[0]
    batch = levels // parts

    def loads(part):
        some = pl.ds(part * batch, batch)
        copies = []
        for f, (source, held) in enumerate(((u_hbm, u_ref), (v_hbm, v_ref))):
            for r in range(2):
                for c in range(2):
                    copies.append(
                        pltpu.make_async_copy(
                            source.at[
                                some, pl.ds(r * (count_x - EDGE), EDGE), pl.ds(c * (count_y - SIDE), SIDE)
                            ],
                            held.at[some, pl.ds(r * EDGE, EDGE), pl.ds(c * SIDE, SIDE)],
                            sem.at[part, 4 * f + 2 * r + c],
                        )
                    )
        return copies

    consts = [
        pltpu.make_async_copy(source, held, const_sem.at[k])
        for k, (source, held) in enumerate(
            (
                (three_hbm, three),
                (two_hbm, two),
                (w_hbm, weights),
                (left_hbm, left),
                (w_ends_hbm, w_ends),
                (w_rest_hbm, w_rest),
            )
        )
    ]
    for copy in loads(0) + consts[:3]:
        copy.start()
    for part in range(1, parts):
        for copy in loads(part):
            copy.start()
    for copy in consts[3:]:
        copy.start()
    for copy in consts[:3]:
        copy.wait()
    for part in range(parts):
        for copy in loads(part):
            copy.wait()

        for level in range(part * batch, (part + 1) * batch):
            at = slice(level * 48, (level + 1) * 48)
            x_high[at], x_low[at] = split(message_sums(three[odd], two[odd], u_ref[level], v_ref[level]))
    sums = column_sums(x_high[...], x_low[...], weights)
    row = lax.broadcasted_iota(jnp.int32, e_ref.shape, 0)
    wide = (row < 16) & (lax.rem(row, 8) < WIDE)
    for place, ref in ((0, e_ref), (8, o_ref)):
        parts = [message_of(sums, level, place) for level in range(levels)]
        ref[...] = jnp.where(wide, packed(parts, WIDE), packed([short_only(p) for p in parts], EXT))
    for copy in consts[3:]:
        copy.wait()


def short_only(strips):
    lane = lax.broadcasted_iota(jnp.int32, strips.shape, 1)
    return jnp.where(lax.rem(lane, HALF) < EXT, strips, 0.0)


def packed(parts, cells):
    return added([pltpu.roll(part, cells * level, 1) for level, part in enumerate(parts)])


def added(terms):
    while len(terms) > 1:
        terms = [a + b for a, b in zip(terms[::2], terms[1::2])] + terms[len(terms) & ~1 :]
    return terms[0]


def message_of(sums, level, place):
    return jnp.concatenate([sums[48 * level + 16 * t + place : 48 * level + 16 * t + place + 8] for t in range(3)], 0)


def middle(ref):
    count_y = ref.shape[-1]
    return pl.ds(SIDE, count_y - 2 * SIDE)


def main_kernel(
    u_ref, v_ref, three, two, ends_high, ends_low, w_ends, w_rest, e_ref, o_ref, x_high, x_low
):
    odd = lax.rem(lax.axis_index("gx"), 2)
    levels, count_x = u_ref.shape[:2]

    def rows_of(level):
        u, v = (
            jnp.concatenate([r[level, :EDGE, middle(r)], r[level, count_x - EDGE :, middle(r)]], 0)
            for r in (u_ref, v_ref)
        )
        at = pl.ds(pl.multiple_of(level * 48, 16), 48)
        x_high[at], x_low[at] = split(message_sums(three[odd], two[odd], u, v))

    each(levels, MAIN_UNROLL, rows_of)
    sums = column_sums(ends_high[...], ends_low[...], w_ends) + column_sums(x_high[...], x_low[...], w_rest)
    for place, ref in ((0, e_ref), (8, o_ref)):
        for level in range(levels):
            ref[level] = message_of(sums, level, place)


def own_rows_of(left, u, v):
    return split(jnp.concatenate([row_sums(left, f) for f in products(u, v)], 0))


def ends_kernel(u_ref, v_ref, left, weights, s_ref, x_high, x_low):
    levels, count_x, count_y = u_ref.shape
    rows, lanes = s_ref.shape
    lane = lax.broadcasted_iota(jnp.int32, (count_x, SIDE), 1)
    for level in range(levels):
        u, v = (
            jnp.where(lane < HALF, r[level, :, :SIDE], r[level, :, count_y - SIDE :]) for r in (u_ref, v_ref)
        )
        at = slice(level * rows, (level + 1) * rows)
        x_high[at], x_low[at] = own_rows_of(left[...], u, v)
    read = jnp.concatenate([weights[:HALF], weights[2 * SIDE - HALF :]], 0)
    wide = rows // 5 * 2
    strips, short = jnp.zeros((wide, lanes), F32), jnp.zeros((rows - wide, lanes), F32)
    for level in range(levels):
        at = slice(level * rows, (level + 1) * rows)
        sums = column_sums(x_high[at], x_low[at], read)
        strips = strips + pltpu.roll(sums[:wide], WIDE * level, 1)
        short = short + pltpu.roll(short_only(sums[wide:]), EXT * level, 1)
    s_ref[:wide] = strips
    s_ref[wide:] = short


def own_kernel(u_ref, v_ref, left, w_ends, w_rest, p_ref, x_high, x_low):
    levels = u_ref.shape[0]
    rows = p_ref.shape[0] // levels
    for level in range(levels):
        at = slice(level * rows, (level + 1) * rows)
        x_high[at], x_low[at] = own_rows_of(left[...], u_ref[level], v_ref[level])
    weights = jnp.concatenate([w_ends[:SIDE], w_rest[...], w_ends[SIDE:]], 0)
    batch = levels // 2
    for level in range(0, levels, batch):
        at = slice(level * rows, (level + batch) * rows)
        p_ref[at] = column_sums(x_high[at], x_low[at], weights)


def low_and_high(odd, e, o):
    return jnp.where(odd == 0, o, e), jnp.where(odd == 0, e, o)


def add_rows(wide_refs, short_refs, own_low, own_high, got_low, got_high):
    for k, ref in enumerate(wide_refs):
        count = ref.shape[0]
        at = 8 * k
        ref[0:RIM] = own_low[at + EXT - RIM : at + EXT]
        ref[count - RIM : count] = own_high[at + RIM : at + 2 * RIM]
        ref[0:WIDE] = ref[0:WIDE] + got_low[at : at + WIDE]
        ref[count - WIDE : count] = ref[count - WIDE : count] + got_high[at : at + WIDE]
    for k, ref in enumerate(short_refs):
        count = ref.shape[0]
        if k < 2:
            at = 16 + EXT * k
            ref[0:EXT] = ref[0:EXT] + got_low[at : at + EXT]
            ref[count - EXT : count] = ref[count - EXT : count] + got_high[at : at + EXT]
        else:
            for h in range(2):
                at = 8 * h + WIDE
                ref[2 * h : 2 * h + 2] = ref[2 * h : 2 * h + 2] + got_low[at : at + 2]
                back = count - EXT + 2 * h
                ref[back : back + 2] = ref[back : back + 2] + got_high[at : at + 2]


def strip_kernel(levels, s_ref, own_e, own_o, got_e, got_o, e_ref, o_ref, us, vs, uus, uvs, vvs):
    odd_x = lax.rem(lax.axis_index("gx"), 2)
    odd_y = lax.rem(lax.axis_index("gy"), 2)
    coarse = uus.shape[0]
    us[RIM : RIM + coarse] = s_ref[0:coarse]
    vs[RIM : RIM + coarse] = s_ref[coarse : 2 * coarse]
    uus[...] = s_ref[2 * coarse : 3 * coarse]
    uvs[...] = s_ref[3 * coarse : 4 * coarse]
    vvs[...] = s_ref[4 * coarse : 5 * coarse]
    own_low, own_high = low_and_high(odd_x, own_e[...], own_o[...])
    got_low, got_high = low_and_high(odd_x, got_e[...], got_o[...])
    add_rows((us, vs), (uus, uvs, vvs), own_low, own_high, got_low, got_high)
    start = e_ref.shape[0] - coarse // 2
    lanes = e_ref.shape[1]
    wide, short = WIDE * levels, EXT * levels

    def laid(fields, ends, from_lane):
        lane = lax.broadcasted_iota(jnp.int32, fields[0].shape, 1)
        total, begin = None, 0
        for field, end in zip(fields, ends):
            there = pltpu.roll(field, (lanes + begin - from_lane) % lanes, 1) if begin != from_lane else field
            total = there if total is None else jnp.where(lane < begin, total, there)
            begin = end
        return total

    h = coarse // 2
    sides = []
    for from_lane in (0, HALF):
        both = laid((us[...], vs[...]), (wide, 2 * wide), from_lane)
        lane = lax.broadcasted_iota(jnp.int32, (coarse, lanes), 1)
        uu = pltpu.roll(uus[...], (lanes + 2 * wide - from_lane) % lanes, 1)
        first = jnp.where(lane < 2 * wide, both[:coarse], uu)
        quarters = (uvs[:h], uvs[h:], vvs[:h], vvs[h:])
        second = laid(quarters, [short * n for n in range(1, 5)], from_lane)
        sides.append((first, both[coarse:], second))
    for low, high, at in zip(*sides, (0, coarse, start)):
        here = slice(at, at + low.shape[0])
        e_ref[here] = jnp.where(odd_y == 0, high, low)
        o_ref[here] = jnp.where(odd_y == 0, low, high)


def first_form(plus_two, plus_one, minus_one, minus_two):
    return (8.0 * plus_one - plus_two - 8.0 * minus_one + minus_two) * (1.0 / 12.0)


def second_form(plus_two, plus_one, centre, minus_one, minus_two):
    return (16.0 * plus_one - plus_two - 30.0 * centre + 16.0 * minus_one - minus_two) * (1.0 / 12.0)


def final_kernel(
    p_ref, xe_own, xo_own, xe_got, xo_got, ye_own, yo_own, ye_got, yo_got, st_hbm, lib_hbm,
    us, vs, uus, uvs, vvs, low_side, high_side, slopes, st_ref, lib_ref, sem,
):
    odd_x = lax.rem(lax.axis_index("gx"), 2)
    odd_y = lax.rem(lax.axis_index("gy"), 2)
    levels, coarse, lanes = st_ref.shape[1:]
    rim_rows = us.shape[0]
    own_low, own_high = low_and_high(odd_y, ye_own[...], yo_own[...])
    got_low, got_high = low_and_high(odd_y, ye_got[...], yo_got[...])
    lane = lax.broadcasted_iota(jnp.int32, own_low.shape, 1)
    row = lax.broadcasted_iota(jnp.int32, own_low.shape, 0)
    wide, short = WIDE * levels, EXT * levels
    start = own_low.shape[0] - coarse // 2
    is_wide = (lane < 2 * wide) & (row < start)
    place = lax.rem(lane, WIDE)
    rim = pltpu.roll(got_low, lanes - EXT, 1) + pltpu.roll(own_low, lanes - RIM, 1)
    ordered = jnp.where(place < RIM, rim, pltpu.roll(got_low, RIM, 1))
    low_side[...] = jnp.where(is_wide, ordered, got_low)
    ahead = pltpu.roll(own_high, EXT, 1)
    high_side[...] = got_high + jnp.where(is_wide & (place >= EXT), ahead, 0.0)

    def out(level):
        return (
            pltpu.make_async_copy(st_ref.at[:, level], st_hbm.at[:, level], sem.at[0, level]),
            pltpu.make_async_copy(lib_ref.at[:, level], lib_hbm.at[:, level], sem.at[1, level]),
        )

    def finish(level):
        def part_of(k):
            return p_ref[pl.ds(pl.multiple_of((5 * level + k) * coarse, 8), coarse)]

        us[RIM : RIM + coarse] = part_of(0)
        vs[RIM : RIM + coarse] = part_of(1)
        for k, ref in enumerate((uus, uvs, vvs)):
            ref[...] = part_of(2 + k)
        own_low, own_high = low_and_high(odd_x, xe_own[level], xo_own[level])
        got_low, got_high = low_and_high(odd_x, xe_got[level], xo_got[level])
        add_rows((us, vs), (uus, uvs, vvs), own_low, own_high, got_low, got_high)

        def sides(at, count, base, cells):
            rim = RIM if cells == WIDE else 0
            first = base + cells * level
            low = pltpu.roll(low_side[at : at + count], lax.rem(2 * lanes - rim - first, lanes), 1)
            high = pltpu.roll(high_side[at : at + count], lanes - EXT - first, 1)
            return low, high

        def joined(field, low, high):
            lane = lax.broadcasted_iota(jnp.int32, field.shape, 1)
            return field + jnp.where(lane < EXT, low, 0.0) + jnp.where(lane >= lanes - EXT, high, 0.0)

        means = []
        found = []
        for k, ref in enumerate((us, vs)):
            low, high = sides(0, rim_rows, k * wide, WIDE)
            f = joined(ref[...], low, high)
            ref[...] = f
            lane = lax.broadcasted_iota(jnp.int32, f.shape, 1)
            plus_one = pltpu.roll(jnp.where(lane < 1, high, f), lanes - 1, 1)
            plus_two = pltpu.roll(jnp.where(lane < 2, high, f), lanes - 2, 1)
            minus_one = pltpu.roll(jnp.where(lane >= lanes - 1, low, f), 1, 1)
            minus_two = pltpu.roll(jnp.where(lane >= lanes - 2, low, f), 2, 1)
            slopes[...] = first_form(plus_two, plus_one, minus_one, minus_two)

            def row(source, by):
                return source[RIM + by : RIM + by + coarse]

            curve_y = second_form(plus_two, plus_one, f, minus_one, minus_two)[RIM : RIM + coarse]
            centre = row(ref, 0)
            shifted = [row(ref, by) for by in (2, 1, -1, -2)]
            grad_x = first_form(*shifted)
            curve_x = second_form(shifted[0], shifted[1], centre, shifted[2], shifted[3])
            grad_y = row(slopes, 0)
            cross = first_form(*[row(slopes, by) for by in (2, 1, -1, -2)])
            means.append(centre)
            found.append((grad_x, grad_y, curve_x, cross, curve_y))

        u, v = means
        low, high = sides(0, coarse, 2 * wide, EXT)
        st_ref[0, level] = joined(uus[...], low, high) - u * u
        for k, (ref, other) in enumerate(((uvs, u), (vvs, v))):
            for h in range(2):
                part = slice(coarse // 2 * h, coarse // 2 * (h + 1))
                low, high = sides(start, coarse // 2, (2 * k + h) * short, EXT)
                st_ref[1 + k, level, part] = joined(ref[part], low, high) - other[part] * v[part]

        (ux, uy, uxx, uxy, uyy), (vx, vy, vxx, vxy, vyy) = found
        vorticity = vx - uy
        features = (ux, uy, vx, vy, uxx, uxy, uyy, vxx, vxy, vyy, vxx - uxy, vxy - uyy)
        for k, feature in enumerate(features):
            lib_ref[4 * k, level] = feature
            lib_ref[4 * k + 1, level] = u * feature
            lib_ref[4 * k + 2, level] = v * feature
            lib_ref[4 * k + 3, level] = vorticity * feature
        for copy in out(level):
            copy.start()

    each(levels, FINAL_UNROLL, finish)
    for level in range(levels):
        for copy in out(level):
            copy.wait()


def pairs_of(axis):
    count = lax.axis_size(axis)
    assert count % 2 == 0
    even = [(i, i ^ 1) for i in range(count)]
    odd = [(i, (i + 1) % count if i % 2 else (i - 1) % count) for i in range(count)]
    return even, odd


def local_call(body, outs, scratch, *operands):
    in_vmem, in_hbm = pl.BlockSpec(memory_space=pltpu.VMEM), pl.BlockSpec(memory_space=pltpu.HBM)
    specs, arrays = [], []
    for operand, here in operands:
        specs.append(in_vmem if here else in_hbm)
        arrays.append(pltpu.with_memory_space_constraint(operand, pltpu.VMEM) if here else pltpu.with_memory_space_constraint(operand, pltpu.HBM))
    return pl.pallas_call(
        body,
        in_specs=specs,
        out_specs=[in_hbm if isinstance(o, jax.ShapeDtypeStruct) else in_vmem for o in outs],
        out_shape=outs,
        scratch_shapes=scratch,
        compiler_params=pltpu.CompilerParams(vmem_limit_bytes=VMEM_BYTES),
    )(*arrays)


def in_order(east_flow, north_flow):
    levels, count_x, count_y = east_flow.shape
    coarse, lanes = count_x // STEP, count_y // STEP
    assert lanes == 2 * HALF and (2 * WIDE + EXT) * levels <= lanes and coarse % 16 == 0
    assert levels % 2 == 0
    assert count_x >= 2 * EDGE and count_y > 2 * SIDE
    three, two = (jnp.asarray(c) for c in message_rows(count_x))
    w_strips, w_ends, w_rest = (jnp.asarray(c) for c in column_weights(count_y))
    left = jnp.asarray(left_operand(taps(range(coarse), count_x)))
    rim_rows = coarse + 2 * RIM
    start = -(-rim_rows // 8) * 8
    side = (start + coarse // 2, lanes)
    own_count = 5 * coarse
    f32, bf16 = functools.partial(pltpu.VMEM, dtype=F32), functools.partial(pltpu.VMEM, dtype=BF16)

    def held(*arrays):
        return [(a, True) for a in arrays]

    (even_x, odd_x), (even_y, odd_y) = pairs_of("gx"), pairs_of("gy")
    parts = 1
    consts = (three, two, w_strips, w_ends, w_rest, left)
    se, so, ends_high, ends_low, *kept = local_call(
        slab_kernel,
        [f32((MSG, lanes))] * 2 + [bf16((48 * levels, 2 * SIDE))] * 2 + [bf16(c.shape) for c in consts],
        [f32((levels, 2 * EDGE, 2 * SIDE))] * 2
        + [pltpu.SemaphoreType.DMA((parts, 8)), pltpu.SemaphoreType.DMA((len(consts),))],
        *[(a, False) for a in (east_flow, north_flow) + consts],
    )
    message_ends = (ends_high, ends_low)
    three, two, w_strips, w_ends, w_rest, left = kept
    so_got = lax.ppermute(so, "gx", odd_x)
    se_got = lax.ppermute(se, "gx", even_x)
    fine = held(east_flow, north_flow)
    xe, xo = local_call(
        main_kernel,
        [f32((levels, MSG, lanes))] * 2,
        [bf16((48 * levels, count_y - 2 * SIDE))] * 2,
        *fine,
        *held(three, two, *message_ends, w_ends, w_rest),
    )
    xo_got = lax.ppermute(xo, "gx", odd_x)
    xe_got = lax.ppermute(xe, "gx", even_x)
    (strips,) = local_call(
        ends_kernel, [f32((own_count, lanes))], [bf16((own_count * levels, SIDE))] * 2, *fine, *held(left, w_strips)
    )
    rows = [f32((rim_rows, lanes))] * 2 + [f32((coarse, lanes))] * 3
    ye, yo = local_call(functools.partial(strip_kernel, levels), [f32(side)] * 2, rows, *held(strips, se, so, se_got, so_got))
    yo_got = lax.ppermute(yo, "gy", odd_y)
    ye_got = lax.ppermute(ye, "gy", even_y)
    (partial_sums,) = local_call(
        own_kernel,
        [f32((own_count * levels, lanes))],
        [bf16((own_count * levels, count_y))] * 2,
        *fine,
        *held(left, w_ends, w_rest),
    )
    outs = [jax.ShapeDtypeStruct((n, levels, coarse, lanes), F32) for n in (3, 48)]
    return local_call(
        final_kernel,
        outs,
        rows
        + [f32(side)] * 2
        + [f32((rim_rows, lanes))]
        + [f32(o.shape) for o in outs]
        + [pltpu.SemaphoreType.DMA((2, levels))],
        *held(partial_sums, xe, xo, xe_got, xo_got, ye, yo, ye_got, yo_got),
    )


def solution(mesh):
    return jax.shard_map(
        in_order,
        mesh=mesh,
        in_specs=(P(None, "gx", "gy"), P(None, "gx", "gy")),
        out_specs=(P(None, None, "gx", "gy"), P(None, None, "gx", "gy")),
        check_vma=False,
    )
```
